512 devices in a mesh: depth: 64 (over y, x, core), az: 8 (over z).
Axes of the slice: x: 4, y: 8, z: 8, core: 2. Of those that a mesh axis runs over, the one named last changes fastest.
Arguments:
- velocity: float32 [6, 1024, 64, 128], P(None, 'depth', 'az'), may hold values from -6 to 6
- stress: float32 [7, 1024, 64, 128], P(None, 'depth', 'az'), may hold values from -6 to 6
- memory: float32 [12, 1024, 64, 128], P(None, 'depth', 'az'), may hold values from -3 to 3
- layer_ids: int32 [256, 32], P('depth'), may hold values from 0 to 7, as said below
- materials: float32 [8, 8], replicated, may hold values from 0.006 to 4, as said below
- jkd: float32 [8, 9], replicated, may hold values from 0.1 to 60, as said below
- source_depth: int32 [1], replicated, may hold values from 0 to 1023
Outputs:
- velocity_out: float32 [6, 1024, 64, 128], P(None, 'depth', 'az')
- stress_out: float32 [7, 1024, 64, 128], P(None, 'depth', 'az')
- memory_out: float32 [12, 1024, 64, 128], P(None, 'depth', 'az')
The draws below stay inside these ranges and needn't reach their ends.
Inputs may be any that keep to these rules, and one draw needn't show every extreme that they name: `layer_ids`: the first 4 radial elements hold 0 (borehole fluid); beyond them each depth element holds one formation row of 1 to 7 for all its radial elements. `materials`: columns: lambda0 0.5 to 1.5, shear modulus 0.3 to 1 (row 0: 0.006 to 0.02), M 0.5 to 1.5, beta 0.3 to 0.9, bulk density 1.5 to 2.5, fluid density 0.8 to 1.2, tortuosity 1.5 to 4, friction 0.5 to 2. `jkd`: omega 0.5 to 5, pole weights 0.1 to 1, pole rates 0.3 to 60.
All inputs are finite; a program needn't handle non-finite values.
Results may differ from the reference program's by a relative error of at most 0.0001.
Values sent between devices are 32-bit elements; how exact they have to be, the bound alone decides.
No kernel may reach another device: no remote copies, remote signals or barrier semaphores. Data moves between devices by JAX's collectives and lax.ppermute only.
A program may use at most 128 MiB of HBM per device.

```python
import math
import jax
import jax.numpy as jnp
import numpy as np
from jax import lax

NR = 128
NT = 64
STEPS = 2
NMAT = 8
RB = 4
NZ = 1024


def draw_layer_ids(key, part):
    layers = jax.random.randint(key, (NZ // 4, 1), 1, NMAT)
    radial_index = jnp.arange(NR // 4)[None, :]
    return jnp.where(radial_index < RB, 0, layers).astype(jnp.int32)


def draw_materials(key, part):
    unit_draw = jax.random.uniform(key, (NMAT, 8), jnp.float32)
    lower_end = jnp.array([0.5, 0.3, 0.5, 0.3, 1.5, 0.8, 1.5, 0.5], jnp.float32)
    upper_end = jnp.array([1.5, 1.0, 1.5, 0.9, 2.5, 1.2, 4.0, 2.0], jnp.float32)
    values = lower_end + (upper_end - lower_end) * unit_draw
    fluid_cell = (jnp.arange(NMAT) == 0)[:, None] & (jnp.arange(8) == 1)[None, :]
    return jnp.where(fluid_cell, 0.02 * values, values).astype(jnp.float32)


def draw_jkd(key, part):
    unit_draw = jax.random.uniform(key, (NMAT, 9), jnp.float32)
    column = jnp.arange(9)[None, :]
    omega_part = 0.5 + 4.5 * unit_draw
    weight_part = 0.1 + 0.9 * unit_draw
    rate_part = jnp.exp(math.log(0.3) + (math.log(60.0) - math.log(0.3)) * unit_draw)
    return jnp.where(column == 0, omega_part, jnp.where(column < 5, weight_part, rate_part)).astype(jnp.float32)


def levels(rng, extent, pieces, low, high):
    gain = 1.0
    for dim, blocks in pieces:
        heights = jax.random.uniform(jax.random.fold_in(jax.random.fold_in(rng, 6), dim), (blocks,), jnp.float32, low / len(pieces), high / len(pieces))
        gain = gain * jnp.repeat(jnp.exp(heights), extent[dim] // blocks).reshape((-1,) + (1,) * (len(extent) - 1 - dim))
    return gain


def noise(rng, dims, deviation, reach, shards=(), kind=jnp.bfloat16):
    loudness = levels(rng, dims, shards, -0.22, 0.18) if shards else 1.0
    entries = jax.random.normal(rng, dims, jnp.float32) * deviation * loudness
    return jnp.minimum(jnp.maximum(entries, -reach), reach).astype(kind)


def setup_inputs(seed: int = 0) -> dict:
    arg_keys = jax.random.split(jax.random.key(seed), 8)
    return {
        "velocity": noise(arg_keys[0], (6, NZ, NT, NR), 1.0, 6.0, ((1, 64), (2, 8)), jnp.float32),
        "stress": noise(arg_keys[1], (7, NZ, NT, NR), 1.0, 6.0, ((1, 64), (2, 8)), jnp.float32),
        "memory": noise(arg_keys[2], (12, NZ, NT, NR), 0.5, 3.0, ((1, 64), (2, 8)), jnp.float32),
        "layer_ids": draw_layer_ids(jax.random.fold_in(arg_keys[7], 71), 0),
        "materials": draw_materials(jax.random.fold_in(arg_keys[7], 71), 0),
        "jkd": draw_jkd(jax.random.fold_in(arg_keys[7], 71), 0),
        "source_depth": jax.random.randint(arg_keys[6], (1,), 0, NZ).astype(jnp.int32),
    }


DT = 0.02
SOURCE_GAIN = 40.0
R_INNER = 1.0
HIGHEST = lax.Precision.HIGHEST

def gll_basis():
    root_value = math.sqrt(3.0 / 7.0)
    gll_nodes = np.array([-1.0, -root_value, 0.0, root_value, 1.0])
    weights = np.array([0.1, 49.0 / 90.0, 32.0 / 45.0, 49.0 / 90.0, 0.1])
    offsets = gll_nodes[:, None] - gll_nodes[None, :] + np.eye(5)
    factors = np.prod(offsets, axis=1)
    derivative = factors[:, None] / factors[None, :] / offsets
    diagonal_part = np.sum(1.0 / offsets, axis=1) - 1.0
    derivative = derivative * (1.0 - np.eye(5)) + np.eye(5) * diagonal_part[:, None]
    return (gll_nodes, weights, derivative)

def radial_operator(node_count):
    gll_nodes, weights, derivative = gll_basis()
    full_count = node_count + 1
    stencil = weights[:, None] * derivative * 2.0
    assembled = np.zeros((full_count, full_count))
    node_mass = np.zeros(full_count)
    for element in range(node_count // 4):
        assembled[4 * element:4 * element + 5, 4 * element:4 * element + 5] += stencil
        node_mass[4 * element:4 * element + 5] += weights
    return (assembled / node_mass[:, None])[:node_count, :node_count]

def radial_positions(node_count):
    gll_nodes, weights, derivative = gll_basis()
    positions = np.arange(node_count)
    return R_INNER + positions // 4 + 0.5 * (1.0 + gll_nodes[positions % 4])

def depth_derivative(fields):
    gll_nodes, weights, derivative = gll_basis()
    stencil = jnp.asarray(weights[:, None] * derivative * 2.0, fields.dtype)
    comps, depth_count, azim_count, radial_count = fields.shape
    elements = depth_count // 4
    extended = jnp.concatenate([fields, jnp.zeros_like(fields[:, :1])], axis=1)
    blocks = jnp.concatenate([fields.reshape(comps, elements, 4, azim_count, radial_count), extended[:, 4::4][:, :, None]], axis=2)
    contrib = jnp.einsum('ij,cejtr->ceitr', stencil, blocks, precision=HIGHEST)
    shifted = jnp.concatenate([jnp.zeros_like(contrib[:, :1, 4]), contrib[:, :-1, 4]], axis=1)
    first_node = contrib[:, :, 0] + shifted
    assembled = jnp.concatenate([first_node[:, :, None], contrib[:, :, 1:4]], axis=2)
    node_mass = np.tile(np.array([weights[0] + weights[4], weights[1], weights[2], weights[3]]), (elements, 1))
    node_mass[0, 0] = weights[0]
    node_mass = jnp.asarray(node_mass, fields.dtype)
    return (assembled / node_mass[None, :, :, None, None]).reshape(comps, depth_count, azim_count, radial_count)

def radial_derivative(fields):
    radial_matrix = jnp.asarray(radial_operator(fields.shape[3]), fields.dtype)
    return jnp.einsum('ij,cztj->czti', radial_matrix, fields, precision=HIGHEST)

def azimuth_derivative(fields):
    azim_count = fields.shape[2]
    spectrum = jnp.fft.rfft(fields, axis=2)
    mode_index = np.arange(azim_count // 2 + 1)
    wave_modes = np.where(mode_index == azim_count // 2, 0.0, mode_index * 1.0)
    return jnp.fft.irfft(1j * jnp.asarray(wave_modes)[:, None] * spectrum, n=azim_count, axis=2)

def reference(velocity, stress, memory, layer_ids, materials, jkd, source_depth):
    combined = jnp.concatenate([materials, jkd], axis=1)[layer_ids]
    per_node = jnp.repeat(jnp.repeat(combined, 4, axis=0), 4, axis=1)
    coeffs = jnp.moveaxis(per_node, 2, 0)[:, :, None, :]
    lame_zero, shear_mod, modulus, coupling = (coeffs[0], coeffs[1], coeffs[2], coeffs[3])
    density, fluid_density, tortuosity, friction = (coeffs[4], coeffs[5], coeffs[6], coeffs[7])
    relax_omega = coeffs[8]
    pole_weights = coeffs[9:13][:, None]
    pole_rates = coeffs[13:17][:, None]
    fluid_inertia = fluid_density * tortuosity
    determinant = density * fluid_inertia - fluid_density * fluid_density
    lame_fluid = lame_zero + coupling * coupling * modulus
    inverse_r = jnp.asarray(1.0 / radial_positions(NR), velocity.dtype)
    depth_total, azim_count = (velocity.shape[1], velocity.shape[2])
    plane_index = jnp.arange(depth_total, dtype=jnp.int32)
    source_mask = ((plane_index == source_depth[0])[:, None, None] & (jnp.arange(NR) < 4 * RB)[None, None, :]).astype(velocity.dtype)
    memory_state = memory.reshape(4, 3, depth_total, azim_count, NR)
    solid_vel, fluid_vel = (velocity[:3], velocity[3:])
    fields = stress
    for time_step in range(STEPS):
        radial_d = radial_derivative(jnp.stack([fields[0], fields[3], fields[4], fields[6]]))
        azim_d = azimuth_derivative(jnp.stack([fields[3], fields[1], fields[5], fields[6]])) * inverse_r
        depth_d = depth_derivative(jnp.stack([fields[4], fields[5], fields[2], fields[6]]))
        stress_div = jnp.stack([radial_d[0] + azim_d[0] + depth_d[0] + (fields[0] - fields[1]) * inverse_r, radial_d[1] + azim_d[1] + depth_d[1] + 2.0 * fields[3] * inverse_r, radial_d[2] + azim_d[2] + depth_d[2] + fields[4] * inverse_r])
        resist = jnp.stack([radial_d[3], azim_d[3], depth_d[3]]) + friction * lax.optimization_barrier(jnp.sum(pole_weights * memory_state, axis=0))
        solid_vel = solid_vel + DT * (fluid_inertia * stress_div + fluid_density * resist) / determinant
        fluid_step = -DT * (fluid_density * stress_div + density * resist) / determinant
        fluid_vel = fluid_vel + fluid_step
        memory_state = (memory_state + fluid_step + DT * relax_omega * fluid_vel) / (1.0 + DT * (pole_rates + relax_omega))
        radial_d = radial_derivative(jnp.stack([solid_vel[0], solid_vel[1], solid_vel[2], fluid_vel[0]]))
        azim_d = azimuth_derivative(jnp.stack([solid_vel[0], solid_vel[1], solid_vel[2], fluid_vel[1]])) * inverse_r
        depth_d = depth_derivative(jnp.stack([solid_vel[0], solid_vel[1], solid_vel[2], fluid_vel[2]]))
        strain_rr = radial_d[0]
        strain_tt = solid_vel[0] * inverse_r + azim_d[1]
        strain_zz = depth_d[2]
        shear_rt = azim_d[0] + radial_d[1] - solid_vel[1] * inverse_r
        shear_rz = depth_d[0] + radial_d[2]
        shear_tz = depth_d[1] + azim_d[2]
        div_solid = strain_rr + strain_tt + strain_zz
        div_fluid = radial_d[3] + fluid_vel[0] * inverse_r + azim_d[3] + depth_d[3]
        bulk_term = lame_fluid * div_solid + coupling * modulus * div_fluid
        source_term = DT * SOURCE_GAIN * math.cos(0.9 * time_step) * source_mask
        fields = jnp.stack([fields[0] + DT * (bulk_term + 2.0 * shear_mod * strain_rr), fields[1] + DT * (bulk_term + 2.0 * shear_mod * strain_tt), fields[2] + DT * (bulk_term + 2.0 * shear_mod * strain_zz), fields[3] + DT * shear_mod * shear_rt, fields[4] + DT * shear_mod * shear_rz, fields[5] + DT * shear_mod * shear_tz, fields[6] - DT * modulus * (coupling * div_solid + div_fluid) + source_term])
    velocity_out = jnp.concatenate([solid_vel, fluid_vel], axis=0)
    memory_out = memory_state.reshape(12, depth_total, azim_count, NR)
    return (velocity_out, fields, memory_out)
```

```python
import functools
import math

import jax
import jax.numpy as jnp
import ml_dtypes
import numpy as np
from jax import lax
from jax.experimental import pallas as pl
from jax.experimental.pallas import tpu as pltpu
from jax.sharding import PartitionSpec as P

NR = 128
NT = 64
RB = 4
PLANES = 16
AZ = 8
GROUP = 16
DT = 0.02
SOURCE = DT * 40.0
R_INNER = 1.0
F32 = jnp.float32
BF16 = jnp.bfloat16
FIELDS_IN = 19
FIELDS_OUT = 14


def gll_basis():
    root_value = math.sqrt(3.0 / 7.0)
    nodes = np.array([-1.0, -root_value, 0.0, root_value, 1.0])
    weights = np.array([0.1, 49.0 / 90.0, 32.0 / 45.0, 49.0 / 90.0, 0.1])
    offsets = nodes[:, None] - nodes[None, :] + np.eye(5)
    factors = np.prod(offsets, axis=1)
    derivative = factors[:, None] / factors[None, :] / offsets
    diagonal = np.sum(1.0 / offsets, axis=1) - 1.0
    derivative = derivative * (1.0 - np.eye(5)) + np.eye(5) * diagonal[:, None]
    return nodes, weights, derivative


NODES, WEIGHTS, DERIV = gll_basis()
ROW = DERIV * np.array([1.0, 2.0, 2.0, 2.0, 1.0])[:, None]


def line_operator(count, first):
    matrix = np.zeros((count + 1, count + 1))
    for e in range(count // 4):
        matrix[4 * e : 4 * e + 5, 4 * e : 4 * e + 5] += ROW
    if first:
        matrix[0] *= 2.0
    else:
        matrix[0, 0] += ROW[4, 4]
    return matrix[:count, :count]


def halves(matrix):
    hi = matrix.astype(np.float32).astype(ml_dtypes.bfloat16)
    lo = (matrix - hi.astype(np.float64)).astype(np.float32).astype(ml_dtypes.bfloat16)
    return np.stack([hi, lo])


def azimuth_operator():
    positions = np.arange(NT)
    offsets = positions[:, None] - positions[None, :]
    modes = np.arange(1, NT // 2)
    phases = 2.0 * np.pi * offsets[:, :, None] * modes / NT
    return -(2.0 / NT) * np.sum(modes * np.sin(phases), axis=2)


def inverse_radius():
    positions = np.arange(NR)
    return 1.0 / (R_INNER + positions // 4 + 0.5 * (1.0 + NODES[positions % 4]))


@functools.lru_cache(None)
def constants():
    groups = NR // GROUP
    c = {}
    c["dr"] = halves(line_operator(NR, True).T)
    items = np.zeros((8, NR, groups, 16))
    for s in range(8):
        for k in range(groups):
            if GROUP * (k + 1) < NR:
                items[s, GROUP * (k + 1), k, 2 * s] = 1.0
            if k:
                items[s, GROUP * k - 4 : GROUP * k, k, 2 * s + 1] = ROW[4, :4]
    c["items"] = halves(items.reshape(8 * NR, 128))
    c["dt"] = halves(azimuth_operator())
    c["mr"] = np.stack([halves(np.kron(np.eye(8), line_operator(16, first).T)) for first in (False, True)])
    c["mz"] = np.stack([halves(np.kron(line_operator(16, first).T, np.eye(16))) for first in (False, True)])
    spread = np.zeros((2, 16))
    spread[0, 12:] = ROW[:4, 4]
    spread[1, 0] = 1.0
    wr = np.zeros((2, 8, 16, 4, 8, 16))
    wz = np.zeros((8, 16, 4, 16, 16))
    for f in range(4):
        for side in range(2):
            for j in range(8):
                for order in range(2):
                    wr[order, j, 8 * order + 2 * f + side, f, j] = spread[side]
            for r in range(16):
                wz[2 * f + side, r, f, :, r] = spread[side]
    c["wr"] = np.stack([halves(w) for w in wr.reshape(2, 128, 512)])
    c["wz"] = halves(wz.reshape(128, 1024))
    q = inverse_radius().astype(np.float32)
    c["q"] = np.broadcast_to(q, (8, NR)).copy()
    c["qg"] = np.broadcast_to(
        np.tile(q.reshape(groups, 1, GROUP), (1, PLANES, 1)).reshape(groups, 1, 256), (groups, 8, 256)
    ).copy()
    return c


def roll(x, shift):
    return pltpu.roll(x, shift % x.shape[-1], x.ndim - 1)


def dot(a, b):
    return jnp.dot(a, b, preferred_element_type=F32)


def parts(x):
    hi = x.astype(BF16)
    return hi, (x - hi.astype(F32)).astype(BF16)


def mm(x, hi, lo):
    xh, xl = parts(x)
    return dot(xh, hi) + dot(xl, hi) + dot(xh, lo)


def coefficients(ids, tab):
    hits = [ids == float(m) for m in range(8)]

    def pick(column):
        value = jnp.where(hits[0], tab[0, column], 0.0)
        for m in range(1, 8):
            value = jnp.where(hits[m], tab[m, column], value)
        return value

    lame, mu, modulus, beta, rho, rho_f, tort, fric = [pick(c) for c in range(8)]
    omega = pick(8)
    weights = [pick(9 + l) for l in range(4)]
    rates = [pick(13 + l) for l in range(4)]
    rho_w = tort * rho_f
    scale = DT / (rho * rho_w - rho_f * rho_f)
    decay = [1.0 / (1.0 + DT * (rate + omega)) for rate in rates]
    gain = sum(a * c for a, c in zip(weights, decay))
    return dict(
        cv=rho_w * scale,
        cf=rho_f * scale,
        cr=rho * scale,
        fric=fric,
        omega=DT * omega,
        weights=weights,
        decay=decay,
        kappa=(1.0 + DT * omega) * gain,
        bulk=DT * (lame + beta * beta * modulus),
        couple=DT * beta * modulus,
        modulus=DT * modulus,
        shear=DT * mu,
    )


def spread_rows(value, first, count, tail=False):
    rows = [jnp.broadcast_to(value[first + e : first + e + 1, :], (8, NR)) for e in range(count + tail)]
    planes = [rows[i // 4] for i in range(4 * count + tail)]
    return jnp.stack(planes)


def combine(row, nodes):
    total = None
    for weight, node in zip(row, nodes):
        term = float(weight) * node
        total = term if total is None else total + term
    return total


def depth_derivative(x, lo, hi, edge, has_below, low=None, high=None):
    count = (x.shape[0] - 1) // 4
    blocks = x[: 4 * count].reshape((count, 4) + x.shape[1:])
    last = [blocks[e + 1, 0] if e + 1 < count else x[4 * count] for e in range(count)]

    def nodes(e):
        return [blocks[e, l] for l in range(4)] + [last[e]]

    out = []
    for e in range(lo, hi + 1):
        upper = combine(ROW[0], nodes(e)) if e < count else high
        lower = combine(ROW[4], nodes(e - 1)) if e > 0 else low
        if e == edge:
            upper = (2.0 - has_below) * upper
            lower = has_below * lower
        out.append(upper + lower)
        if e < hi:
            for i in range(1, 4):
                out.append(combine(ROW[i], nodes(e)))
    return jnp.stack(out)


def below_partial(x):
    return combine(ROW[4, :4], [x[l] for l in range(4)])


def lane_groups():
    return lax.broadcasted_iota(jnp.int32, (8, NR), 1) // GROUP


def exchange_groups(x):
    groups = lane_groups()
    rows = [x[j] for j in range(8)]
    for s in (4, 2, 1):
        low = (groups & s) == 0
        for j in range(8):
            if not j & s:
                a, b = rows[j], rows[j + s]
                rows[j] = jnp.where(low, a, roll(b, GROUP * s))
                rows[j + s] = jnp.where(low, roll(a, -GROUP * s), b)
    return rows


def flat(x):
    return x.reshape(-1, NR)


def prepare(v, s, psi, ids, tab, vw, t_out, up, dn):
    c = coefficients(ids[...], tab)

    def sp(value):
        return spread_rows(value, 2, 4)

    weights = [sp(w) for w in c["weights"]]
    cf = sp(c["cf"] * c["fric"])
    cr = sp(c["cr"] * c["fric"])
    decayed = [sp(w * d) for w, d in zip(c["weights"], c["decay"])]
    for i in range(3):
        memory = [psi[3 * l + i] for l in range(4)]
        total = sum(w * m for w, m in zip(weights, memory))
        t_out[i] = sum(w * (m - v[3 + i]) for w, m in zip(decayed, memory))
        vi = v[i] + cf * total
        wi = v[3 + i] - cr * total
        for f, x in ((i, vi), (3 + i, wi)):
            vw[f] = x
            up[56 + 8 * f : 64 + 8 * f] = x[8:]
            dn[35 + 5 * f : 40 + 5 * f] = x[:5]
    for f in range(7):
        up[8 * f : 8 * f + 8] = s[f, 8:]
        dn[5 * f : 5 * f + 5] = s[f, :5]
    for i, f in enumerate((4, 5, 2, 6)):
        nodes = [s[f, 4 + l] for l in range(5)]
        up[104 + i] = combine(ROW[4], nodes)
        dn[65 + i] = combine(ROW[0], nodes)
    own = ids[...]
    rows = lax.broadcasted_iota(jnp.int32, (8, NR), 0)
    up[108] = jnp.where(rows < 2, pltpu.roll(own, 4, 0), 0.0)
    dn[69] = jnp.where(rows >= 6, pltpu.roll(own, 4, 0), 0.0)


def launch(s, vw, t_in, up, dn, ids, tab, info, dr_m, items, q_ref, pk, keep):
    has_below = info[1].astype(F32)
    has_above = info[2].astype(F32)
    own = ids[...]
    rows = lax.broadcasted_iota(jnp.int32, (8, NR), 0)
    own = jnp.where((rows >= 2) & (rows < 6), own, 0.0)
    c = coefficients(own + up[108] + dn[69], tab)
    q = q_ref[...]

    def radial(fields):
        stacked = jnp.concatenate([flat(x) for x in fields], axis=0)
        out = mm(stacked, dr_m[0], dr_m[1])
        count = fields[0].shape[0]
        return [out[8 * count * i : 8 * count * (i + 1)].reshape(count, 8, NR) for i in range(len(fields))]

    def ext(f):
        return jnp.concatenate([up[8 * f : 8 * f + 8], s[f], dn[5 * f : 5 * f + 5]], axis=0)

    def ext_v(f):
        return jnp.concatenate(
            [up[56 + 8 * f : 64 + 8 * f], vw[f], dn[35 + 5 * f : 40 + 5 * f]], axis=0
        )

    above29 = lax.broadcasted_iota(jnp.int32, (29, 8, NR), 0) < 24
    mask29 = jnp.where(above29, 1.0, has_above)
    rr, tt, zz, rt, rz, tz, p = [ext(f) for f in range(7)]
    cv, cf, cr = [spread_rows(c[n], 0, 7, True) for n in ("cv", "cf", "cr")]
    r_rr, r_rt, r_rz, r_p = radial([rr, rt, rz, p])
    z_rz, z_tz, z_zz, z_p = [
        depth_derivative(x, 0, 7, 2, has_below, up[104 + i], dn[65 + i]) for i, x in enumerate((rz, tz, zz, p))
    ]
    d_r = r_rr + z_rz + q * (rr - tt)
    d_t = r_rt + z_tz + 2.0 * q * rt
    d_z = r_rz + z_zz + q * rz
    v1 = [
        mask29 * (ext_v(0) + cv * d_r + cf * r_p),
        mask29 * (ext_v(1) + cv * d_t),
        mask29 * (ext_v(2) + cv * d_z + cf * z_p),
    ]
    w1 = [
        mask29 * (ext_v(3) - cf * d_r - cr * r_p),
        mask29 * (ext_v(4) - cf * d_t),
        mask29 * (ext_v(5) - cf * d_z - cr * z_p),
    ]
    q_rt, q_tt, q_tz, q_p = q * rt, q * tt, q * tz, q * p
    u = [cv * q_rt, cv * q_tt + cf * q_p, cv * q_tz]
    uw = [-(cf * q_rt), -(cf * q_tt + cr * q_p), -(cf * q_tz)]

    def pack(f, planes):
        for g in range(2):
            chunks = exchange_groups(planes[8 * g : 8 * g + 8])
            for k in range(8):
                pk[k, 2 * f + g] = chunks[k]

    for f, x in enumerate((3, 1, 5, 6)):
        pack(f, s[x])
    fric = spread_rows(c["fric"], 2, 4)
    kappa = spread_rows(c["kappa"], 2, 4)
    grads = (r_p, None, z_p)
    for i, d in enumerate((d_r, d_t, d_z)):
        g = fric * (t_in[i] + kappa * w1[i][8:24])
        if grads[i] is not None:
            g = g + grads[i][8:24]
        a = cv[8:24] * d[8:24] + cf[8:24] * g
        b = cf[8:24] * d[8:24] + cr[8:24] * g
        pack(4 + i, v1[i][8:24])
        pack(7 + i, w1[i][8:24])
        pack(10 + i, a)
        keep[i] = v1[i][8:24]
        keep[3 + i] = w1[i][8:24]
        keep[6 + i] = a
        keep[9 + i] = b
        if i == 1:
            pack(13, b)

    bulk, couple, modulus, shear = [
        spread_rows(c[n], 1, 6)[:21] for n in ("bulk", "couple", "modulus", "shear")
    ]
    mask21 = jnp.where(lax.broadcasted_iota(jnp.int32, (21, 8, NR), 0) < 20, 1.0, has_above)
    plane21 = lax.broadcasted_iota(jnp.int32, (21, 8, NR), 0) - 4
    lane21 = lax.broadcasted_iota(jnp.int32, (21, 8, NR), 2)
    source = jnp.where((plane21 == info[0]) & (lane21 < 4 * RB), SOURCE, 0.0)

    def stresses(v, w, extra):
        inner = slice(4, 25)
        vr, vt, wr = v[0][inner], v[1][inner], w[0][inner]
        r_r, r_t, r_z, r_w = radial([vr, vt, v[2][inner], wr])
        z_r, z_t, z_z, z_w = [depth_derivative(x, 1, 6, 2, has_below) for x in (v[0], v[1], v[2], w[2])]
        e_tt, g_rt, g_tz, div_w = q * vr, r_t - q * vt, z_t, r_w + q * wr + z_w
        if extra is not None:
            e_tt, g_rt, g_tz, div_w = e_tt + extra[1], g_rt + extra[0], g_tz + extra[2], div_w + extra[3]
        div_v = r_r + e_tt + z_z
        total = bulk * div_v + couple * div_w
        return dict(
            rr=mask21 * (total + 2.0 * shear * r_r),
            zz=mask21 * (total + 2.0 * shear * z_z),
            rt=mask21 * (shear * g_rt),
            rz=mask21 * (shear * (z_r + r_z)),
            tz=mask21 * (shear * g_tz),
            p=mask21 * (-(couple * div_v + modulus * div_w) + (source if extra is None else 0.0)),
        )

    x0 = stresses(v1, w1, None)
    inner = slice(4, 25)
    x1 = stresses(u, uw, [q * v1[0][inner], q * v1[1][inner], q * v1[2][inner], q * w1[1][inner]])
    e2, dw2 = q * u[1][inner], q * uw[1][inner]
    total2 = bulk * e2 + couple * dw2
    x2 = dict(
        rr=mask21 * total2,
        zz=mask21 * total2,
        rt=mask21 * (shear * (q * u[0][inner])),
        tz=mask21 * (shear * (q * u[2][inner])),
        p=mask21 * (-(couple * e2 + modulus * dw2)),
    )

    def radius_items(fields):
        stacked = jnp.concatenate([flat(x) for x in fields], axis=1)
        return mm(stacked, items[0], items[1]).reshape(-1, 8, NR)

    def depth_items(fields, first):
        out = []
        for x in fields:
            out.append(x[first + 20])
            out.append(has_below * below_partial(x[first : first + 4]))
        return jnp.stack(out)

    velocity_r = [v1[0], v1[1], v1[2], w1[0], u[0], u[1], u[2], uw[0]]
    pack(14, radius_items([x[8:24] for x in velocity_r]))
    names_r = ("rr", "rt", "rz", "p")
    pack(15, radius_items([x[n][4:20] for x in (x0, x1) for n in names_r]))
    pack(16, depth_items([v1[0], v1[1], v1[2], w1[2], u[0], u[1], u[2], uw[2]], 4))
    names_z = ("rz", "tz", "zz", "p")
    pack(17, depth_items([x[n] for x in (x0, x1) for n in names_z], 0))
    zero8 = jnp.zeros((8, 8, NR), F32)
    second = [x2[n][4 + 8 * h : 12 + 8 * h] if n in x2 else zero8 for h in range(2) for n in names_r]
    zero21 = jnp.zeros((21, 8, NR), F32)
    pack(
        18,
        jnp.concatenate(
            [radius_items(second), depth_items([x2[n] if n in x2 else zero21 for n in names_z], 0)], axis=0
        ),
    )


def ring(recv, ids, tab, info, dt_m, mr, mz, wr, wz, qg, out):
    c = coefficients(ids[...], tab)
    group = info[3]
    q = qg[group]
    sel_r = info[4]
    sel_z = info[5]

    def field(f):
        return jnp.concatenate([recv[:, 2 * f], recv[:, 2 * f + 1]], axis=-1)

    def az(fields):
        x = jnp.concatenate([y.reshape(NT, -1) for y in fields], axis=1)
        xh, xl = parts(x)
        y = dot(dt_m[0], xh) + dot(dt_m[0], xl) + dot(dt_m[1], xh)
        res, at = [], 0
        for f in fields:
            n = f.shape[-1]
            res.append(y[:, at : at + n].reshape(f.shape))
            at += n
        return res

    def by_half(x):
        x = x.reshape(NT, 256)
        return [x[:, :128], x[:, 128:]]

    mr_h, mr_l = mr[sel_r, 0], mr[sel_r, 1]
    mz_h, mz_l = mz[sel_z, 0], mz[sel_z, 1]

    def radial(fields, halo):
        stacked = jnp.concatenate([h for f in fields for h in by_half(f)], axis=0)
        y = mm(stacked, mr_h, mr_l)
        res = []
        for i in range(len(fields)):
            halves_ = [
                y[128 * i + 64 * g : 128 * i + 64 * g + 64] + halo[64 * g : 64 * g + 64, 128 * i : 128 * i + 128]
                for g in range(2)
            ]
            res.append(jnp.concatenate(halves_, axis=1).reshape(8, 8, 256))
        return res

    def depth(fields, halo):
        stacked = jnp.concatenate([f.reshape(NT, 256) for f in fields], axis=0)
        y = mm(stacked, mz_h, mz_l)
        return [
            (y[64 * i : 64 * i + 64] + halo[:, 256 * i : 256 * i + 256]).reshape(8, 8, 256)
            for i in range(len(fields))
        ]

    rt, tt, tz, p = [field(f) for f in range(4)]
    pr2, pr3 = field(14), field(15)
    pd2 = [recv[:, 32], recv[:, 33]]
    pd3 = [recv[:, 34], recv[:, 35]]
    px = field(18)
    s_rt, s_tt, s_tz, s_p, d_pr2, d_pr3, d_pd2, d_pd3, d_px = az([rt, tt, tz, p, pr2, pr3, pd2[1], pd3[1], px])
    (dd_px,) = az([d_px])
    wr0, wr1 = (wr[0, 0], wr[0, 1]), (wr[1, 0], wr[1, 1])

    def stack_halves(x):
        return jnp.concatenate(by_half(x), axis=0)

    def radius_halo(zero, one):
        return mm(stack_halves(zero), *wr0) + mm(stack_halves(one), *wr1)

    hr2 = radius_halo(pr2, d_pr2)
    hz2 = mm((pd2[0] + d_pd2).reshape(NT, 128), wz[0], wz[1])
    half = dd_px.reshape(NT, 256)[:, :128]
    hr3 = radius_halo(pr3, d_pr3) + jnp.concatenate([mm(half, *wr0), mm(half, *wr1)], axis=0)
    hz3 = mm((pd3[0] + d_pd3).reshape(NT, 128) + dd_px.reshape(NT, 256)[:, 128:], wz[0], wz[1])

    cv, cf, cr = c["cv"], c["cf"], c["cr"]
    q_rt, q_tt, q_tz, q_p = q * s_rt, q * s_tt, q * s_tz, q * s_p
    dw = [-(cf * q_rt), -(cf * q_tt + cr * q_p), -(cf * q_tz)]
    v1 = [
        field(4) + cv * q_rt,
        field(5) + cv * q_tt + cf * q_p,
        field(6) + cv * q_tz,
    ]
    w1 = [field(7 + i) + dw[i] for i in range(3)]
    r_r, r_t, r_z, r_w = radial([v1[0], v1[1], v1[2], w1[0]], hr2)
    z_r, z_t, z_z, z_w = depth([v1[0], v1[1], v1[2], w1[2]], hz2)
    a_r, a_t, a_z, a_w = az([v1[0], v1[1], v1[2], w1[1]])
    e_tt = q * (v1[0] + a_t)
    div_v = r_r + e_tt + z_z
    div_w = r_w + q * (w1[0] + a_w) + z_w
    total = c["bulk"] * div_v + c["couple"] * div_w
    shear = c["shear"]
    lanes = lax.broadcasted_iota(jnp.int32, (8, 256), 1) // GROUP
    source = jnp.where((lanes == info[0]) & (group == 0), SOURCE, 0.0)
    n_rr = total + 2.0 * shear * r_r
    n_tt = total + 2.0 * shear * e_tt
    n_zz = total + 2.0 * shear * z_z
    n_rt = shear * (q * (a_r - v1[1]) + r_t)
    n_rz = shear * (z_r + r_z)
    n_tz = shear * (z_t + q * a_z)
    n_p = source - (c["couple"] * div_v + c["modulus"] * div_w)

    r_rr, r_rt, r_rz, r_p = radial([n_rr, n_rt, n_rz, n_p], hr3)
    z_rz, z_tz, z_zz, z_p = depth([n_rz, n_tz, n_zz, n_p], hz3)
    a_rt, a_tt, a_tz, a_p = az([n_rt, n_tt, n_tz, n_p])
    d_r = q_rt + r_rr + z_rz + q * (a_rt + n_rr - n_tt)
    d_t = q_tt + r_rt + z_tz + q * (a_tt + 2.0 * n_rt)
    d_z = q_tz + r_rz + z_zz + q * (a_tz + n_rz)
    fk = c["fric"] * c["kappa"]
    g_r = r_p + fk * dw[0]
    g_t = q_p + q * a_p + fk * dw[1]
    g_z = z_p + fk * dw[2]
    sums = [
        2.0 * v1[0] + field(10) + cv * d_r + cf * g_r,
        2.0 * v1[1] + field(11) + cv * d_t + cf * g_t,
        2.0 * v1[2] + field(12) + cv * d_z + cf * g_z,
        2.0 * w1[1] - field(13) - cf * d_t - cr * g_t,
    ]
    results = [s_rt, s_tt, s_tz, s_p, d_r, d_t, d_z, g_r, g_t, g_z] + az(sums)
    for f, x in enumerate(results):
        out[:, 2 * f] = x[:, :, :128]
        out[:, 2 * f + 1] = x[:, :, 128:]


def finish(recv, keep, v, s, psi, ids, tab, info, dr_m, q_ref, v_out, s_out, m_out, up, dn):
    has_below = info[1].astype(F32)
    c = coefficients(ids[...], tab)
    q = q_ref[...]

    def sp(value):
        return spread_rows(value, 2, 4)

    def unpack(f):
        planes = []
        for g in range(2):
            planes += exchange_groups([recv[k, 2 * f + g] for k in range(8)])
        return jnp.stack(planes)

    cv, cf, cr = sp(c["cv"]), sp(c["cf"]), sp(c["cr"])
    q_rt, q_tt, q_tz, q_p = [q * unpack(f) for f in range(4)]
    dv = [cv * q_rt, cv * q_tt + cf * q_p, cv * q_tz]
    dw = [-(cf * q_rt), -(cf * q_tt + cr * q_p), -(cf * q_tz)]
    sums_v, sums_w = [], []
    omega = sp(c["omega"])
    decay = [sp(d) for d in c["decay"]]
    for i in range(3):
        d, g = unpack(4 + i), unpack(7 + i)
        v1 = keep[i] + dv[i]
        w1 = keep[3 + i] + dw[i]
        v2 = v1 + keep[6 + i] + cv * d + cf * g
        w2 = w1 - keep[9 + i] - cf * d - cr * g
        v_out[i] = v2
        v_out[3 + i] = w2
        sums_v.append(v1 + v2)
        sums_w.append(w1 + w2)
        first = w1 - v[3 + i] + omega * w1
        second = w2 - w1 + omega * w2
        for l in range(4):
            m_out[3 * l + i] = decay[l] * (decay[l] * (psi[3 * l + i] + first) + second)
    halo = [sums_v[0], sums_v[1], sums_v[2], sums_w[2]]
    for i, x in enumerate(halo):
        up[i] = below_partial(x[12:])
        dn[i] = x[0]
    zero = jnp.zeros((1, 8, NR), F32)
    z_r, z_t, z_z, z_w = [
        depth_derivative(jnp.concatenate([x, zero], axis=0), 0, 4, 0, has_below, float(ROW[4, 4]) * x[0], zero[0])[:16]
        for x in halo
    ]
    stacked = jnp.concatenate([flat(x) for x in (sums_v[0], sums_v[1], sums_v[2], sums_w[0])], axis=0)
    y = mm(stacked, dr_m[0], dr_m[1])
    r_r, r_t, r_z, r_w = [y[128 * i : 128 * i + 128].reshape(16, 8, NR) for i in range(4)]
    a_r, a_t, a_z, a_w = [unpack(10 + i) for i in range(4)]
    e_tt = q * (sums_v[0] + a_t)
    div_v = r_r + e_tt + z_z
    div_w = r_w + q * (sums_w[0] + a_w) + z_w
    couple, shear = sp(c["couple"]), sp(c["shear"])
    total = sp(c["bulk"]) * div_v + couple * div_w
    plane = lax.broadcasted_iota(jnp.int32, (16, 8, NR), 0)
    lane = lax.broadcasted_iota(jnp.int32, (16, 8, NR), 2)
    source = jnp.where((plane == info[0]) & (lane < 4 * RB), SOURCE * (1.0 + math.cos(0.9)), 0.0)
    s_out[0] = s[0] + total + 2.0 * shear * r_r
    s_out[1] = s[1] + total + 2.0 * shear * e_tt
    s_out[2] = s[2] + total + 2.0 * shear * z_z
    s_out[3] = s[3] + shear * (q * (a_r - sums_v[1]) + r_t)
    s_out[4] = s[4] + shear * (z_r + r_z)
    s_out[5] = s[5] + shear * (z_t + q * a_z)
    s_out[6] = s[6] + source - (couple * div_v + sp(c["modulus"]) * div_w)


def close(s, up, dn, ids, tab, info, s_out):
    has_below = info[1].astype(F32)
    c = coefficients(ids[...], tab)

    def update(plane, row, z_r, z_t, z_z, z_w):
        def at(name):
            return jnp.broadcast_to(c[name][row : row + 1, :], (8, NR))

        bulk, couple, modulus, shear = at("bulk"), at("couple"), at("modulus"), at("shear")
        total = bulk * z_z + couple * z_w
        s_out[0, plane] = s[0, plane] + total
        s_out[1, plane] = s[1, plane] + total
        s_out[2, plane] = s[2, plane] + total + 2.0 * shear * z_z
        s_out[3, plane] = s[3, plane]
        s_out[4, plane] = s[4, plane] + shear * z_r
        s_out[5, plane] = s[5, plane] + shear * z_t
        s_out[6, plane] = s[6, plane] - (couple * z_z + modulus * z_w)

    update(0, 2, *[has_below * up[i] for i in range(4)])
    for plane in range(12, 16):
        weight = float(ROW[plane - 12, 4])
        update(plane, 5, *[weight * dn[i] for i in range(4)])
    for f in range(7):
        s_out[f, 1:12] = s[f, 1:12]


def call(body, inputs, shapes, smem=(), cost=None):
    specs = [
        pl.BlockSpec(memory_space=pltpu.SMEM if i in smem else pltpu.VMEM) for i in range(len(inputs))
    ]
    out = pl.pallas_call(
        body,
        out_shape=[jax.ShapeDtypeStruct(x, F32) for x in shapes],
        in_specs=specs,
        out_specs=[pl.BlockSpec(memory_space=pltpu.VMEM) for _ in shapes],
        compiler_params=pltpu.CompilerParams(vmem_limit_bytes=48 * 2**20),
        cost_estimate=pl.CostEstimate(flops=cost or 10**7, bytes_accessed=10**7, transcendentals=0),
        name=body.__name__,
    )(*inputs)
    return out


def shift(value, steps):
    count = lax.axis_size("depth")
    first, last = max(0, -steps), min(count, count - steps)
    return lax.ppermute(value, "depth", [(i, i + steps) for i in range(first, last)])


def on_device(velocity, stress, memory, layer_ids, materials, jkd, source_depth):
    c = constants()
    row = lax.axis_index("depth")
    group = lax.axis_index("az")
    tab = jnp.concatenate([materials, jkd], axis=1)
    first = (row == 0).astype(jnp.int32)
    last = (row == lax.axis_size("depth") - 1).astype(jnp.int32)
    info = jnp.stack(
        [
            source_depth[0] - PLANES * row,
            1 - first,
            1 - last,
            group,
            (group == 0).astype(jnp.int32),
            first,
        ]
    ).astype(jnp.int32)
    ids = jnp.repeat(layer_ids.astype(F32), 4, axis=1)
    ids_own = jnp.pad(ids, ((2, 2), (0, 0)))
    ids_group = lax.dynamic_slice_in_dim(ids, GROUP * group, GROUP, axis=1)
    ids_group = jnp.broadcast_to(jnp.repeat(ids_group, 4, axis=0).reshape(1, 256), (8, 256))
    block = (PLANES, AZ, NR)
    vw, t_part, up, dn = call(
        prepare,
        [velocity, stress, memory, ids_own, tab],
        [(6,) + block, (3,) + block, (109, AZ, NR), (70, AZ, NR)],
        smem=(4,),
    )
    up, dn = shift(up, 1), shift(dn, -1)
    packed, keep = call(
        launch,
        [stress, vw, t_part, up, dn, ids_own, tab, info, c["dr"], c["items"], c["q"]],
        [(8, 2 * FIELDS_IN, AZ, NR), (12,) + block],
        smem=(6, 7),
    )
    packed = lax.all_to_all(packed, "az", split_axis=0, concat_axis=0, tiled=True)
    (back,) = call(
        ring,
        [packed, ids_group, tab, info, c["dt"], c["mr"], c["mz"], c["wr"], c["wz"], c["qg"]],
        [(8, 2 * FIELDS_OUT, AZ, NR)],
        smem=(2, 3),
    )
    back = lax.all_to_all(back, "az", split_axis=0, concat_axis=0, tiled=True)
    v_out, s_part, m_out, up, dn = call(
        finish,
        [back, keep, velocity, stress, memory, ids_own, tab, info, c["dr"], c["q"]],
        [(6,) + block, (7,) + block, (12,) + block, (4, AZ, NR), (4, AZ, NR)],
        smem=(6, 7),
    )
    up, dn = shift(up, 1), shift(dn, -1)
    (s_out,) = call(close, [s_part, up, dn, ids_own, tab, info], [(7,) + block], smem=(4, 5))
    return v_out, s_out, m_out


def solution(mesh):
    field = P(None, "depth", "az", None)
    return jax.shard_map(
        on_device,
        mesh=mesh,
        in_specs=(field, field, field, P("depth", None), P(), P(), P()),
        out_specs=(field, field, field),
        check_vma=False,
    )
```

```python
import functools
import math

import jax
import jax.numpy as jnp
import ml_dtypes
import numpy as np
from jax import lax
from jax.experimental import pallas as pl
from jax.experimental.pallas import tpu as pltpu
from jax.sharding import PartitionSpec as P

NR = 128
NT = 64
RB = 4
PLANES = 16
AZ = 8
GROUP = 16
DT = 0.02
SOURCE = DT * 40.0
R_INNER = 1.0
F32 = jnp.float32
BF16 = jnp.bfloat16
FIELDS_IN = 18
FIELDS_OUT = 14
VMEM_LIMIT = 32 * 2**20
VMEM_FULL = 56 * 2**20
SHARED = ("cv", "cf", "cr", "bulk", "couple", "modulus", "shear")
OWN = SHARED + ("fric", "kappa", "omega", "decay0", "decay1", "decay2", "decay3")
FLAGS = len(OWN)
RING = SHARED + ("fk",)


def gll_basis():
    root_value = math.sqrt(3.0 / 7.0)
    nodes = np.array([-1.0, -root_value, 0.0, root_value, 1.0])
    weights = np.array([0.1, 49.0 / 90.0, 32.0 / 45.0, 49.0 / 90.0, 0.1])
    offsets = nodes[:, None] - nodes[None, :] + np.eye(5)
    factors = np.prod(offsets, axis=1)
    derivative = factors[:, None] / factors[None, :] / offsets
    diagonal = np.sum(1.0 / offsets, axis=1) - 1.0
    derivative = derivative * (1.0 - np.eye(5)) + np.eye(5) * diagonal[:, None]
    return nodes, weights, derivative


NODES, WEIGHTS, DERIV = gll_basis()
ROW = DERIV * np.array([1.0, 2.0, 2.0, 2.0, 1.0])[:, None]


def line_operator(count, first):
    matrix = np.zeros((count + 1, count + 1))
    for e in range(count // 4):
        matrix[4 * e : 4 * e + 5, 4 * e : 4 * e + 5] += ROW
    if first:
        matrix[0] *= 2.0
    else:
        matrix[0, 0] += ROW[4, 4]
    return matrix[:count, :count]


def halves(matrix):
    hi = matrix.astype(np.float32).astype(ml_dtypes.bfloat16)
    lo = (matrix - hi.astype(np.float64)).astype(np.float32).astype(ml_dtypes.bfloat16)
    return np.stack([hi, lo])


def azimuth_operator():
    positions = np.arange(NT)
    offsets = positions[:, None] - positions[None, :]
    modes = np.arange(1, NT // 2)
    phases = 2.0 * np.pi * offsets[:, :, None] * modes / NT
    return -(2.0 / NT) * np.sum(modes * np.sin(phases), axis=2)


@functools.lru_cache(None)
def constants():
    groups = NR // GROUP
    c = {}
    c["dr"] = halves(line_operator(NR, True).T)
    items = np.zeros((8, NR, groups, 16))
    for s in range(8):
        for k in range(groups):
            if GROUP * (k + 1) < NR:
                items[s, GROUP * (k + 1), k, 2 * s] = 1.0
            if k:
                items[s, GROUP * k - 4 : GROUP * k, k, 2 * s + 1] = ROW[4, :4]
    c["items"] = halves(items.reshape(8 * NR, 128))
    c["dt"] = halves(azimuth_operator())
    c["mr"] = np.stack([halves(np.kron(np.eye(8), line_operator(16, first).T)) for first in (False, True)])
    c["mz"] = np.stack([halves(np.kron(line_operator(16, first).T, np.eye(16))) for first in (False, True)])
    spread = np.zeros((2, 16))
    spread[0, 12:] = ROW[:4, 4]
    spread[1, 0] = 1.0
    wr = np.zeros((2, 8, 16, 4, 8, 16))
    wz = np.zeros((8, 16, 4, 16, 16))
    for f in range(4):
        for side in range(2):
            for j in range(8):
                for order in range(2):
                    wr[order, j, 8 * order + 2 * f + side, f, j] = spread[side]
            for r in range(16):
                wz[2 * f + side, r, f, :, r] = spread[side]
    c["wr"] = np.stack([halves(w) for w in wr.reshape(2, 128, 512)])
    c["wz"] = halves(wz.reshape(128, 1024))
    return c


def roll(x, shift):
    return pltpu.roll(x, shift % x.shape[-1], x.ndim - 1)


def dot(a, b):
    return jnp.dot(a, b, preferred_element_type=F32)


def parts(x):
    hi = x.astype(BF16)
    return hi, (x - hi.astype(F32)).astype(BF16)


def mm(x, hi, lo):
    xh, xl = parts(x)
    return dot(xh, hi) + dot(xl, hi) + dot(xh, lo)


def inverse_radius(group, width):
    lane = lax.broadcasted_iota(jnp.int32, (8, 128 if width == NR else 256), 1) % width
    place = lane % 4
    offset = jnp.zeros(lane.shape, F32)
    for j in range(4):
        offset = jnp.where(place == j, float(R_INNER + 0.5 * (1.0 + NODES[j])), offset)
    return 1.0 / (offset + (lane // 4 + 4 * group).astype(F32))


def own_ids(lids):
    row = lax.broadcasted_iota(jnp.int32, (8, NR), 0)
    fluid = lax.broadcasted_iota(jnp.int32, (8, NR), 1) < 4 * RB
    value = jnp.zeros((8, NR), jnp.int32)
    for e in range(4):
        value = jnp.where(row == 2 + e, jnp.where(fluid, lids[e, 0], lids[e, NR // 4 - 1]), value)
    return value.astype(F32)


def coefficients(ids, tab):
    hits = [ids == float(m) for m in range(8)]
    materials, jkd = tab

    def pick(table, column):
        value = jnp.where(hits[0], table[0, column], 0.0)
        for m in range(1, 8):
            value = jnp.where(hits[m], table[m, column], value)
        return value

    lame, mu, modulus, beta, rho, rho_f, tort, fric = [pick(materials, c) for c in range(8)]
    omega = pick(jkd, 0)
    weights = [pick(jkd, 1 + l) for l in range(4)]
    rates = [pick(jkd, 5 + l) for l in range(4)]
    rho_w = tort * rho_f
    scale = DT / (rho * rho_w - rho_f * rho_f)
    decay = [1.0 / (1.0 + DT * (rate + omega)) for rate in rates]
    gain = sum(a * c for a, c in zip(weights, decay))
    return dict(
        cv=rho_w * scale,
        cf=rho_f * scale,
        cr=rho * scale,
        fric=fric,
        omega=DT * omega,
        weights=weights,
        decay=decay,
        decay0=decay[0],
        decay1=decay[1],
        decay2=decay[2],
        decay3=decay[3],
        kappa=(1.0 + DT * omega) * gain,
        fk=fric * ((1.0 + DT * omega) * gain),
        bulk=DT * (lame + beta * beta * modulus),
        couple=DT * beta * modulus,
        modulus=DT * modulus,
        shear=DT * mu,
    )


def spread_rows(value, first, count, tail=False):
    rows = [jnp.broadcast_to(value[first + e : first + e + 1, :], (8, NR)) for e in range(count + tail)]
    planes = [rows[i // 4] for i in range(4 * count + tail)]
    return jnp.stack(planes)


def combine(row, nodes):
    total = None
    for weight, node in zip(row, nodes):
        term = float(weight) * node
        total = term if total is None else total + term
    return total


def depth_derivative(x, lo, hi, edge, has_below, low=None, high=None):
    count = (x.shape[0] - 1) // 4
    blocks = x[: 4 * count].reshape((count, 4) + x.shape[1:])
    last = [blocks[e + 1, 0] if e + 1 < count else x[4 * count] for e in range(count)]

    def nodes(e):
        return [blocks[e, l] for l in range(4)] + [last[e]]

    out = []
    for e in range(lo, hi + 1):
        upper = combine(ROW[0], nodes(e)) if e < count else high
        lower = combine(ROW[4], nodes(e - 1)) if e > 0 else low
        if e == edge:
            upper = (2.0 - has_below) * upper
            lower = has_below * lower
        out.append(upper + lower)
        if e < hi:
            for i in range(1, 4):
                out.append(combine(ROW[i], nodes(e)))
    return jnp.stack(out)


def below_partial(x):
    return combine(ROW[4, :4], [x[l] for l in range(4)])


def lane_groups():
    return lax.broadcasted_iota(jnp.int32, (8, NR), 1) // GROUP


def exchange_groups(x):
    groups = lane_groups()
    rows = [x[j] for j in range(8)]
    for s in (4, 2, 1):
        low = (groups & s) == 0
        for j in range(8):
            if not j & s:
                a, b = rows[j], rows[j + s]
                rows[j] = jnp.where(low, a, roll(b, GROUP * s))
                rows[j + s] = jnp.where(low, roll(a, -GROUP * s), b)
    return rows


def flat(x):
    return x.reshape(-1, NR)


def prepare(
    lids_hbm, mat_hbm, jkd_hbm, src_hbm, psi_hbm, v_hbm, s_hbm,
    vw, t_out, up, dn, coef, ring_coef,
    lids, mat, jkd, src, psi, v, s, sems,
):
    pairs = (
        (lids_hbm, lids), (mat_hbm, mat), (jkd_hbm, jkd), (src_hbm, src), (psi_hbm, psi), (v_hbm, v), (s_hbm, s)
    )
    copies = [pltpu.make_async_copy(a, b, sems.at[i]) for i, (a, b) in enumerate(pairs)]
    for copy in copies:
        copy.start()
    for copy in copies[:4]:
        copy.wait()
    device = lax.axis_index("depth")
    rows = lax.broadcasted_iota(jnp.int32, (8, NR), 0)
    c = coefficients(own_ids(lids), (mat, jkd))
    mine = (rows >= 2) & (rows < 6)
    for n, name in enumerate(OWN):
        coef[n] = jnp.where(mine, c[name], 0.0)
    source = (src[0] - PLANES * device).astype(F32)
    coef[FLAGS] = jnp.full((8, NR), jnp.where(device > 0, 1.0, 0.0), F32)
    coef[FLAGS + 1] = jnp.full((8, NR), jnp.where(device < lax.axis_size("depth") - 1, 1.0, 0.0), F32)
    coef[FLAGS + 2] = jnp.full((8, NR), source, F32)
    for n, name in enumerate(SHARED):
        swapped = pltpu.roll(c[name], 4, 0)
        up[108 + n] = jnp.where(rows < 2, swapped, 0.0)
        dn[69 + n] = jnp.where(rows >= 6, swapped, 0.0)
    element = lax.broadcasted_iota(jnp.int32, (8, 256), 1) // 64
    group = lax.axis_index("az")
    ids = jnp.zeros((8, 256), jnp.int32)
    for e in range(4):
        ids = jnp.where(element == e, lids[e, 4 * group], ids)
    rc = coefficients(ids.astype(F32), (mat, jkd))
    for n, name in enumerate(RING):
        ring_coef[n] = rc[name]
    ring_coef[len(RING)] = jnp.full((8, 256), source, F32)

    def sp(value):
        return spread_rows(value, 2, 4)

    weights = [sp(w) for w in c["weights"]]
    cf = sp(c["cf"] * c["fric"])
    cr = sp(c["cr"] * c["fric"])
    decayed = [sp(w * d) for w, d in zip(c["weights"], c["decay"])]
    for copy in copies[4:]:
        copy.wait()
    for i in range(3):
        memory = [psi[3 * l + i] for l in range(4)]
        total = sum(w * m for w, m in zip(weights, memory))
        t_out[i] = sum(w * (m - v[3 + i]) for w, m in zip(decayed, memory))
        vi = v[i] + cf * total
        wi = v[3 + i] - cr * total
        for f, x in ((i, vi), (3 + i, wi)):
            vw[f] = x
            up[56 + 8 * f : 64 + 8 * f] = x[8:]
            dn[35 + 5 * f : 40 + 5 * f] = x[:5]
    for f in range(7):
        up[8 * f : 8 * f + 8] = s[f, 8:]
        dn[5 * f : 5 * f + 5] = s[f, :5]
    for i, f in enumerate((4, 5, 2, 6)):
        nodes = [s[f, 4 + l] for l in range(5)]
        up[104 + i] = combine(ROW[4], nodes)
        dn[65 + i] = combine(ROW[0], nodes)


def launch(s, vw, t_in, up, dn, coef, dr_m, items, pk, keep):
    has_below = coef[FLAGS]
    has_above = coef[FLAGS + 1]
    c = {name: coef[n] for n, name in enumerate(OWN)}
    for n, name in enumerate(SHARED):
        c[name] = c[name] + up[108 + n] + dn[69 + n]
    q = inverse_radius(0, NR)

    def radial(fields):
        stacked = jnp.concatenate([flat(x) for x in fields], axis=0)
        out = mm(stacked, dr_m[0], dr_m[1])
        count = fields[0].shape[0]
        return [out[8 * count * i : 8 * count * (i + 1)].reshape(count, 8, NR) for i in range(len(fields))]

    def ext(f):
        return jnp.concatenate([up[8 * f : 8 * f + 8], s[f], dn[5 * f : 5 * f + 5]], axis=0)

    def ext_v(f):
        return jnp.concatenate(
            [up[56 + 8 * f : 64 + 8 * f], vw[f], dn[35 + 5 * f : 40 + 5 * f]], axis=0
        )

    above29 = lax.broadcasted_iota(jnp.int32, (29, 8, NR), 0) < 24
    mask29 = jnp.where(above29, 1.0, has_above)
    rr, tt, zz, rt, rz, tz, p = [ext(f) for f in range(7)]
    cv, cf, cr = [spread_rows(c[n], 0, 7, True) for n in ("cv", "cf", "cr")]
    r_rr, r_rt, r_rz, r_p = radial([rr, rt, rz, p])
    z_rz, z_tz, z_zz, z_p = [
        depth_derivative(x, 0, 7, 2, has_below, up[104 + i], dn[65 + i]) for i, x in enumerate((rz, tz, zz, p))
    ]
    d_r = r_rr + z_rz + q * (rr - tt)
    d_t = r_rt + z_tz + 2.0 * q * rt
    d_z = r_rz + z_zz + q * rz
    v1 = [
        mask29 * (ext_v(0) + cv * d_r + cf * r_p),
        mask29 * (ext_v(1) + cv * d_t),
        mask29 * (ext_v(2) + cv * d_z + cf * z_p),
    ]
    w1 = [
        mask29 * (ext_v(3) - cf * d_r - cr * r_p),
        mask29 * (ext_v(4) - cf * d_t),
        mask29 * (ext_v(5) - cf * d_z - cr * z_p),
    ]
    q_rt, q_tt, q_tz, q_p = q * rt, q * tt, q * tz, q * p
    u = [cv * q_rt, cv * q_tt + cf * q_p, cv * q_tz]
    uw = [-(cf * q_rt), -(cf * q_tt + cr * q_p), -(cf * q_tz)]

    def pack(f, planes):
        for g in range(2):
            chunks = exchange_groups(planes[8 * g : 8 * g + 8])
            for k in range(8):
                pk[k, 2 * f + g] = chunks[k]

    for f, x in enumerate((3, 1, 5, 6)):
        pack(f, s[x])
    fric = spread_rows(c["fric"], 2, 4)
    kappa = spread_rows(c["kappa"], 2, 4)
    grads = (r_p, None, z_p)
    for i, d in enumerate((d_r, d_t, d_z)):
        g = fric * (t_in[i] + kappa * w1[i][8:24])
        if grads[i] is not None:
            g = g + grads[i][8:24]
        a = cv[8:24] * d[8:24] + cf[8:24] * g
        b = cf[8:24] * d[8:24] + cr[8:24] * g
        pack(4 + i, v1[i][8:24])
        pack(9 + i, a)
        keep[i] = v1[i][8:24]
        keep[3 + i] = w1[i][8:24]
        keep[6 + i] = a
        keep[9 + i] = b
        if i == 1:
            pack(7, w1[i][8:24])
            pack(12, b)

    bulk, couple, modulus, shear = [
        spread_rows(c[n], 1, 6)[:21] for n in ("bulk", "couple", "modulus", "shear")
    ]
    mask21 = jnp.where(lax.broadcasted_iota(jnp.int32, (21, 8, NR), 0) < 20, 1.0, has_above)
    plane21 = lax.broadcasted_iota(jnp.int32, (21, 8, NR), 0) - 4
    lane21 = lax.broadcasted_iota(jnp.int32, (21, 8, NR), 2)
    source = jnp.where((plane21.astype(F32) == coef[FLAGS + 2]) & (lane21 < 4 * RB), SOURCE, 0.0)

    def stresses(v, w, extra):
        inner = slice(4, 25)
        vr, vt, wr = v[0][inner], v[1][inner], w[0][inner]
        r_r, r_t, r_z, r_w = radial([vr, vt, v[2][inner], wr])
        z_r, z_t, z_z, z_w = [depth_derivative(x, 1, 6, 2, has_below) for x in (v[0], v[1], v[2], w[2])]
        e_tt, g_rt, g_tz, div_w = q * vr, r_t - q * vt, z_t, r_w + q * wr + z_w
        if extra is not None:
            e_tt, g_rt, g_tz, div_w = e_tt + extra[1], g_rt + extra[0], g_tz + extra[2], div_w + extra[3]
        div_v = r_r + e_tt + z_z
        total = bulk * div_v + couple * div_w
        return dict(
            rr=mask21 * (total + 2.0 * shear * r_r),
            zz=mask21 * (total + 2.0 * shear * z_z),
            rt=mask21 * (shear * g_rt),
            rz=mask21 * (shear * (z_r + r_z)),
            tz=mask21 * (shear * g_tz),
            p=mask21 * (-(couple * div_v + modulus * div_w) + (source if extra is None else 0.0)),
            w=div_w,
        )

    x0 = stresses(v1, w1, None)
    pack(8, x0["w"][4:20])
    inner = slice(4, 25)
    x1 = stresses(u, uw, [q * v1[0][inner], q * v1[1][inner], q * v1[2][inner], q * w1[1][inner]])
    e2, dw2 = q * u[1][inner], q * uw[1][inner]
    total2 = bulk * e2 + couple * dw2
    x2 = dict(
        rr=mask21 * total2,
        zz=mask21 * total2,
        rt=mask21 * (shear * (q * u[0][inner])),
        tz=mask21 * (shear * (q * u[2][inner])),
        p=mask21 * (-(couple * e2 + modulus * dw2)),
    )

    def radius_items(fields):
        slots = [i for i, x in enumerate(fields) if x is not None]
        stacked = jnp.concatenate([flat(fields[i]) for i in slots], axis=1)
        hi, lo = [jnp.concatenate([items[h, NR * i : NR * i + NR] for i in slots], axis=0) for h in range(2)]
        return mm(stacked, hi, lo).reshape(-1, 8, NR)

    def depth_items(fields, first):
        out = []
        for x in fields:
            if x is None:
                out += [jnp.zeros((8, NR), F32)] * 2
            else:
                out.append(x[first + 20])
                out.append(has_below * below_partial(x[first : first + 4]))
        return jnp.stack(out)

    velocity_r = [v1[0][8:24], v1[1][8:24], v1[2][8:24], None] + [x[8:24] for x in (u[0], u[1], u[2], uw[0])]
    pack(13, radius_items(velocity_r))
    names_r = ("rr", "rt", "rz", "p")
    pack(14, radius_items([x[n][4:20] for x in (x0, x1) for n in names_r]))
    pack(15, depth_items([v1[0], v1[1], v1[2], None, u[0], u[1], u[2], uw[2]], 4))
    names_z = ("rz", "tz", "zz", "p")
    pack(16, depth_items([x[n] for x in (x0, x1) for n in names_z], 0))
    second = [x2[n][4 + 8 * h : 12 + 8 * h] if n in x2 else None for h in range(2) for n in names_r]
    pack(17, jnp.concatenate([radius_items(second), depth_items([x2.get(n) for n in names_z], 0)], axis=0))


def ring(
    recv, coef, dt_hbm, mr_hbm, mz_hbm, wr_hbm, wz_hbm, out, dt_m, mr, mz, wr, wz, sems
):
    group = lax.axis_index("az")
    first_r = jnp.where(group == 0, 1, 0)
    first_z = jnp.where(lax.axis_index("depth") == 0, 1, 0)
    sources = (dt_hbm, wr_hbm, wz_hbm, mr_hbm.at[first_r], mz_hbm.at[first_z])
    copies = [
        pltpu.make_async_copy(a, b, sems.at[i]) for i, (a, b) in enumerate(zip(sources, (dt_m, wr, wz, mr, mz)))
    ]
    for copy in copies:
        copy.start()
    c = {name: coef[n] for n, name in enumerate(RING)}
    q = inverse_radius(group, GROUP)
    for copy in copies:
        copy.wait()

    def field(f):
        return jnp.concatenate([recv[:, 2 * f], recv[:, 2 * f + 1]], axis=-1)

    def az(fields):
        x = jnp.concatenate([y.reshape(NT, -1) for y in fields], axis=1)
        xh, xl = parts(x)
        y = dot(dt_m[0], xh) + dot(dt_m[0], xl) + dot(dt_m[1], xh)
        res, at = [], 0
        for f in fields:
            n = f.shape[-1]
            res.append(y[:, at : at + n].reshape(f.shape))
            at += n
        return res

    def by_half(x):
        x = x.reshape(NT, 256)
        return [x[:, :128], x[:, 128:]]

    mr_h, mr_l = mr[0], mr[1]
    mz_h, mz_l = mz[0], mz[1]

    def radial(fields, halo):
        stacked = jnp.concatenate([h for f in fields for h in by_half(f)], axis=0)
        y = mm(stacked, mr_h, mr_l)
        res = []
        for i in range(len(fields)):
            halves_ = [
                y[128 * i + 64 * g : 128 * i + 64 * g + 64] + halo[64 * g : 64 * g + 64, 128 * i : 128 * i + 128]
                for g in range(2)
            ]
            res.append(jnp.concatenate(halves_, axis=1).reshape(8, 8, 256))
        return res

    def depth(fields, halo):
        stacked = jnp.concatenate([f.reshape(NT, 256) for f in fields], axis=0)
        y = mm(stacked, mz_h, mz_l)
        return [
            (y[64 * i : 64 * i + 64] + halo[:, 256 * i : 256 * i + 256]).reshape(8, 8, 256)
            for i in range(len(fields))
        ]

    rt, tt, tz, p = [field(f) for f in range(4)]
    pr2, pr3 = field(13), field(14)
    pd2 = [recv[:, 30], recv[:, 31]]
    pd3 = [recv[:, 32], recv[:, 33]]
    px = field(17)
    s_rt, s_tt, s_tz, s_p, d_pr2, d_pr3, d_pd2, d_pd3, d_px = az([rt, tt, tz, p, pr2, pr3, pd2[1], pd3[1], px])
    (dd_px,) = az([d_px])
    wr0, wr1 = (wr[0, 0], wr[0, 1]), (wr[1, 0], wr[1, 1])

    def stack_halves(x):
        return jnp.concatenate(by_half(x), axis=0)

    def radius_halo(zero, one):
        return mm(stack_halves(zero), *wr0) + mm(stack_halves(one), *wr1)

    hr2 = radius_halo(pr2, d_pr2)
    hz2 = mm((pd2[0] + d_pd2).reshape(NT, 128), wz[0], wz[1])
    half = dd_px.reshape(NT, 256)[:, :128]
    hr3 = radius_halo(pr3, d_pr3) + jnp.concatenate([mm(half, *wr0), mm(half, *wr1)], axis=0)
    hz3 = mm((pd3[0] + d_pd3).reshape(NT, 128) + dd_px.reshape(NT, 256)[:, 128:], wz[0], wz[1])

    cv, cf, cr = c["cv"], c["cf"], c["cr"]
    q_rt, q_tt, q_tz, q_p = q * s_rt, q * s_tt, q * s_tz, q * s_p
    dw = [-(cf * q_rt), -(cf * q_tt + cr * q_p), -(cf * q_tz)]
    v1 = [
        field(4) + cv * q_rt,
        field(5) + cv * q_tt + cf * q_p,
        field(6) + cv * q_tz,
    ]
    w1_t = field(7) + dw[1]
    r_r, r_t, r_z, r_w = radial([v1[0], v1[1], v1[2], dw[0]], hr2)
    z_r, z_t, z_z, z_w = depth([v1[0], v1[1], v1[2], dw[2]], hz2)
    a_r, a_t, a_z, a_w = az([v1[0], v1[1], v1[2], w1_t])
    e_tt = q * (v1[0] + a_t)
    div_v = r_r + e_tt + z_z
    div_w = field(8) + r_w + q * (dw[0] + a_w) + z_w
    total = c["bulk"] * div_v + c["couple"] * div_w
    shear = c["shear"]
    lanes = lax.broadcasted_iota(jnp.int32, (8, 256), 1) // GROUP
    source = jnp.where(lanes.astype(F32) == coef[len(RING)], jnp.where(group == 0, SOURCE, 0.0), 0.0)
    n_rr = total + 2.0 * shear * r_r
    n_tt = total + 2.0 * shear * e_tt
    n_zz = total + 2.0 * shear * z_z
    n_rt = shear * (q * (a_r - v1[1]) + r_t)
    n_rz = shear * (z_r + r_z)
    n_tz = shear * (z_t + q * a_z)
    n_p = source - (c["couple"] * div_v + c["modulus"] * div_w)

    r_rr, r_rt, r_rz, r_p = radial([n_rr, n_rt, n_rz, n_p], hr3)
    z_rz, z_tz, z_zz, z_p = depth([n_rz, n_tz, n_zz, n_p], hz3)
    a_rt, a_tt, a_tz, a_p = az([n_rt, n_tt, n_tz, n_p])
    d_r = q_rt + r_rr + z_rz + q * (a_rt + n_rr - n_tt)
    d_t = q_tt + r_rt + z_tz + q * (a_tt + 2.0 * n_rt)
    d_z = q_tz + r_rz + z_zz + q * (a_tz + n_rz)
    fk = c["fk"]
    g_r = r_p + fk * dw[0]
    g_t = q_p + q * a_p + fk * dw[1]
    g_z = z_p + fk * dw[2]
    sums = [
        2.0 * v1[0] + field(9) + cv * d_r + cf * g_r,
        2.0 * v1[1] + field(10) + cv * d_t + cf * g_t,
        2.0 * v1[2] + field(11) + cv * d_z + cf * g_z,
        2.0 * w1_t - field(12) - cf * d_t - cr * g_t,
    ]
    results = [s_rt, s_tt, s_tz, s_p, d_r, d_t, d_z, g_r, g_t, g_z] + az(sums)
    for f, x in enumerate(results):
        out[:, 2 * f] = x[:, :, :128]
        out[:, 2 * f + 1] = x[:, :, 128:]


def unpack(recv, f):
    planes = []
    for g in range(2):
        planes += exchange_groups([recv[k, 2 * f + g] for k in range(8)])
    return jnp.stack(planes)


def advance(recv, keep, coef, v_out, mid, up, dn):
    c = {name: coef[n] for n, name in enumerate(OWN)}
    q = inverse_radius(0, NR)
    cv, cf, cr = [spread_rows(c[n], 2, 4) for n in ("cv", "cf", "cr")]
    q_rt, q_tt, q_tz, q_p = [q * unpack(recv, f) for f in range(4)]
    dv = [cv * q_rt, cv * q_tt + cf * q_p, cv * q_tz]
    dw = [-(cf * q_rt), -(cf * q_tt + cr * q_p), -(cf * q_tz)]
    for i in range(3):
        d, g = unpack(recv, 4 + i), unpack(recv, 7 + i)
        v1 = keep[i] + dv[i]
        w1 = keep[3 + i] + dw[i]
        v2 = v1 + keep[6 + i] + cv * d + cf * g
        w2 = w1 - keep[9 + i] - cf * d - cr * g
        v_out[i] = v2
        v_out[3 + i] = w2
        mid[i] = v1
        mid[3 + i] = w1
        x = v1 + v2
        up[i] = below_partial(x[12:])
        dn[i] = x[0]
        if i == 2:
            x = w1 + w2
            up[3] = below_partial(x[12:])
            dn[3] = x[0]


def settle(recv, v2, mid, v, s, psi, coef, dr_m, s_out, m_out, edge):
    has_below = coef[FLAGS]
    c = {name: coef[n] for n, name in enumerate(OWN)}
    q = inverse_radius(0, NR)

    def sp(value):
        return spread_rows(value, 2, 4)

    omega = sp(c["omega"])
    decay = [sp(c[f"decay{l}"]) for l in range(4)]
    for i in range(3):
        w1, w2 = mid[3 + i], v2[3 + i]
        first = w1 - v[3 + i] + omega * w1
        second = w2 - w1 + omega * w2
        for l in range(4):
            m_out[3 * l + i] = decay[l] * (decay[l] * (psi[3 * l + i] + first) + second)
    sums = [mid[i] + v2[i] for i in range(6)]
    zero = jnp.zeros((1, 8, NR), F32)
    z_r, z_t, z_z, z_w = [
        depth_derivative(jnp.concatenate([x, zero], axis=0), 0, 4, 0, has_below, float(ROW[4, 4]) * x[0], zero[0])[:16]
        for x in (sums[0], sums[1], sums[2], sums[5])
    ]
    stacked = jnp.concatenate([flat(x) for x in sums[:4]], axis=0)
    y = mm(stacked, dr_m[0], dr_m[1])
    r_r, r_t, r_z, r_w = [y[128 * i : 128 * i + 128].reshape(16, 8, NR) for i in range(4)]
    a_r, a_t, a_z, a_w = [unpack(recv, 10 + i) for i in range(4)]
    e_tt = q * (sums[0] + a_t)
    div_v = r_r + e_tt + z_z
    div_w = r_w + q * (sums[3] + a_w) + z_w
    couple, shear = sp(c["couple"]), sp(c["shear"])
    total = sp(c["bulk"]) * div_v + couple * div_w
    plane = lax.broadcasted_iota(jnp.int32, (16, 8, NR), 0)
    lane = lax.broadcasted_iota(jnp.int32, (16, 8, NR), 2)
    source = jnp.where((plane.astype(F32) == coef[FLAGS + 2]) & (lane < 4 * RB), SOURCE * (1.0 + math.cos(0.9)), 0.0)
    updates = [
        total + 2.0 * shear * r_r,
        total + 2.0 * shear * e_tt,
        total + 2.0 * shear * z_z,
        shear * (q * (a_r - sums[1]) + r_t),
        shear * (z_r + r_z),
        shear * (z_t + q * a_z),
        source - (couple * div_v + sp(c["modulus"]) * div_w),
    ]
    for f, x in enumerate(updates):
        x = s[f] + x
        s_out[f] = x
        edge[f, 0] = x[0]
        edge[f, 1:] = x[12:]


def close(s_in, edge, up, dn, coef, s_out, new, sems):
    has_below = coef[FLAGS]
    c = {name: coef[n] for n, name in enumerate(OWN)}

    def update(slot, row, z_r, z_t, z_z, z_w):
        def at(name):
            return jnp.broadcast_to(c[name][row : row + 1, :], (8, NR))

        bulk, couple, modulus, shear = at("bulk"), at("couple"), at("modulus"), at("shear")
        total = bulk * z_z + couple * z_w
        new[0, slot] = edge[0, slot] + total
        new[1, slot] = edge[1, slot] + total
        new[2, slot] = edge[2, slot] + total + 2.0 * shear * z_z
        new[3, slot] = edge[3, slot]
        new[4, slot] = edge[4, slot] + shear * z_r
        new[5, slot] = edge[5, slot] + shear * z_t
        new[6, slot] = edge[6, slot] - (couple * z_z + modulus * z_w)

    update(0, 2, *[has_below * up[i] for i in range(4)])
    for slot in range(1, 5):
        weight = float(ROW[slot - 1, 4])
        update(slot, 5, *[weight * dn[i] for i in range(4)])
    copies = [
        pltpu.make_async_copy(new.at[:, 0:1], s_out.at[:, 0:1], sems.at[0]),
        pltpu.make_async_copy(new.at[:, 1:5], s_out.at[:, 12:16], sems.at[1]),
    ]
    for copy in copies:
        copy.start()
    for copy in copies:
        copy.wait()


def call(body, inputs, shapes, hbm=(), scratch=(), out_hbm=False, alias=None, micros=1, vmem=VMEM_LIMIT):
    def space(i):
        return pltpu.HBM if i in hbm else pltpu.VMEM

    return pl.pallas_call(
        body,
        out_shape=[jax.ShapeDtypeStruct(x, F32) for x in shapes],
        in_specs=[pl.BlockSpec(memory_space=space(i)) for i in range(len(inputs))],
        out_specs=[pl.BlockSpec(memory_space=pltpu.HBM if out_hbm else pltpu.VMEM) for _ in shapes],
        scratch_shapes=list(scratch),
        input_output_aliases=alias or {},
        compiler_params=pltpu.CompilerParams(vmem_limit_bytes=vmem),
        cost_estimate=pl.CostEstimate(flops=0, bytes_accessed=3 * 10**6 * micros, transcendentals=0),
        name=body.__name__,
    )(*inputs)


def shift(value, steps):
    count = lax.axis_size("depth")
    first, last = max(0, -steps), min(count, count - steps)
    return lax.ppermute(value, "depth", [(i, i + steps) for i in range(first, last)])


def on_device(velocity, stress, memory, layer_ids, materials, jkd, source_depth):
    c = constants()
    block = (PLANES, AZ, NR)
    tables = [layer_ids, materials, jkd, source_depth]
    vw, t_part, up, dn, coef, ring_coef = call(
        prepare,
        tables + [memory, velocity, stress],
        [(6,) + block, (3,) + block, (115, AZ, NR), (76, AZ, NR), (FLAGS + 3, 8, NR), (len(RING) + 1, 8, 256)],
        hbm=range(7),
        scratch=[pltpu.SMEM(x.shape, x.dtype) for x in tables]
        + [pltpu.VMEM((n,) + block, F32) for n in (12, 6, 7)]
        + [pltpu.SemaphoreType.DMA((7,))],
        vmem=VMEM_FULL,
    )
    up, dn = shift(up, 1), shift(dn, -1)
    packed, keep = call(
        launch,
        [stress, vw, t_part, up, dn, coef, c["dr"], c["items"]],
        [(8, 2 * FIELDS_IN, AZ, NR), (12,) + block],
        micros=4,
    )
    packed = lax.all_to_all(packed, "az", split_axis=0, concat_axis=0, tiled=True)
    matrices = [c[n] for n in ("dt", "mr", "mz", "wr", "wz")]
    shapes = [m.shape[1:] if n in (1, 2) else m.shape for n, m in enumerate(matrices)]
    (back,) = call(
        ring,
        [packed, ring_coef] + matrices,
        [(8, 2 * FIELDS_OUT, AZ, NR)],
        hbm=range(2, 7),
        scratch=[pltpu.VMEM(x, BF16) for x in shapes] + [pltpu.SemaphoreType.DMA((5,))],
        micros=3,
        vmem=VMEM_FULL,
    )
    back = lax.all_to_all(back, "az", split_axis=0, concat_axis=0, tiled=True)
    v_out, mid, up, dn = call(
        advance,
        [back, keep, coef],
        [(6,) + block, (6,) + block, (4, AZ, NR), (4, AZ, NR)],
    )
    up, dn = shift(up, 1), shift(dn, -1)
    s_part, m_out, edge = call(
        settle,
        [back, v_out, mid, velocity, stress, memory, coef, c["dr"]],
        [(7,) + block, (12,) + block, (7, 5, AZ, NR)],
        micros=3,
    )
    (s_out,) = call(
        close,
        [s_part, edge, up, dn, coef],
        [(7,) + block],
        hbm=(0,),
        scratch=[pltpu.VMEM((7, 5, AZ, NR), F32), pltpu.SemaphoreType.DMA((2,))],
        out_hbm=True,
        alias={0: 0},
    )
    return v_out, s_out, m_out


def solution(mesh):
    field = P(None, "depth", "az", None)
    return jax.shard_map(
        on_device,
        mesh=mesh,
        in_specs=(field, field, field, P("depth", None), P(), P(), P()),
        out_specs=(field, field, field),
        check_vma=False,
    )
```

```python
import functools
import math

import jax
import jax.numpy as jnp
import ml_dtypes
import numpy as np
from jax import lax
from jax.experimental import pallas as pl
from jax.experimental.pallas import tpu as pltpu
from jax.sharding import PartitionSpec as P

NR = 128
NT = 64
RB = 4
PLANES = 16
AZ = 8
GROUP = 16
DT = 0.02
SOURCE = DT * 40.0
R_INNER = 1.0
F32 = jnp.float32
BF16 = jnp.bfloat16
FIELDS_IN = 18
FIELDS_OUT = 14
VMEM_LIMIT = 32 * 2**20
VMEM_FULL = 56 * 2**20
SHARED = ("cv", "cf", "cr", "bulk", "couple", "modulus", "shear")
OWN = SHARED + ("fric", "kappa", "omega", "decay0", "decay1", "decay2", "decay3")
FLAGS = len(OWN)
COEF = 9 * PLANES
RING = SHARED + ("fk",)


def gll_basis():
    root_value = math.sqrt(3.0 / 7.0)
    nodes = np.array([-1.0, -root_value, 0.0, root_value, 1.0])
    weights = np.array([0.1, 49.0 / 90.0, 32.0 / 45.0, 49.0 / 90.0, 0.1])
    offsets = nodes[:, None] - nodes[None, :] + np.eye(5)
    factors = np.prod(offsets, axis=1)
    derivative = factors[:, None] / factors[None, :] / offsets
    diagonal = np.sum(1.0 / offsets, axis=1) - 1.0
    derivative = derivative * (1.0 - np.eye(5)) + np.eye(5) * diagonal[:, None]
    return nodes, weights, derivative


NODES, WEIGHTS, DERIV = gll_basis()
ROW = DERIV * np.array([1.0, 2.0, 2.0, 2.0, 1.0])[:, None]


def line_operator(count, first):
    matrix = np.zeros((count + 1, count + 1))
    for e in range(count // 4):
        matrix[4 * e : 4 * e + 5, 4 * e : 4 * e + 5] += ROW
    if first:
        matrix[0] *= 2.0
    else:
        matrix[0, 0] += ROW[4, 4]
    return matrix[:count, :count]


def halves(matrix):
    hi = matrix.astype(np.float32).astype(ml_dtypes.bfloat16)
    lo = (matrix - hi.astype(np.float64)).astype(np.float32).astype(ml_dtypes.bfloat16)
    return np.stack([hi, lo])


def azimuth_operator():
    positions = np.arange(NT)
    offsets = positions[:, None] - positions[None, :]
    modes = np.arange(1, NT // 2)
    phases = 2.0 * np.pi * offsets[:, :, None] * modes / NT
    return -(2.0 / NT) * np.sum(modes * np.sin(phases), axis=2)


@functools.lru_cache(None)
def constants():
    groups = NR // GROUP
    c = {}
    c["dr"] = halves(line_operator(NR, True).T)
    items = np.zeros((8, NR, groups, 16))
    for s in range(8):
        for k in range(groups):
            if GROUP * (k + 1) < NR:
                items[s, GROUP * (k + 1), k, 2 * s] = 1.0
            if k:
                items[s, GROUP * k - 4 : GROUP * k, k, 2 * s + 1] = ROW[4, :4]
    c["items"] = halves(items.reshape(8 * NR, 128))
    c["dt"] = halves(azimuth_operator())
    c["mr"] = np.stack([halves(np.kron(np.eye(8), line_operator(16, first).T)) for first in (False, True)])
    c["mz"] = np.stack([halves(np.kron(line_operator(16, first).T, np.eye(16))) for first in (False, True)])
    spread = np.zeros((2, 16))
    spread[0, 12:] = ROW[:4, 4]
    spread[1, 0] = 1.0
    wr = np.zeros((2, 8, 16, 4, 8, 16))
    wz = np.zeros((8, 16, 4, 16, 16))
    for f in range(4):
        for side in range(2):
            for j in range(8):
                for order in range(2):
                    wr[order, j, 8 * order + 2 * f + side, f, j] = spread[side]
            for r in range(16):
                wz[2 * f + side, r, f, :, r] = spread[side]
    c["wr"] = np.stack([halves(w) for w in wr.reshape(2, 128, 512)])
    c["wz"] = halves(wz.reshape(128, 1024))
    return c


def roll(x, shift):
    return pltpu.roll(x, shift % x.shape[-1], x.ndim - 1)


def dot(a, b):
    return jnp.dot(a, b, preferred_element_type=F32)


def parts(x):
    hi = x.astype(BF16)
    return hi, (x - hi.astype(F32)).astype(BF16)


def mm(x, hi, lo):
    xh, xl = parts(x)
    return dot(xh, hi) + dot(xl, hi) + dot(xh, lo)


def inverse_radius(group, width):
    lane = lax.broadcasted_iota(jnp.int32, (8, 128 if width == NR else 256), 1) % width
    place = lane % 4
    offset = jnp.zeros(lane.shape, F32)
    for j in range(4):
        offset = jnp.where(place == j, float(R_INNER + 0.5 * (1.0 + NODES[j])), offset)
    return 1.0 / (offset + (lane // 4 + 4 * group).astype(F32))


def own_ids(lids):
    row = lax.broadcasted_iota(jnp.int32, (8, NR), 0)
    fluid = lax.broadcasted_iota(jnp.int32, (8, NR), 1) < 4 * RB
    value = jnp.zeros((8, NR), jnp.int32)
    for e in range(4):
        value = jnp.where(row == 2 + e, jnp.where(fluid, lids[e, 0], lids[e, NR // 4 - 1]), value)
    return value.astype(F32)


def coefficients(ids, tab):
    hits = [ids == float(m) for m in range(8)]
    materials, jkd = tab

    def pick(table, column):
        value = jnp.where(hits[0], table[0, column], 0.0)
        for m in range(1, 8):
            value = jnp.where(hits[m], table[m, column], value)
        return value

    lame, mu, modulus, beta, rho, rho_f, tort, fric = [pick(materials, c) for c in range(8)]
    omega = pick(jkd, 0)
    weights = [pick(jkd, 1 + l) for l in range(4)]
    rates = [pick(jkd, 5 + l) for l in range(4)]
    rho_w = tort * rho_f
    scale = DT / (rho * rho_w - rho_f * rho_f)
    decay = [1.0 / (1.0 + DT * (rate + omega)) for rate in rates]
    gain = sum(a * c for a, c in zip(weights, decay))
    return dict(
        cv=rho_w * scale,
        cf=rho_f * scale,
        cr=rho * scale,
        fric=fric,
        omega=DT * omega,
        weights=weights,
        decay=decay,
        decay0=decay[0],
        decay1=decay[1],
        decay2=decay[2],
        decay3=decay[3],
        kappa=(1.0 + DT * omega) * gain,
        fk=fric * ((1.0 + DT * omega) * gain),
        bulk=DT * (lame + beta * beta * modulus),
        couple=DT * beta * modulus,
        modulus=DT * modulus,
        shear=DT * mu,
    )


def spread_rows(value, first, count, tail=False):
    rows = [jnp.broadcast_to(value[first + e : first + e + 1, :], (8, NR)) for e in range(count + tail)]
    planes = [rows[i // 4] for i in range(4 * count + tail)]
    return jnp.stack(planes)


def combine(row, nodes):
    total = None
    for weight, node in zip(row, nodes):
        term = float(weight) * node
        total = term if total is None else total + term
    return total


def depth_derivative(x, lo, hi, edge, has_below, low=None, high=None):
    count = (x.shape[0] - 1) // 4
    blocks = x[: 4 * count].reshape((count, 4) + x.shape[1:])
    last = [blocks[e + 1, 0] if e + 1 < count else x[4 * count] for e in range(count)]

    def nodes(e):
        return [blocks[e, l] for l in range(4)] + [last[e]]

    out = []
    for e in range(lo, hi + 1):
        upper = combine(ROW[0], nodes(e)) if e < count else high
        lower = combine(ROW[4], nodes(e - 1)) if e > 0 else low
        if e == edge:
            upper = (2.0 - has_below) * upper
            lower = has_below * lower
        out.append(upper + lower)
        if e < hi:
            for i in range(1, 4):
                out.append(combine(ROW[i], nodes(e)))
    return jnp.stack(out)


def below_partial(x):
    return combine(ROW[4, :4], [x[l] for l in range(4)])


def lane_groups():
    return lax.broadcasted_iota(jnp.int32, (8, NR), 1) // GROUP


def exchange_groups(x):
    groups = lane_groups()
    rows = [x[j] for j in range(8)]
    for s in (4, 2, 1):
        low = (groups & s) == 0
        for j in range(8):
            if not j & s:
                a, b = rows[j], rows[j + s]
                rows[j] = jnp.where(low, a, roll(b, GROUP * s))
                rows[j + s] = jnp.where(low, roll(a, -GROUP * s), b)
    return rows


def flat(x):
    return x.reshape(-1, NR)


def prepare(
    lids_hbm, mat_hbm, jkd_hbm, src_hbm, psi_hbm, v_hbm, s_hbm,
    state, up, dn, ring_coef,
    lids, mat, jkd, src, psi, v, s, sems,
):
    pairs = (
        (lids_hbm, lids), (mat_hbm, mat), (jkd_hbm, jkd), (src_hbm, src), (psi_hbm, psi), (v_hbm, v), (s_hbm, s)
    )
    copies = [pltpu.make_async_copy(a, b, sems.at[i]) for i, (a, b) in enumerate(pairs)]
    for copy in copies:
        copy.start()
    for copy in copies[:4]:
        copy.wait()
    device = lax.axis_index("depth")
    rows = lax.broadcasted_iota(jnp.int32, (8, NR), 0)
    c = coefficients(own_ids(lids), (mat, jkd))
    mine = (rows >= 2) & (rows < 6)
    for n, name in enumerate(OWN):
        state[COEF + n] = jnp.where(mine, c[name], 0.0)
    source = (src[0] - PLANES * device).astype(F32)
    state[COEF + FLAGS] = jnp.full((8, NR), jnp.where(device > 0, 1.0, 0.0), F32)
    state[COEF + FLAGS + 1] = jnp.full((8, NR), jnp.where(device < lax.axis_size("depth") - 1, 1.0, 0.0), F32)
    state[COEF + FLAGS + 2] = jnp.full((8, NR), source, F32)
    for n, name in enumerate(SHARED):
        swapped = pltpu.roll(c[name], 4, 0)
        up[108 + n] = jnp.where(rows < 2, swapped, 0.0)
        dn[69 + n] = jnp.where(rows >= 6, swapped, 0.0)
    element = lax.broadcasted_iota(jnp.int32, (8, 256), 1) // 64
    group = lax.axis_index("az")
    ids = jnp.zeros((8, 256), jnp.int32)
    for e in range(4):
        ids = jnp.where(element == e, lids[e, 4 * group], ids)
    rc = coefficients(ids.astype(F32), (mat, jkd))
    for n, name in enumerate(RING):
        ring_coef[n] = rc[name]
    ring_coef[len(RING)] = jnp.full((8, 256), source, F32)

    def sp(value):
        return spread_rows(value, 2, 4)

    weights = [sp(w) for w in c["weights"]]
    cf = sp(c["cf"] * c["fric"])
    cr = sp(c["cr"] * c["fric"])
    decayed = [sp(w * d) for w, d in zip(c["weights"], c["decay"])]
    for copy in copies[4:]:
        copy.wait()
    for i in range(3):
        memory = [psi[3 * l + i] for l in range(4)]
        total = sum(w * m for w, m in zip(weights, memory))
        state[96 + 16 * i : 112 + 16 * i] = sum(w * (m - v[3 + i]) for w, m in zip(decayed, memory))
        vi = v[i] + cf * total
        wi = v[3 + i] - cr * total
        for f, x in ((i, vi), (3 + i, wi)):
            state[16 * f : 16 * f + 16] = x
            up[56 + 8 * f : 64 + 8 * f] = x[8:]
            dn[35 + 5 * f : 40 + 5 * f] = x[:5]
    for f in range(7):
        up[8 * f : 8 * f + 8] = s[f, 8:]
        dn[5 * f : 5 * f + 5] = s[f, :5]
    for i, f in enumerate((4, 5, 2, 6)):
        nodes = [s[f, 4 + l] for l in range(5)]
        up[104 + i] = combine(ROW[4], nodes)
        dn[65 + i] = combine(ROW[0], nodes)


def stage(*refs):
    *pairs, sems = refs
    count = 6
    first_r = jnp.where(lax.axis_index("az") == 0, 1, 0)
    first_z = jnp.where(lax.axis_index("depth") == 0, 1, 0)
    sources = list(pairs[:count])
    sources[0] = sources[0].at[first_r]
    sources[1] = sources[1].at[first_z]
    state = sources.pop()
    sources += [state.at[0:96], state.at[96:COEF], state.at[COEF:]]
    copies = [pltpu.make_async_copy(a, b, sems.at[i]) for i, (a, b) in enumerate(zip(sources, pairs[count:]))]
    for copy in copies:
        copy.start()
    for copy in copies:
        copy.wait()


def launch(s, vw, t_in, up, dn, coef, dr_m, items, pk, keep):
    has_below = coef[FLAGS]
    has_above = coef[FLAGS + 1]
    c = {name: coef[n] for n, name in enumerate(OWN)}
    for n, name in enumerate(SHARED):
        c[name] = c[name] + up[108 + n] + dn[69 + n]
    q = inverse_radius(0, NR)

    def radial(fields):
        stacked = jnp.concatenate([flat(x) for x in fields], axis=0)
        out = mm(stacked, dr_m[0], dr_m[1])
        count = fields[0].shape[0]
        return [out[8 * count * i : 8 * count * (i + 1)].reshape(count, 8, NR) for i in range(len(fields))]

    def ext(f):
        return jnp.concatenate([up[8 * f : 8 * f + 8], s[f], dn[5 * f : 5 * f + 5]], axis=0)

    def ext_v(f):
        return jnp.concatenate(
            [up[56 + 8 * f : 64 + 8 * f], vw[16 * f : 16 * f + 16], dn[35 + 5 * f : 40 + 5 * f]], axis=0
        )

    above29 = lax.broadcasted_iota(jnp.int32, (29, 8, NR), 0) < 24
    mask29 = jnp.where(above29, 1.0, has_above)
    rr, tt, zz, rt, rz, tz, p = [ext(f) for f in range(7)]
    cv, cf, cr = [spread_rows(c[n], 0, 7, True) for n in ("cv", "cf", "cr")]
    r_rr, r_rt, r_rz, r_p = radial([rr, rt, rz, p])
    z_rz, z_tz, z_zz, z_p = [
        depth_derivative(x, 0, 7, 2, has_below, up[104 + i], dn[65 + i]) for i, x in enumerate((rz, tz, zz, p))
    ]
    d_r = r_rr + z_rz + q * (rr - tt)
    d_t = r_rt + z_tz + 2.0 * q * rt
    d_z = r_rz + z_zz + q * rz
    v1 = [
        mask29 * (ext_v(0) + cv * d_r + cf * r_p),
        mask29 * (ext_v(1) + cv * d_t),
        mask29 * (ext_v(2) + cv * d_z + cf * z_p),
    ]
    w1 = [
        mask29 * (ext_v(3) - cf * d_r - cr * r_p),
        mask29 * (ext_v(4) - cf * d_t),
        mask29 * (ext_v(5) - cf * d_z - cr * z_p),
    ]
    q_rt, q_tt, q_tz, q_p = q * rt, q * tt, q * tz, q * p
    u = [cv * q_rt, cv * q_tt + cf * q_p, cv * q_tz]
    uw = [-(cf * q_rt), -(cf * q_tt + cr * q_p), -(cf * q_tz)]

    def pack(f, planes):
        for g in range(2):
            chunks = exchange_groups(planes[8 * g : 8 * g + 8])
            for k in range(8):
                pk[k, 2 * f + g] = chunks[k]

    for f, x in enumerate((3, 1, 5, 6)):
        pack(f, s[x])
    fric = spread_rows(c["fric"], 2, 4)
    kappa = spread_rows(c["kappa"], 2, 4)
    grads = (r_p, None, z_p)
    for i, d in enumerate((d_r, d_t, d_z)):
        g = fric * (t_in[16 * i : 16 * i + 16] + kappa * w1[i][8:24])
        if grads[i] is not None:
            g = g + grads[i][8:24]
        a = cv[8:24] * d[8:24] + cf[8:24] * g
        b = cf[8:24] * d[8:24] + cr[8:24] * g
        pack(4 + i, v1[i][8:24])
        pack(9 + i, a)
        keep[i] = v1[i][8:24]
        keep[3 + i] = w1[i][8:24]
        keep[6 + i] = a
        keep[9 + i] = b
        if i == 1:
            pack(7, w1[i][8:24])
            pack(12, b)

    bulk, couple, modulus, shear = [
        spread_rows(c[n], 1, 6)[:21] for n in ("bulk", "couple", "modulus", "shear")
    ]
    mask21 = jnp.where(lax.broadcasted_iota(jnp.int32, (21, 8, NR), 0) < 20, 1.0, has_above)
    plane21 = lax.broadcasted_iota(jnp.int32, (21, 8, NR), 0) - 4
    lane21 = lax.broadcasted_iota(jnp.int32, (21, 8, NR), 2)
    source = jnp.where((plane21.astype(F32) == coef[FLAGS + 2]) & (lane21 < 4 * RB), SOURCE, 0.0)

    def stresses(v, w, extra):
        inner = slice(4, 25)
        vr, vt, wr = v[0][inner], v[1][inner], w[0][inner]
        r_r, r_t, r_z, r_w = radial([vr, vt, v[2][inner], wr])
        z_r, z_t, z_z, z_w = [depth_derivative(x, 1, 6, 2, has_below) for x in (v[0], v[1], v[2], w[2])]
        e_tt, g_rt, g_tz, div_w = q * vr, r_t - q * vt, z_t, r_w + q * wr + z_w
        if extra is not None:
            e_tt, g_rt, g_tz, div_w = e_tt + extra[1], g_rt + extra[0], g_tz + extra[2], div_w + extra[3]
        div_v = r_r + e_tt + z_z
        total = bulk * div_v + couple * div_w
        return dict(
            rr=mask21 * (total + 2.0 * shear * r_r),
            zz=mask21 * (total + 2.0 * shear * z_z),
            rt=mask21 * (shear * g_rt),
            rz=mask21 * (shear * (z_r + r_z)),
            tz=mask21 * (shear * g_tz),
            p=mask21 * (-(couple * div_v + modulus * div_w) + (source if extra is None else 0.0)),
            w=div_w,
        )

    x0 = stresses(v1, w1, None)
    pack(8, x0["w"][4:20])
    inner = slice(4, 25)
    x1 = stresses(u, uw, [q * v1[0][inner], q * v1[1][inner], q * v1[2][inner], q * w1[1][inner]])
    e2, dw2 = q * u[1][inner], q * uw[1][inner]
    total2 = bulk * e2 + couple * dw2
    x2 = dict(
        rr=mask21 * total2,
        zz=mask21 * total2,
        rt=mask21 * (shear * (q * u[0][inner])),
        tz=mask21 * (shear * (q * u[2][inner])),
        p=mask21 * (-(couple * e2 + modulus * dw2)),
    )

    def radius_items(fields):
        slots = [i for i, x in enumerate(fields) if x is not None]
        stacked = jnp.concatenate([flat(fields[i]) for i in slots], axis=1)
        hi, lo = [jnp.concatenate([items[h, NR * i : NR * i + NR] for i in slots], axis=0) for h in range(2)]
        return mm(stacked, hi, lo).reshape(-1, 8, NR)

    def depth_items(fields, first):
        out = []
        for x in fields:
            if x is None:
                out += [jnp.zeros((8, NR), F32)] * 2
            else:
                out.append(x[first + 20])
                out.append(has_below * below_partial(x[first : first + 4]))
        return jnp.stack(out)

    velocity_r = [v1[0][8:24], v1[1][8:24], v1[2][8:24], None] + [x[8:24] for x in (u[0], u[1], u[2], uw[0])]
    pack(13, radius_items(velocity_r))
    names_r = ("rr", "rt", "rz", "p")
    pack(14, radius_items([x[n][4:20] for x in (x0, x1) for n in names_r]))
    pack(15, depth_items([v1[0], v1[1], v1[2], None, u[0], u[1], u[2], uw[2]], 4))
    names_z = ("rz", "tz", "zz", "p")
    pack(16, depth_items([x[n] for x in (x0, x1) for n in names_z], 0))
    second = [x2[n][4 + 8 * h : 12 + 8 * h] if n in x2 else None for h in range(2) for n in names_r]
    pack(17, jnp.concatenate([radius_items(second), depth_items([x2.get(n) for n in names_z], 0)], axis=0))


def ring(recv, coef, mr, mz, dt_m, wr, wz, out):
    group = lax.axis_index("az")
    c = {name: coef[n] for n, name in enumerate(RING)}
    q = inverse_radius(group, GROUP)

    def field(f):
        return jnp.concatenate([recv[:, 2 * f], recv[:, 2 * f + 1]], axis=-1)

    def az(fields):
        x = jnp.concatenate([y.reshape(NT, -1) for y in fields], axis=1)
        xh, xl = parts(x)
        y = dot(dt_m[0], xh) + dot(dt_m[0], xl) + dot(dt_m[1], xh)
        res, at = [], 0
        for f in fields:
            n = f.shape[-1]
            res.append(y[:, at : at + n].reshape(f.shape))
            at += n
        return res

    def by_half(x):
        x = x.reshape(NT, 256)
        return [x[:, :128], x[:, 128:]]

    mr_h, mr_l = mr[0], mr[1]
    mz_h, mz_l = mz[0], mz[1]

    def radial(fields, halo):
        stacked = jnp.concatenate([h for f in fields for h in by_half(f)], axis=0)
        y = mm(stacked, mr_h, mr_l)
        res = []
        for i in range(len(fields)):
            halves_ = [
                y[128 * i + 64 * g : 128 * i + 64 * g + 64] + halo[64 * g : 64 * g + 64, 128 * i : 128 * i + 128]
                for g in range(2)
            ]
            res.append(jnp.concatenate(halves_, axis=1).reshape(8, 8, 256))
        return res

    def depth(fields, halo):
        stacked = jnp.concatenate([f.reshape(NT, 256) for f in fields], axis=0)
        y = mm(stacked, mz_h, mz_l)
        return [
            (y[64 * i : 64 * i + 64] + halo[:, 256 * i : 256 * i + 256]).reshape(8, 8, 256)
            for i in range(len(fields))
        ]

    rt, tt, tz, p = [field(f) for f in range(4)]
    pr2, pr3 = field(13), field(14)
    pd2 = [recv[:, 30], recv[:, 31]]
    pd3 = [recv[:, 32], recv[:, 33]]
    px = field(17)
    s_rt, s_tt, s_tz, s_p, d_pr2, d_pr3, d_pd2, d_pd3, d_px = az([rt, tt, tz, p, pr2, pr3, pd2[1], pd3[1], px])
    (dd_px,) = az([d_px])
    wr0, wr1 = (wr[0, 0], wr[0, 1]), (wr[1, 0], wr[1, 1])

    def stack_halves(x):
        return jnp.concatenate(by_half(x), axis=0)

    def radius_halo(zero, one):
        return mm(stack_halves(zero), *wr0) + mm(stack_halves(one), *wr1)

    hr2 = radius_halo(pr2, d_pr2)
    hz2 = mm((pd2[0] + d_pd2).reshape(NT, 128), wz[0], wz[1])
    half = dd_px.reshape(NT, 256)[:, :128]
    hr3 = radius_halo(pr3, d_pr3) + jnp.concatenate([mm(half, *wr0), mm(half, *wr1)], axis=0)
    hz3 = mm((pd3[0] + d_pd3).reshape(NT, 128) + dd_px.reshape(NT, 256)[:, 128:], wz[0], wz[1])

    cv, cf, cr = c["cv"], c["cf"], c["cr"]
    q_rt, q_tt, q_tz, q_p = q * s_rt, q * s_tt, q * s_tz, q * s_p
    dw = [-(cf * q_rt), -(cf * q_tt + cr * q_p), -(cf * q_tz)]
    v1 = [
        field(4) + cv * q_rt,
        field(5) + cv * q_tt + cf * q_p,
        field(6) + cv * q_tz,
    ]
    w1_t = field(7) + dw[1]
    r_r, r_t, r_z, r_w = radial([v1[0], v1[1], v1[2], dw[0]], hr2)
    z_r, z_t, z_z, z_w = depth([v1[0], v1[1], v1[2], dw[2]], hz2)
    a_r, a_t, a_z, a_w = az([v1[0], v1[1], v1[2], w1_t])
    e_tt = q * (v1[0] + a_t)
    div_v = r_r + e_tt + z_z
    div_w = field(8) + r_w + q * (dw[0] + a_w) + z_w
    total = c["bulk"] * div_v + c["couple"] * div_w
    shear = c["shear"]
    lanes = lax.broadcasted_iota(jnp.int32, (8, 256), 1) // GROUP
    source = jnp.where(lanes.astype(F32) == coef[len(RING)], jnp.where(group == 0, SOURCE, 0.0), 0.0)
    n_rr = total + 2.0 * shear * r_r
    n_tt = total + 2.0 * shear * e_tt
    n_zz = total + 2.0 * shear * z_z
    n_rt = shear * (q * (a_r - v1[1]) + r_t)
    n_rz = shear * (z_r + r_z)
    n_tz = shear * (z_t + q * a_z)
    n_p = source - (c["couple"] * div_v + c["modulus"] * div_w)

    r_rr, r_rt, r_rz, r_p = radial([n_rr, n_rt, n_rz, n_p], hr3)
    z_rz, z_tz, z_zz, z_p = depth([n_rz, n_tz, n_zz, n_p], hz3)
    a_rt, a_tt, a_tz, a_p = az([n_rt, n_tt, n_tz, n_p])
    d_r = q_rt + r_rr + z_rz + q * (a_rt + n_rr - n_tt)
    d_t = q_tt + r_rt + z_tz + q * (a_tt + 2.0 * n_rt)
    d_z = q_tz + r_rz + z_zz + q * (a_tz + n_rz)
    fk = c["fk"]
    g_r = r_p + fk * dw[0]
    g_t = q_p + q * a_p + fk * dw[1]
    g_z = z_p + fk * dw[2]
    sums = [
        2.0 * v1[0] + field(9) + cv * d_r + cf * g_r,
        2.0 * v1[1] + field(10) + cv * d_t + cf * g_t,
        2.0 * v1[2] + field(11) + cv * d_z + cf * g_z,
        2.0 * w1_t - field(12) - cf * d_t - cr * g_t,
    ]
    results = [s_rt, s_tt, s_tz, s_p, d_r, d_t, d_z, g_r, g_t, g_z] + az(sums)
    for f, x in enumerate(results):
        out[:, 2 * f] = x[:, :, :128]
        out[:, 2 * f + 1] = x[:, :, 128:]


def unpack(recv, f):
    planes = []
    for g in range(2):
        planes += exchange_groups([recv[k, 2 * f + g] for k in range(8)])
    return jnp.stack(planes)


def advance(recv, keep, coef, new, mid, up, dn):
    c = {name: coef[n] for n, name in enumerate(OWN)}
    q = inverse_radius(0, NR)
    cv, cf, cr = [spread_rows(c[n], 2, 4) for n in ("cv", "cf", "cr")]
    q_rt, q_tt, q_tz, q_p = [q * unpack(recv, f) for f in range(4)]
    dv = [cv * q_rt, cv * q_tt + cf * q_p, cv * q_tz]
    dw = [-(cf * q_rt), -(cf * q_tt + cr * q_p), -(cf * q_tz)]
    for i in range(3):
        d, g = unpack(recv, 4 + i), unpack(recv, 7 + i)
        v1 = keep[i] + dv[i]
        w1 = keep[3 + i] + dw[i]
        v2 = v1 + keep[6 + i] + cv * d + cf * g
        w2 = w1 - keep[9 + i] - cf * d - cr * g
        new[i] = v2
        new[3 + i] = w2
        mid[i] = v1
        mid[3 + i] = w1
        x = v1 + v2
        up[i] = below_partial(x[12:])
        dn[i] = x[0]
        if i == 2:
            x = w1 + w2
            up[3] = below_partial(x[12:])
            dn[3] = x[0]


def settle(recv, v2, mid, v, s, psi, coef, dr_m, v_out, s_out, m_out, edge):
    v_out[...] = v2[...]
    has_below = coef[FLAGS]
    c = {name: coef[n] for n, name in enumerate(OWN)}
    q = inverse_radius(0, NR)

    def sp(value):
        return spread_rows(value, 2, 4)

    omega = sp(c["omega"])
    decay = [sp(c[f"decay{l}"]) for l in range(4)]
    for i in range(3):
        w1, w2 = mid[3 + i], v2[3 + i]
        first = w1 - v[3 + i] + omega * w1
        second = w2 - w1 + omega * w2
        for l in range(4):
            m_out[3 * l + i] = decay[l] * (decay[l] * (psi[3 * l + i] + first) + second)
    sums = [mid[i] + v2[i] for i in range(6)]
    zero = jnp.zeros((1, 8, NR), F32)
    z_r, z_t, z_z, z_w = [
        depth_derivative(jnp.concatenate([x, zero], axis=0), 0, 4, 0, has_below, float(ROW[4, 4]) * x[0], zero[0])[:16]
        for x in (sums[0], sums[1], sums[2], sums[5])
    ]
    stacked = jnp.concatenate([flat(x) for x in sums[:4]], axis=0)
    y = mm(stacked, dr_m[0], dr_m[1])
    r_r, r_t, r_z, r_w = [y[128 * i : 128 * i + 128].reshape(16, 8, NR) for i in range(4)]
    a_r, a_t, a_z, a_w = [unpack(recv, 10 + i) for i in range(4)]
    e_tt = q * (sums[0] + a_t)
    div_v = r_r + e_tt + z_z
    div_w = r_w + q * (sums[3] + a_w) + z_w
    couple, shear = sp(c["couple"]), sp(c["shear"])
    total = sp(c["bulk"]) * div_v + couple * div_w
    plane = lax.broadcasted_iota(jnp.int32, (16, 8, NR), 0)
    lane = lax.broadcasted_iota(jnp.int32, (16, 8, NR), 2)
    source = jnp.where((plane.astype(F32) == coef[FLAGS + 2]) & (lane < 4 * RB), SOURCE * (1.0 + math.cos(0.9)), 0.0)
    updates = [
        total + 2.0 * shear * r_r,
        total + 2.0 * shear * e_tt,
        total + 2.0 * shear * z_z,
        shear * (q * (a_r - sums[1]) + r_t),
        shear * (z_r + r_z),
        shear * (z_t + q * a_z),
        source - (couple * div_v + sp(c["modulus"]) * div_w),
    ]
    for f, x in enumerate(updates):
        x = s[f] + x
        s_out[f] = x
        edge[f, 0] = x[0]
        edge[f, 1:] = x[12:]


def close(s_in, edge, up, dn, coef, s_out, new, sems):
    has_below = coef[FLAGS]
    c = {name: coef[n] for n, name in enumerate(OWN)}

    def update(slot, row, z_r, z_t, z_z, z_w):
        def at(name):
            return jnp.broadcast_to(c[name][row : row + 1, :], (8, NR))

        bulk, couple, modulus, shear = at("bulk"), at("couple"), at("modulus"), at("shear")
        total = bulk * z_z + couple * z_w
        new[0, slot] = edge[0, slot] + total
        new[1, slot] = edge[1, slot] + total
        new[2, slot] = edge[2, slot] + total + 2.0 * shear * z_z
        new[3, slot] = edge[3, slot]
        new[4, slot] = edge[4, slot] + shear * z_r
        new[5, slot] = edge[5, slot] + shear * z_t
        new[6, slot] = edge[6, slot] - (couple * z_z + modulus * z_w)

    update(0, 2, *[has_below * up[i] for i in range(4)])
    for slot in range(1, 5):
        weight = float(ROW[slot - 1, 4])
        update(slot, 5, *[weight * dn[i] for i in range(4)])
    copies = [
        pltpu.make_async_copy(new.at[:, 0:1], s_out.at[:, 0:1], sems.at[0]),
        pltpu.make_async_copy(new.at[:, 1:5], s_out.at[:, 12:16], sems.at[1]),
    ]
    for copy in copies:
        copy.start()
    for copy in copies:
        copy.wait()


def call(body, inputs, shapes, types=None, hbm=(), scratch=(), out_hbm=False, alias=None, micros=1, vmem=VMEM_LIMIT):
    def space(i):
        return pltpu.HBM if i in hbm else pltpu.VMEM

    return pl.pallas_call(
        body,
        out_shape=[jax.ShapeDtypeStruct(x, t) for x, t in zip(shapes, types or [F32] * len(shapes))],
        in_specs=[pl.BlockSpec(memory_space=space(i)) for i in range(len(inputs))],
        out_specs=[pl.BlockSpec(memory_space=pltpu.HBM if out_hbm else pltpu.VMEM) for _ in shapes],
        scratch_shapes=list(scratch),
        input_output_aliases=alias or {},
        compiler_params=pltpu.CompilerParams(vmem_limit_bytes=vmem),
        cost_estimate=pl.CostEstimate(flops=0, bytes_accessed=3 * 10**6 * micros, transcendentals=0),
        name=body.__name__,
    )(*inputs)


def shift(value, steps):
    count = lax.axis_size("depth")
    first, last = max(0, -steps), min(count, count - steps)
    return lax.ppermute(value, "depth", [(i, i + steps) for i in range(first, last)])


def on_device(velocity, stress, memory, layer_ids, materials, jkd, source_depth):
    c = constants()
    block = (PLANES, AZ, NR)
    tables = [layer_ids, materials, jkd, source_depth]
    state, up, dn, ring_coef = call(
        prepare,
        tables + [memory, velocity, stress],
        [(COEF + FLAGS + 3, AZ, NR), (115, AZ, NR), (76, AZ, NR), (len(RING) + 1, 8, 256)],
        hbm=range(7),
        scratch=[pltpu.SMEM(x.shape, x.dtype) for x in tables]
        + [pltpu.VMEM((n,) + block, F32) for n in (12, 6, 7)]
        + [pltpu.SemaphoreType.DMA((7,))],
        vmem=VMEM_FULL,
    )
    up, dn = shift(up, 1), shift(dn, -1)
    staged = [c[n] for n in ("mr", "mz", "dt", "wr", "wz")]
    shapes = [x.shape[1:] if n < 2 else x.shape for n, x in enumerate(staged)]
    *matrices, vw, t_part, coef = call(
        stage,
        staged + [state],
        shapes + [(96, AZ, NR), (48, AZ, NR), (FLAGS + 3, AZ, NR)],
        types=[BF16] * 5 + [F32] * 3,
        hbm=range(6),
        scratch=[pltpu.SemaphoreType.DMA((8,))],
    )
    packed, keep = call(
        launch,
        [stress, vw, t_part, up, dn, coef, c["dr"], c["items"]],
        [(8, 2 * FIELDS_IN, AZ, NR), (12,) + block],
        micros=4,
    )
    packed = lax.all_to_all(packed, "az", split_axis=0, concat_axis=0, tiled=True)
    (back,) = call(ring, [packed, ring_coef] + matrices, [(8, 2 * FIELDS_OUT, AZ, NR)], micros=3)
    back = lax.all_to_all(back, "az", split_axis=0, concat_axis=0, tiled=True)
    new, mid, up, dn = call(
        advance,
        [back, keep, coef],
        [(6,) + block, (6,) + block, (4, AZ, NR), (4, AZ, NR)],
    )
    up, dn = shift(up, 1), shift(dn, -1)
    v_out, s_part, m_out, edge = call(
        settle,
        [back, new, mid, velocity, stress, memory, coef, c["dr"]],
        [(6,) + block, (7,) + block, (12,) + block, (7, 5, AZ, NR)],
        micros=3,
    )
    (s_out,) = call(
        close,
        [s_part, edge, up, dn, coef],
        [(7,) + block],
        hbm=(0,),
        scratch=[pltpu.VMEM((7, 5, AZ, NR), F32), pltpu.SemaphoreType.DMA((2,))],
        out_hbm=True,
        alias={0: 0},
    )
    return v_out, s_out, m_out


def solution(mesh):
    field = P(None, "depth", "az", None)
    return jax.shard_map(
        on_device,
        mesh=mesh,
        in_specs=(field, field, field, P("depth", None), P(), P(), P()),
        out_specs=(field, field, field),
        check_vma=False,
    )
```

```python
import functools
import math

import jax
import jax.numpy as jnp
import ml_dtypes
import numpy as np
from jax import lax
from jax.experimental import pallas as pl
from jax.experimental.pallas import tpu as pltpu
from jax.sharding import PartitionSpec as P

NR = 128
NT = 64
RB = 4
PLANES = 16
AZ = 8
GROUP = 16
DT = 0.02
SOURCE = DT * 40.0
R_INNER = 1.0
F32 = jnp.float32
BF16 = jnp.bfloat16
FIELDS_IN = 18
FIELDS_OUT = 14
VMEM_LIMIT = 32 * 2**20
VMEM_FULL = 56 * 2**20
UP_COEF = 52
DN_COEF = 20
SHARED = ("cv", "cf", "cr", "bulk", "couple", "modulus", "shear")
OWN = SHARED + ("fric", "kappa", "omega", "decay0", "decay1", "decay2", "decay3")
FLAGS = len(OWN)
COEF = 12 * PLANES
RING = SHARED + ("fk",)


def gll_basis():
    root_value = math.sqrt(3.0 / 7.0)
    nodes = np.array([-1.0, -root_value, 0.0, root_value, 1.0])
    weights = np.array([0.1, 49.0 / 90.0, 32.0 / 45.0, 49.0 / 90.0, 0.1])
    offsets = nodes[:, None] - nodes[None, :] + np.eye(5)
    factors = np.prod(offsets, axis=1)
    derivative = factors[:, None] / factors[None, :] / offsets
    diagonal = np.sum(1.0 / offsets, axis=1) - 1.0
    derivative = derivative * (1.0 - np.eye(5)) + np.eye(5) * diagonal[:, None]
    return nodes, weights, derivative


NODES, WEIGHTS, DERIV = gll_basis()
ROW = DERIV * np.array([1.0, 2.0, 2.0, 2.0, 1.0])[:, None]


def line_operator(count, first):
    matrix = np.zeros((count + 1, count + 1))
    for e in range(count // 4):
        matrix[4 * e : 4 * e + 5, 4 * e : 4 * e + 5] += ROW
    if first:
        matrix[0] *= 2.0
    else:
        matrix[0, 0] += ROW[4, 4]
    return matrix[:count, :count]


def halves(matrix):
    hi = matrix.astype(np.float32).astype(ml_dtypes.bfloat16)
    lo = (matrix - hi.astype(np.float64)).astype(np.float32).astype(ml_dtypes.bfloat16)
    return np.stack([hi, lo])


def azimuth_operator():
    positions = np.arange(NT)
    offsets = positions[:, None] - positions[None, :]
    modes = np.arange(1, NT // 2)
    phases = 2.0 * np.pi * offsets[:, :, None] * modes / NT
    return -(2.0 / NT) * np.sum(modes * np.sin(phases), axis=2)


@functools.lru_cache(None)
def constants():
    groups = NR // GROUP
    c = {}
    c["dr"] = halves(line_operator(NR, True).T)
    items = np.zeros((8, NR, groups, 16))
    for s in range(8):
        for k in range(groups):
            if GROUP * (k + 1) < NR:
                items[s, GROUP * (k + 1), k, 2 * s] = 1.0
            if k:
                items[s, GROUP * k - 4 : GROUP * k, k, 2 * s + 1] = ROW[4, :4]
    c["items"] = halves(items.reshape(8 * NR, 128))
    c["dt"] = halves(azimuth_operator())
    c["mr"] = np.stack([halves(np.kron(np.eye(8), line_operator(16, first).T)) for first in (False, True)])
    c["mz"] = np.stack([halves(np.kron(line_operator(16, first).T, np.eye(16))) for first in (False, True)])
    spread = np.zeros((2, 16))
    spread[0, 12:] = ROW[:4, 4]
    spread[1, 0] = 1.0
    wr = np.zeros((2, 8, 16, 4, 8, 16))
    wz = np.zeros((8, 16, 4, 16, 16))
    for f in range(4):
        for side in range(2):
            for j in range(8):
                for order in range(2):
                    wr[order, j, 8 * order + 2 * f + side, f, j] = spread[side]
            for r in range(16):
                wz[2 * f + side, r, f, :, r] = spread[side]
    c["wr"] = np.stack([halves(w) for w in wr.reshape(2, 128, 512)])
    c["wz"] = halves(wz.reshape(128, 1024))
    return c


def roll(x, shift):
    return pltpu.roll(x, shift % x.shape[-1], x.ndim - 1)


def dot(a, b):
    return jnp.dot(a, b, preferred_element_type=F32)


def parts(x):
    hi = x.astype(BF16)
    return hi, (x - hi.astype(F32)).astype(BF16)


def mm(x, hi, lo):
    xh, xl = parts(x)
    return dot(xh, hi) + dot(xl, hi) + dot(xh, lo)


def inverse_radius(group, width):
    lane = lax.broadcasted_iota(jnp.int32, (8, 128 if width == NR else 256), 1) % width
    place = lane % 4
    offset = jnp.zeros(lane.shape, F32)
    for j in range(4):
        offset = jnp.where(place == j, float(R_INNER + 0.5 * (1.0 + NODES[j])), offset)
    return 1.0 / (offset + (lane // 4 + 4 * group).astype(F32))


def own_ids(lids):
    row = lax.broadcasted_iota(jnp.int32, (8, NR), 0)
    fluid = lax.broadcasted_iota(jnp.int32, (8, NR), 1) < 4 * RB
    value = jnp.zeros((8, NR), jnp.int32)
    for e in range(4):
        value = jnp.where(row == 2 + e, jnp.where(fluid, lids[e, 0], lids[e, NR // 4 - 1]), value)
    return value.astype(F32)


def coefficients(ids, tab):
    hits = [ids == float(m) for m in range(8)]
    materials, jkd = tab

    def pick(table, column):
        value = jnp.where(hits[0], table[0, column], 0.0)
        for m in range(1, 8):
            value = jnp.where(hits[m], table[m, column], value)
        return value

    lame, mu, modulus, beta, rho, rho_f, tort, fric = [pick(materials, c) for c in range(8)]
    omega = pick(jkd, 0)
    weights = [pick(jkd, 1 + l) for l in range(4)]
    rates = [pick(jkd, 5 + l) for l in range(4)]
    rho_w = tort * rho_f
    scale = DT / (rho * rho_w - rho_f * rho_f)
    decay = [1.0 / (1.0 + DT * (rate + omega)) for rate in rates]
    gain = sum(a * c for a, c in zip(weights, decay))
    return dict(
        cv=rho_w * scale,
        cf=rho_f * scale,
        cr=rho * scale,
        fric=fric,
        omega=DT * omega,
        weights=weights,
        decay=decay,
        decay0=decay[0],
        decay1=decay[1],
        decay2=decay[2],
        decay3=decay[3],
        kappa=(1.0 + DT * omega) * gain,
        fk=fric * ((1.0 + DT * omega) * gain),
        bulk=DT * (lame + beta * beta * modulus),
        couple=DT * beta * modulus,
        modulus=DT * modulus,
        shear=DT * mu,
    )


def spread_rows(value, first, count, tail=False):
    rows = [jnp.broadcast_to(value[first + e : first + e + 1, :], (8, NR)) for e in range(count + tail)]
    planes = [rows[i // 4] for i in range(4 * count + tail)]
    return jnp.stack(planes)


def combine(row, nodes):
    total = None
    for weight, node in zip(row, nodes):
        term = float(weight) * node
        total = term if total is None else total + term
    return total


def depth_derivative(x, lo, hi, edge, has_below, low=None, high=None):
    count = (x.shape[0] - 1) // 4
    blocks = x[: 4 * count].reshape((count, 4) + x.shape[1:])
    last = [blocks[e + 1, 0] if e + 1 < count else x[4 * count] for e in range(count)]

    def nodes(e):
        return [blocks[e, l] for l in range(4)] + [last[e]]

    out = []
    for e in range(lo, hi + 1):
        upper = combine(ROW[0], nodes(e)) if e < count else high
        lower = combine(ROW[4], nodes(e - 1)) if e > 0 else low
        if e == edge:
            upper = (2.0 - has_below) * upper
            lower = has_below * lower
        out.append(upper + lower)
        if e < hi:
            for i in range(1, 4):
                out.append(combine(ROW[i], nodes(e)))
    return jnp.stack(out)


def below_partial(x):
    return combine(ROW[4, :4], [x[l] for l in range(4)])


def lane_groups():
    return lax.broadcasted_iota(jnp.int32, (8, NR), 1) // GROUP


def exchange_groups(x):
    groups = lane_groups()
    rows = [x[j] for j in range(8)]
    for s in (4, 2, 1):
        low = (groups & s) == 0
        for j in range(8):
            if not j & s:
                a, b = rows[j], rows[j + s]
                rows[j] = jnp.where(low, a, roll(b, GROUP * s))
                rows[j + s] = jnp.where(low, roll(a, -GROUP * s), b)
    return rows


def flat(x):
    return x.reshape(-1, NR)


def prepare(
    lids_hbm, mat_hbm, jkd_hbm, src_hbm, s_hbm, psi_hbm, v_hbm, dr_hbm,
    state, up, dn, ring_coef,
    lids, mat, jkd, src, s, psi, v, dr_m, sems,
):
    pairs = (
        (lids_hbm, lids), (mat_hbm, mat), (jkd_hbm, jkd), (src_hbm, src), (s_hbm, s), (psi_hbm, psi),
        (v_hbm, v), (dr_hbm, dr_m),
    )
    copies = [pltpu.make_async_copy(a, b, sems.at[i]) for i, (a, b) in enumerate(pairs)]
    for copy in copies:
        copy.start()
    for copy in copies[:4]:
        copy.wait()
    device = lax.axis_index("depth")
    rows = lax.broadcasted_iota(jnp.int32, (8, NR), 0)
    c = coefficients(own_ids(lids), (mat, jkd))
    mine = (rows >= 2) & (rows < 6)
    for n, name in enumerate(OWN):
        state[COEF + n] = jnp.where(mine, c[name], 0.0)
    source = (src[0] - PLANES * device).astype(F32)
    state[COEF + FLAGS] = jnp.full((8, NR), jnp.where(device > 0, 1.0, 0.0), F32)
    state[COEF + FLAGS + 1] = jnp.full((8, NR), jnp.where(device < lax.axis_size("depth") - 1, 1.0, 0.0), F32)
    state[COEF + FLAGS + 2] = jnp.full((8, NR), source, F32)
    for n, name in enumerate(SHARED):
        swapped = pltpu.roll(c[name], 4, 0)
        up[UP_COEF + n] = jnp.where(rows < 2, swapped, 0.0)
        dn[DN_COEF + n] = jnp.where(rows >= 6, swapped, 0.0)
    element = lax.broadcasted_iota(jnp.int32, (8, 256), 1) // 64
    group = lax.axis_index("az")
    ids = jnp.zeros((8, 256), jnp.int32)
    for e in range(4):
        ids = jnp.where(element == e, lids[e, 4 * group], ids)
    rc = coefficients(ids.astype(F32), (mat, jkd))
    for n, name in enumerate(RING):
        ring_coef[n] = rc[name]
    ring_coef[len(RING)] = jnp.full((8, 256), source, F32)

    def sp(value):
        return spread_rows(value, 2, 4)

    has_below = jnp.where(device > 0, 1.0, 0.0)
    q = inverse_radius(0, NR)
    cv, cf, cr, fric = [sp(c[n]) for n in ("cv", "cf", "cr", "fric")]
    weights = [sp(w) for w in c["weights"]]
    decayed = [sp(w * d) for w, d in zip(c["weights"], c["decay"])]
    for copy in copies[4:]:
        copy.wait()
    rr, tt, zz, rt, rz, tz, p = [s[f] for f in range(7)]
    stacked = jnp.concatenate([flat(x) for x in (rr, rt, rz, p)], axis=0)
    y = mm(stacked, dr_m[0], dr_m[1])
    r_rr, r_rt, r_rz, r_p = [y[128 * i : 128 * i + 128].reshape(16, 8, NR) for i in range(4)]
    zero = jnp.zeros((1, 8, NR), F32)
    z_rz, z_tz, z_zz, z_p = [
        depth_derivative(jnp.concatenate([x, zero], axis=0), 0, 4, 0, has_below, float(ROW[4, 4]) * x[0], zero[0])[:16]
        for x in (rz, tz, zz, p)
    ]
    div = [r_rr + z_rz + q * (rr - tt), r_rt + z_tz + 2.0 * q * rt, r_rz + z_zz + q * rz]
    grads = (r_p, None, z_p)
    new = []
    for i in range(3):
        memory = [psi[3 * l + i] for l in range(4)]
        total = sum(w * m for w, m in zip(weights, memory))
        later = sum(w * (m - v[3 + i]) for w, m in zip(decayed, memory))
        g0, g1 = fric * total, fric * later
        if grads[i] is not None:
            g0, g1 = g0 + grads[i], g1 + grads[i]
        d_v, d_w = cv * div[i], cf * div[i]
        for n, x in enumerate(
            (v[i] + d_v + cf * g0, v[3 + i] - d_w - cr * g0, d_v + cf * g1, d_w + cr * g1)
        ):
            at = 16 * (3 * n + i)
            state[at : at + 16] = x
            if n < 2:
                f = 3 * n + i
                up[4 * f : 4 * f + 4] = x[12:]
                dn[f] = x[0]
                if f < 3 or f == 5:
                    place = min(f, 3)
                    up[40 + place] = below_partial(x[8:12])
                    dn[12 + place] = combine(ROW[0, 1:], [x[1 + l] for l in range(4)])
    q_rt, q_tt, q_tz, q_p = q * rt, q * tt, q * tz, q * p
    u = [cv * q_rt, cv * q_tt + cf * q_p, cv * q_tz, -(cf * q_tz)]
    for i, x in enumerate(u):
        up[44 + i] = below_partial(x[8:12])
        dn[16 + i] = combine(ROW[0, 1:], [x[1 + l] for l in range(4)])
    for i, x in enumerate((rt, tt, tz, p)):
        up[24 + 4 * i : 28 + 4 * i] = x[12:]
    for i, x in enumerate((rt, tt, tz, p, rz, zz)):
        dn[6 + i] = x[0]
    for i, x in enumerate((rz, tz, zz, p)):
        up[48 + i] = below_partial(x[12:])


def stage(*refs):
    *pairs, sems = refs
    count = 6
    first_r = jnp.where(lax.axis_index("az") == 0, 1, 0)
    first_z = jnp.where(lax.axis_index("depth") == 0, 1, 0)
    sources = list(pairs[:count])
    sources[0] = sources[0].at[first_r]
    sources[1] = sources[1].at[first_z]
    state = sources.pop()
    sources += [state.at[0:COEF], state.at[COEF:]]
    copies = [pltpu.make_async_copy(a, b, sems.at[i]) for i, (a, b) in enumerate(zip(sources, pairs[count:]))]
    for copy in copies:
        copy.start()
    for copy in copies:
        copy.wait()


def launch(s, state, up, dn, coef, dr_m, items, pk, keep):
    has_below = coef[FLAGS]
    has_above = coef[FLAGS + 1]
    c = {name: coef[n] for n, name in enumerate(OWN)}
    for n, name in enumerate(SHARED):
        c[name] = c[name] + up[UP_COEF + n] + dn[DN_COEF + n]
    q = inverse_radius(0, NR)
    cv, cf, cr, bulk, couple, modulus, shear = [spread_rows(c[n], 1, 5, True) for n in SHARED]

    def radial(fields):
        stacked = jnp.concatenate([flat(x) for x in fields], axis=0)
        out = mm(stacked, dr_m[0], dr_m[1])
        count = fields[0].shape[0]
        return [out[8 * count * i : 8 * count * (i + 1)].reshape(count, 8, NR) for i in range(len(fields))]

    def added(f, partial, above):
        x = s[f]
        planes = [float(ROW[l, 4]) * x[0] for l in range(4)]
        planes.append(has_below * partial)
        planes += [float(ROW[l, 4]) * above for l in range(4)]
        planes.append(has_above * below_partial(x[12:]))
        return jnp.stack(planes)

    def edges(x):
        return jnp.concatenate([x[:5], x[16:]], axis=0)

    e_cv, e_cf, e_cr = edges(cv), edges(cf), edges(cr)
    m_rz, m_tz, m_zz, m_p = [
        added(f, up[48 + i], dn[n]) for i, (f, n) in enumerate(((4, 10), (5, 8), (2, 11), (6, 9)))
    ]
    to_v = [e_cv * m_rz, e_cv * m_tz, e_cv * m_zz + e_cf * m_p]
    to_w = [e_cf * m_rz, e_cf * m_tz, e_cf * m_zz + e_cr * m_p]

    def inner_planes(n, more):
        x = state[16 * n : 16 * n + 16]
        return [x[:1] + more[4:5], x[1:12], x[12:] + more[5:9]]

    def whole(f, more):
        ends = [up[4 * f : 4 * f + 4] + more[:4]], [dn[f : f + 1] + more[9:]]
        return jnp.concatenate(ends[0] + inner_planes(f, more) + ends[1], axis=0)

    v1 = [whole(i, to_v[i]) for i in range(3)]
    w1 = [whole(3 + i, -to_w[i]) for i in range(3)]
    q_rt, q_tt, q_tz, q_p = [
        q * jnp.concatenate([up[24 + 4 * i : 28 + 4 * i], s[f], dn[6 + i : 7 + i]], axis=0)
        for i, f in enumerate((3, 1, 5, 6))
    ]
    u = [cv * q_rt, cv * q_tt + cf * q_p, cv * q_tz]
    uw = [-(cf * q_rt), -(cf * q_tt + cr * q_p), -(cf * q_tz)]

    def pack(f, planes):
        for g in range(2):
            chunks = exchange_groups(planes[8 * g : 8 * g + 8])
            for k in range(8):
                pk[k, 2 * f + g] = chunks[k]

    for f, x in enumerate((3, 1, 5, 6)):
        pack(f, s[x])
    fk = spread_rows(c["fric"] * c["kappa"], 2, 4)
    o_cf, o_cr = cf[4:20], cr[4:20]
    for i in range(3):
        v_i, w_i = v1[i][4:20], w1[i][4:20]
        a = jnp.concatenate(inner_planes(6 + i, to_v[i]), axis=0) + o_cf * (fk * w_i)
        b = jnp.concatenate(inner_planes(9 + i, to_w[i]), axis=0) + o_cr * (fk * w_i)
        pack(4 + i, v_i)
        pack(9 + i, a)
        keep[i] = v_i
        keep[3 + i] = w_i
        keep[6 + i] = a
        keep[9 + i] = b
        if i == 1:
            pack(7, w_i)
            pack(12, b)

    mask21 = jnp.where(lax.broadcasted_iota(jnp.int32, (21, 8, NR), 0) < 20, 1.0, has_above)
    plane21 = lax.broadcasted_iota(jnp.int32, (21, 8, NR), 0) - 4
    lane21 = lax.broadcasted_iota(jnp.int32, (21, 8, NR), 2)
    source = jnp.where((plane21.astype(F32) == coef[FLAGS + 2]) & (lane21 < 4 * RB), SOURCE, 0.0)

    def stresses(v, w, extra):
        at = 12 if extra is None else 16
        low = 40 if extra is None else 44
        vr, vt, wr = v[0], v[1], w[0]
        r_r, r_t, r_z, r_w = radial([vr, vt, v[2], wr])
        z_r, z_t, z_z, z_w = [
            depth_derivative(
                x,
                0,
                5,
                1,
                has_below,
                up[low + n] + float(ROW[4, 4]) * x[0],
                dn[at + n] + float(ROW[0, 0]) * x[20],
            )
            for n, x in enumerate((v[0], v[1], v[2], w[2]))
        ]
        e_tt, g_rt, g_tz, div_w = q * vr, r_t - q * vt, z_t, r_w + q * wr + z_w
        if extra is not None:
            e_tt, g_rt, g_tz, div_w = e_tt + extra[1], g_rt + extra[0], g_tz + extra[2], div_w + extra[3]
        div_v = r_r + e_tt + z_z
        total = bulk * div_v + couple * div_w
        return dict(
            rr=mask21 * (total + 2.0 * shear * r_r),
            zz=mask21 * (total + 2.0 * shear * z_z),
            rt=mask21 * (shear * g_rt),
            rz=mask21 * (shear * (z_r + r_z)),
            tz=mask21 * (shear * g_tz),
            p=mask21 * (-(couple * div_v + modulus * div_w) + (source if extra is None else 0.0)),
            w=div_w,
        )

    x0 = stresses(v1, w1, None)
    pack(8, x0["w"][4:20])
    x1 = stresses(u, uw, [q * v1[0], q * v1[1], q * v1[2], q * w1[1]])
    e2, dw2 = q * u[1], q * uw[1]
    total2 = bulk * e2 + couple * dw2
    x2 = dict(
        rr=mask21 * total2,
        zz=mask21 * total2,
        rt=mask21 * (shear * (q * u[0])),
        tz=mask21 * (shear * (q * u[2])),
        p=mask21 * (-(couple * e2 + modulus * dw2)),
    )

    def radius_items(fields):
        slots = [i for i, x in enumerate(fields) if x is not None]
        stacked = jnp.concatenate([flat(fields[i]) for i in slots], axis=1)
        hi, lo = [jnp.concatenate([items[h, NR * i : NR * i + NR] for i in slots], axis=0) for h in range(2)]
        return mm(stacked, hi, lo).reshape(-1, 8, NR)

    def depth_items(fields):
        out = []
        for x in fields:
            if x is None:
                out += [jnp.zeros((8, NR), F32)] * 2
            else:
                out.append(x[20])
                out.append(has_below * below_partial(x[:4]))
        return jnp.stack(out)

    velocity_r = [v1[0], v1[1], v1[2], None, u[0], u[1], u[2], uw[0]]
    pack(13, radius_items([None if x is None else x[4:20] for x in velocity_r]))
    names_r = ("rr", "rt", "rz", "p")
    pack(14, radius_items([x[n][4:20] for x in (x0, x1) for n in names_r]))
    pack(15, depth_items([v1[0], v1[1], v1[2], None, u[0], u[1], u[2], uw[2]]))
    names_z = ("rz", "tz", "zz", "p")
    pack(16, depth_items([x[n] for x in (x0, x1) for n in names_z]))
    second = [x2[n][4 + 8 * h : 12 + 8 * h] if n in x2 else None for h in range(2) for n in names_r]
    pack(17, jnp.concatenate([radius_items(second), depth_items([x2.get(n) for n in names_z])], axis=0))


def ring(recv, coef, mr, mz, dt_m, wr, wz, out):
    group = lax.axis_index("az")
    c = {name: coef[n] for n, name in enumerate(RING)}
    q = inverse_radius(group, GROUP)

    def field(f):
        return jnp.concatenate([recv[:, 2 * f], recv[:, 2 * f + 1]], axis=-1)

    def az(fields):
        x = jnp.concatenate([y.reshape(NT, -1) for y in fields], axis=1)
        xh, xl = parts(x)
        y = dot(dt_m[0], xh) + dot(dt_m[0], xl) + dot(dt_m[1], xh)
        res, at = [], 0
        for f in fields:
            n = f.shape[-1]
            res.append(y[:, at : at + n].reshape(f.shape))
            at += n
        return res

    def by_half(x):
        x = x.reshape(NT, 256)
        return [x[:, :128], x[:, 128:]]

    mr_h, mr_l = mr[0], mr[1]
    mz_h, mz_l = mz[0], mz[1]

    def radial(fields, halo):
        stacked = jnp.concatenate([h for f in fields for h in by_half(f)], axis=0)
        y = mm(stacked, mr_h, mr_l)
        res = []
        for i in range(len(fields)):
            halves_ = [
                y[128 * i + 64 * g : 128 * i + 64 * g + 64] + halo[64 * g : 64 * g + 64, 128 * i : 128 * i + 128]
                for g in range(2)
            ]
            res.append(jnp.concatenate(halves_, axis=1).reshape(8, 8, 256))
        return res

    def depth(fields, halo):
        stacked = jnp.concatenate([f.reshape(NT, 256) for f in fields], axis=0)
        y = mm(stacked, mz_h, mz_l)
        return [
            (y[64 * i : 64 * i + 64] + halo[:, 256 * i : 256 * i + 256]).reshape(8, 8, 256)
            for i in range(len(fields))
        ]

    rt, tt, tz, p = [field(f) for f in range(4)]
    pr2, pr3 = field(13), field(14)
    pd2 = [recv[:, 30], recv[:, 31]]
    pd3 = [recv[:, 32], recv[:, 33]]
    px = field(17)
    s_rt, s_tt, s_tz, s_p, d_pr2, d_pr3, d_pd2, d_pd3, d_px = az([rt, tt, tz, p, pr2, pr3, pd2[1], pd3[1], px])
    (dd_px,) = az([d_px])
    wr0, wr1 = (wr[0, 0], wr[0, 1]), (wr[1, 0], wr[1, 1])

    def stack_halves(x):
        return jnp.concatenate(by_half(x), axis=0)

    def radius_halo(zero, one):
        return mm(stack_halves(zero), *wr0) + mm(stack_halves(one), *wr1)

    hr2 = radius_halo(pr2, d_pr2)
    hz2 = mm((pd2[0] + d_pd2).reshape(NT, 128), wz[0], wz[1])
    half = dd_px.reshape(NT, 256)[:, :128]
    hr3 = radius_halo(pr3, d_pr3) + jnp.concatenate([mm(half, *wr0), mm(half, *wr1)], axis=0)
    hz3 = mm((pd3[0] + d_pd3).reshape(NT, 128) + dd_px.reshape(NT, 256)[:, 128:], wz[0], wz[1])

    cv, cf, cr = c["cv"], c["cf"], c["cr"]
    q_rt, q_tt, q_tz, q_p = q * s_rt, q * s_tt, q * s_tz, q * s_p
    dw = [-(cf * q_rt), -(cf * q_tt + cr * q_p), -(cf * q_tz)]
    v1 = [
        field(4) + cv * q_rt,
        field(5) + cv * q_tt + cf * q_p,
        field(6) + cv * q_tz,
    ]
    w1_t = field(7) + dw[1]
    r_r, r_t, r_z, r_w = radial([v1[0], v1[1], v1[2], dw[0]], hr2)
    z_r, z_t, z_z, z_w = depth([v1[0], v1[1], v1[2], dw[2]], hz2)
    a_r, a_t, a_z, a_w = az([v1[0], v1[1], v1[2], w1_t])
    e_tt = q * (v1[0] + a_t)
    div_v = r_r + e_tt + z_z
    div_w = field(8) + r_w + q * (dw[0] + a_w) + z_w
    total = c["bulk"] * div_v + c["couple"] * div_w
    shear = c["shear"]
    lanes = lax.broadcasted_iota(jnp.int32, (8, 256), 1) // GROUP
    source = jnp.where(lanes.astype(F32) == coef[len(RING)], jnp.where(group == 0, SOURCE, 0.0), 0.0)
    n_rr = total + 2.0 * shear * r_r
    n_tt = total + 2.0 * shear * e_tt
    n_zz = total + 2.0 * shear * z_z
    n_rt = shear * (q * (a_r - v1[1]) + r_t)
    n_rz = shear * (z_r + r_z)
    n_tz = shear * (z_t + q * a_z)
    n_p = source - (c["couple"] * div_v + c["modulus"] * div_w)

    r_rr, r_rt, r_rz, r_p = radial([n_rr, n_rt, n_rz, n_p], hr3)
    z_rz, z_tz, z_zz, z_p = depth([n_rz, n_tz, n_zz, n_p], hz3)
    a_rt, a_tt, a_tz, a_p = az([n_rt, n_tt, n_tz, n_p])
    d_r = q_rt + r_rr + z_rz + q * (a_rt + n_rr - n_tt)
    d_t = q_tt + r_rt + z_tz + q * (a_tt + 2.0 * n_rt)
    d_z = q_tz + r_rz + z_zz + q * (a_tz + n_rz)
    fk = c["fk"]
    g_r = r_p + fk * dw[0]
    g_t = q_p + q * a_p + fk * dw[1]
    g_z = z_p + fk * dw[2]
    sums = [
        2.0 * v1[0] + field(9) + cv * d_r + cf * g_r,
        2.0 * v1[1] + field(10) + cv * d_t + cf * g_t,
        2.0 * v1[2] + field(11) + cv * d_z + cf * g_z,
        2.0 * w1_t - field(12) - cf * d_t - cr * g_t,
    ]
    results = [s_rt, s_tt, s_tz, s_p, d_r, d_t, d_z, g_r, g_t, g_z] + az(sums)
    for f, x in enumerate(results):
        out[:, 2 * f] = x[:, :, :128]
        out[:, 2 * f + 1] = x[:, :, 128:]


def unpack(recv, f):
    planes = []
    for g in range(2):
        planes += exchange_groups([recv[k, 2 * f + g] for k in range(8)])
    return jnp.stack(planes)


def advance(recv, keep, coef, new, mid, up, dn):
    c = {name: coef[n] for n, name in enumerate(OWN)}
    q = inverse_radius(0, NR)
    cv, cf, cr = [spread_rows(c[n], 2, 4) for n in ("cv", "cf", "cr")]
    q_rt, q_tt, q_tz, q_p = [q * unpack(recv, f) for f in range(4)]
    dv = [cv * q_rt, cv * q_tt + cf * q_p, cv * q_tz]
    dw = [-(cf * q_rt), -(cf * q_tt + cr * q_p), -(cf * q_tz)]
    for i in range(3):
        d, g = unpack(recv, 4 + i), unpack(recv, 7 + i)
        v1 = keep[i] + dv[i]
        w1 = keep[3 + i] + dw[i]
        v2 = v1 + keep[6 + i] + cv * d + cf * g
        w2 = w1 - keep[9 + i] - cf * d - cr * g
        new[i] = v2
        new[3 + i] = w2
        mid[i] = v1
        mid[3 + i] = w1
        x = v1 + v2
        up[i] = below_partial(x[12:])
        dn[i] = x[0]
        if i == 2:
            x = w1 + w2
            up[3] = below_partial(x[12:])
            dn[3] = x[0]


def settle(recv, v2, mid, v, s, psi, coef, dr_m, v_out, s_out, m_out, edge):
    v_out[...] = v2[...]
    has_below = coef[FLAGS]
    c = {name: coef[n] for n, name in enumerate(OWN)}
    q = inverse_radius(0, NR)

    def sp(value):
        return spread_rows(value, 2, 4)

    omega = sp(c["omega"])
    decay = [sp(c[f"decay{l}"]) for l in range(4)]
    for i in range(3):
        w1, w2 = mid[3 + i], v2[3 + i]
        first = w1 - v[3 + i] + omega * w1
        second = w2 - w1 + omega * w2
        for l in range(4):
            m_out[3 * l + i] = decay[l] * (decay[l] * (psi[3 * l + i] + first) + second)
    sums = [mid[i] + v2[i] for i in range(6)]
    zero = jnp.zeros((1, 8, NR), F32)
    z_r, z_t, z_z, z_w = [
        depth_derivative(jnp.concatenate([x, zero], axis=0), 0, 4, 0, has_below, float(ROW[4, 4]) * x[0], zero[0])[:16]
        for x in (sums[0], sums[1], sums[2], sums[5])
    ]
    stacked = jnp.concatenate([flat(x) for x in sums[:4]], axis=0)
    y = mm(stacked, dr_m[0], dr_m[1])
    r_r, r_t, r_z, r_w = [y[128 * i : 128 * i + 128].reshape(16, 8, NR) for i in range(4)]
    a_r, a_t, a_z, a_w = [unpack(recv, 10 + i) for i in range(4)]
    e_tt = q * (sums[0] + a_t)
    div_v = r_r + e_tt + z_z
    div_w = r_w + q * (sums[3] + a_w) + z_w
    couple, shear = sp(c["couple"]), sp(c["shear"])
    total = sp(c["bulk"]) * div_v + couple * div_w
    plane = lax.broadcasted_iota(jnp.int32, (16, 8, NR), 0)
    lane = lax.broadcasted_iota(jnp.int32, (16, 8, NR), 2)
    source = jnp.where((plane.astype(F32) == coef[FLAGS + 2]) & (lane < 4 * RB), SOURCE * (1.0 + math.cos(0.9)), 0.0)
    updates = [
        total + 2.0 * shear * r_r,
        total + 2.0 * shear * e_tt,
        total + 2.0 * shear * z_z,
        shear * (q * (a_r - sums[1]) + r_t),
        shear * (z_r + r_z),
        shear * (z_t + q * a_z),
        source - (couple * div_v + sp(c["modulus"]) * div_w),
    ]
    for f, x in enumerate(updates):
        x = s[f] + x
        s_out[f] = x
        edge[f, 0] = x[0]
        edge[f, 1:] = x[12:]


def close(s_in, edge, up, dn, coef, s_out, new, sems):
    has_below = coef[FLAGS]
    c = {name: coef[n] for n, name in enumerate(OWN)}

    def update(slot, row, z_r, z_t, z_z, z_w):
        def at(name):
            return jnp.broadcast_to(c[name][row : row + 1, :], (8, NR))

        bulk, couple, modulus, shear = at("bulk"), at("couple"), at("modulus"), at("shear")
        total = bulk * z_z + couple * z_w
        new[0, slot] = edge[0, slot] + total
        new[1, slot] = edge[1, slot] + total
        new[2, slot] = edge[2, slot] + total + 2.0 * shear * z_z
        new[3, slot] = edge[3, slot]
        new[4, slot] = edge[4, slot] + shear * z_r
        new[5, slot] = edge[5, slot] + shear * z_t
        new[6, slot] = edge[6, slot] - (couple * z_z + modulus * z_w)

    update(0, 2, *[has_below * up[i] for i in range(4)])
    for slot in range(1, 5):
        weight = float(ROW[slot - 1, 4])
        update(slot, 5, *[weight * dn[i] for i in range(4)])
    copies = [
        pltpu.make_async_copy(new.at[:, 0:1], s_out.at[:, 0:1], sems.at[0]),
        pltpu.make_async_copy(new.at[:, 1:5], s_out.at[:, 12:16], sems.at[1]),
    ]
    for copy in copies:
        copy.start()
    for copy in copies:
        copy.wait()


def call(body, inputs, shapes, types=None, hbm=(), scratch=(), out_hbm=False, alias=None, micros=1, vmem=VMEM_LIMIT):
    def space(i):
        return pltpu.HBM if i in hbm else pltpu.VMEM

    return pl.pallas_call(
        body,
        out_shape=[jax.ShapeDtypeStruct(x, t) for x, t in zip(shapes, types or [F32] * len(shapes))],
        in_specs=[pl.BlockSpec(memory_space=space(i)) for i in range(len(inputs))],
        out_specs=[pl.BlockSpec(memory_space=pltpu.HBM if out_hbm else pltpu.VMEM) for _ in shapes],
        scratch_shapes=list(scratch),
        input_output_aliases=alias or {},
        compiler_params=pltpu.CompilerParams(vmem_limit_bytes=vmem),
        cost_estimate=pl.CostEstimate(flops=0, bytes_accessed=3 * 10**6 * micros, transcendentals=0),
        name=body.__name__,
    )(*inputs)


def shift(value, steps):
    count = lax.axis_size("depth")
    first, last = max(0, -steps), min(count, count - steps)
    return lax.ppermute(value, "depth", [(i, i + steps) for i in range(first, last)])


def on_device(velocity, stress, memory, layer_ids, materials, jkd, source_depth):
    c = constants()
    block = (PLANES, AZ, NR)
    tables = [layer_ids, materials, jkd, source_depth]
    state, up, dn, ring_coef = call(
        prepare,
        tables + [stress, memory, velocity, c["dr"]],
        [(COEF + FLAGS + 3, AZ, NR), (UP_COEF + 7, AZ, NR), (DN_COEF + 7, AZ, NR), (len(RING) + 1, 8, 256)],
        hbm=range(8),
        scratch=[pltpu.SMEM(x.shape, x.dtype) for x in tables]
        + [pltpu.VMEM((n,) + block, F32) for n in (7, 12, 6)]
        + [pltpu.VMEM(c["dr"].shape, BF16), pltpu.SemaphoreType.DMA((8,))],
        vmem=VMEM_FULL,
    )
    up, dn = shift(up, 1), shift(dn, -1)
    staged = [c[n] for n in ("mr", "mz", "dt", "wr", "wz")]
    shapes = [x.shape[1:] if n < 2 else x.shape for n, x in enumerate(staged)]
    *matrices, state, coef = call(
        stage,
        staged + [state],
        shapes + [(COEF, AZ, NR), (FLAGS + 3, AZ, NR)],
        types=[BF16] * 5 + [F32] * 2,
        hbm=range(6),
        scratch=[pltpu.SemaphoreType.DMA((7,))],
    )
    packed, keep = call(
        launch,
        [stress, state, up, dn, coef, c["dr"], c["items"]],
        [(8, 2 * FIELDS_IN, AZ, NR), (12,) + block],
        micros=4,
    )
    packed = lax.all_to_all(packed, "az", split_axis=0, concat_axis=0, tiled=True)
    (back,) = call(ring, [packed, ring_coef] + matrices, [(8, 2 * FIELDS_OUT, AZ, NR)], micros=3)
    back = lax.all_to_all(back, "az", split_axis=0, concat_axis=0, tiled=True)
    new, mid, up, dn = call(
        advance,
        [back, keep, coef],
        [(6,) + block, (6,) + block, (4, AZ, NR), (4, AZ, NR)],
    )
    up, dn = shift(up, 1), shift(dn, -1)
    v_out, s_part, m_out, edge = call(
        settle,
        [back, new, mid, velocity, stress, memory, coef, c["dr"]],
        [(6,) + block, (7,) + block, (12,) + block, (7, 5, AZ, NR)],
        micros=3,
    )
    (s_out,) = call(
        close,
        [s_part, edge, up, dn, coef],
        [(7,) + block],
        hbm=(0,),
        scratch=[pltpu.VMEM((7, 5, AZ, NR), F32), pltpu.SemaphoreType.DMA((2,))],
        out_hbm=True,
        alias={0: 0},
    )
    return v_out, s_out, m_out


def solution(mesh):
    field = P(None, "depth", "az", None)
    return jax.shard_map(
        on_device,
        mesh=mesh,
        in_specs=(field, field, field, P("depth", None), P(), P(), P()),
        out_specs=(field, field, field),
        check_vma=False,
    )
```

```python
import functools
import math

import jax
import jax.numpy as jnp
import ml_dtypes
import numpy as np
from jax import lax
from jax.experimental import pallas as pl
from jax.experimental.pallas import tpu as pltpu
from jax.sharding import PartitionSpec as P

NR = 128
NT = 64
RB = 4
PLANES = 16
AZ = 8
GROUP = 16
DT = 0.02
SOURCE = DT * 40.0
R_INNER = 1.0
F32 = jnp.float32
BF16 = jnp.bfloat16
FIELDS_IN = 18
FIELDS_OUT = 14
VMEM_LIMIT = 32 * 2**20
VMEM_FULL = 56 * 2**20
UP_COEF = 52
DN_COEF = 20
SHARED = ("cv", "cf", "cr", "bulk", "couple", "modulus", "shear")
OWN = SHARED + ("fric", "kappa", "omega", "decay0", "decay1", "decay2", "decay3")
FLAGS = len(OWN)
COEF = 12 * PLANES
RING = SHARED + ("fk",)


def gll_basis():
    root_value = math.sqrt(3.0 / 7.0)
    nodes = np.array([-1.0, -root_value, 0.0, root_value, 1.0])
    weights = np.array([0.1, 49.0 / 90.0, 32.0 / 45.0, 49.0 / 90.0, 0.1])
    offsets = nodes[:, None] - nodes[None, :] + np.eye(5)
    factors = np.prod(offsets, axis=1)
    derivative = factors[:, None] / factors[None, :] / offsets
    diagonal = np.sum(1.0 / offsets, axis=1) - 1.0
    derivative = derivative * (1.0 - np.eye(5)) + np.eye(5) * diagonal[:, None]
    return nodes, weights, derivative


NODES, WEIGHTS, DERIV = gll_basis()
ROW = DERIV * np.array([1.0, 2.0, 2.0, 2.0, 1.0])[:, None]


def line_operator(count, first):
    matrix = np.zeros((count + 1, count + 1))
    for e in range(count // 4):
        matrix[4 * e : 4 * e + 5, 4 * e : 4 * e + 5] += ROW
    if first:
        matrix[0] *= 2.0
    else:
        matrix[0, 0] += ROW[4, 4]
    return matrix[:count, :count]


def halves(matrix):
    hi = matrix.astype(np.float32).astype(ml_dtypes.bfloat16)
    lo = (matrix - hi.astype(np.float64)).astype(np.float32).astype(ml_dtypes.bfloat16)
    return np.stack([hi, lo])


def azimuth_operator():
    positions = np.arange(NT)
    offsets = positions[:, None] - positions[None, :]
    modes = np.arange(1, NT // 2)
    phases = 2.0 * np.pi * offsets[:, :, None] * modes / NT
    return -(2.0 / NT) * np.sum(modes * np.sin(phases), axis=2)


@functools.lru_cache(None)
def constants():
    groups = NR // GROUP
    c = {}
    c["dr"] = halves(line_operator(NR, True).T)
    items = np.zeros((8, NR, groups, 16))
    for s in range(8):
        for k in range(groups):
            if GROUP * (k + 1) < NR:
                items[s, GROUP * (k + 1), k, 2 * s] = 1.0
            if k:
                items[s, GROUP * k - 4 : GROUP * k, k, 2 * s + 1] = ROW[4, :4]
    c["items"] = halves(items.reshape(8 * NR, 128))
    c["dt"] = halves(azimuth_operator())
    c["mr"] = np.stack([halves(np.kron(np.eye(8), line_operator(16, first).T)) for first in (False, True)])
    c["mz"] = np.stack([halves(np.kron(line_operator(16, first).T, np.eye(16))) for first in (False, True)])
    spread = np.zeros((2, 16))
    spread[0, 12:] = ROW[:4, 4]
    spread[1, 0] = 1.0
    wr = np.zeros((2, 8, 16, 4, 8, 16))
    wz = np.zeros((8, 16, 4, 16, 16))
    for f in range(4):
        for side in range(2):
            for j in range(8):
                for order in range(2):
                    wr[order, j, 8 * order + 2 * f + side, f, j] = spread[side]
            for r in range(16):
                wz[2 * f + side, r, f, :, r] = spread[side]
    c["wr"] = np.stack([halves(w) for w in wr.reshape(2, 128, 512)])
    c["wz"] = halves(wz.reshape(128, 1024))
    return c


def roll(x, shift):
    return pltpu.roll(x, shift % x.shape[-1], x.ndim - 1)


def dot(a, b):
    return jnp.dot(a, b, preferred_element_type=F32)


def parts(x):
    hi = x.astype(BF16)
    return hi, (x - hi.astype(F32)).astype(BF16)


def mm(x, hi, lo):
    xh, xl = parts(x)
    return dot(xh, hi) + dot(xl, hi) + dot(xh, lo)


def inverse_radius(group, width):
    lane = lax.broadcasted_iota(jnp.int32, (8, 128 if width == NR else 256), 1) % width
    place = lane % 4
    offset = jnp.zeros(lane.shape, F32)
    for j in range(4):
        offset = jnp.where(place == j, float(R_INNER + 0.5 * (1.0 + NODES[j])), offset)
    return 1.0 / (offset + (lane // 4 + 4 * group).astype(F32))


def own_ids(lids):
    row = lax.broadcasted_iota(jnp.int32, (8, NR), 0)
    fluid = lax.broadcasted_iota(jnp.int32, (8, NR), 1) < 4 * RB
    value = jnp.zeros((8, NR), jnp.int32)
    for e in range(4):
        value = jnp.where(row == 2 + e, jnp.where(fluid, lids[e, 0], lids[e, NR // 4 - 1]), value)
    return value.astype(F32)


def coefficients(ids, tab):
    hits = [ids == float(m) for m in range(8)]
    materials, jkd = tab

    def pick(table, column):
        value = jnp.where(hits[0], table[0, column], 0.0)
        for m in range(1, 8):
            value = jnp.where(hits[m], table[m, column], value)
        return value

    lame, mu, modulus, beta, rho, rho_f, tort, fric = [pick(materials, c) for c in range(8)]
    omega = pick(jkd, 0)
    weights = [pick(jkd, 1 + l) for l in range(4)]
    rates = [pick(jkd, 5 + l) for l in range(4)]
    rho_w = tort * rho_f
    scale = DT / (rho * rho_w - rho_f * rho_f)
    decay = [1.0 / (1.0 + DT * (rate + omega)) for rate in rates]
    gain = sum(a * c for a, c in zip(weights, decay))
    return dict(
        cv=rho_w * scale,
        cf=rho_f * scale,
        cr=rho * scale,
        fric=fric,
        omega=DT * omega,
        weights=weights,
        decay=decay,
        decay0=decay[0],
        decay1=decay[1],
        decay2=decay[2],
        decay3=decay[3],
        kappa=(1.0 + DT * omega) * gain,
        fk=fric * ((1.0 + DT * omega) * gain),
        bulk=DT * (lame + beta * beta * modulus),
        couple=DT * beta * modulus,
        modulus=DT * modulus,
        shear=DT * mu,
    )


def spread_rows(value, first, count, tail=False):
    rows = [jnp.broadcast_to(value[first + e : first + e + 1, :], (8, NR)) for e in range(count + tail)]
    planes = [rows[i // 4] for i in range(4 * count + tail)]
    return jnp.stack(planes)


def combine(row, nodes):
    total = None
    for weight, node in zip(row, nodes):
        term = float(weight) * node
        total = term if total is None else total + term
    return total


def depth_derivative(x, lo, hi, edge, has_below, low=None, high=None):
    count = (x.shape[0] - 1) // 4
    blocks = x[: 4 * count].reshape((count, 4) + x.shape[1:])
    last = [blocks[e + 1, 0] if e + 1 < count else x[4 * count] for e in range(count)]

    def nodes(e):
        return [blocks[e, l] for l in range(4)] + [last[e]]

    out = []
    for e in range(lo, hi + 1):
        upper = combine(ROW[0], nodes(e)) if e < count else high
        lower = combine(ROW[4], nodes(e - 1)) if e > 0 else low
        if e == edge:
            upper = (2.0 - has_below) * upper
            lower = has_below * lower
        out.append(upper + lower)
        if e < hi:
            for i in range(1, 4):
                out.append(combine(ROW[i], nodes(e)))
    return jnp.stack(out)


def below_partial(x):
    return combine(ROW[4, :4], [x[l] for l in range(4)])


def lane_groups():
    return lax.broadcasted_iota(jnp.int32, (8, NR), 1) // GROUP


def exchange_groups(x):
    groups = lane_groups()
    rows = [roll(x[j], GROUP * j) if j else x[j] for j in range(8)]
    for s in (1, 2, 4):
        stay = (groups & s) == 0
        rows = [jnp.where(stay, rows[j], rows[(j + s) % 8]) for j in range(8)]
    return [roll(rows[-k % 8], -GROUP * k) if k else rows[0] for k in range(8)]


def for_each(count, body, unroll=4):
    lax.fori_loop(0, count, lambda i, _: (body(i), 0)[1], 0, unroll=unroll)


def flat(x):
    return x.reshape(-1, NR)


def prepare(
    lids_hbm, mat_hbm, jkd_hbm, s_hbm, psi_hbm, v_hbm, dr_hbm,
    state, up, dn, ring_coef,
    lids, mat, jkd, s, psi, v, dr_m, sems,
):
    pairs = (
        (lids_hbm, lids), (mat_hbm, mat), (jkd_hbm, jkd), (s_hbm, s), (psi_hbm, psi),
        (v_hbm, v), (dr_hbm, dr_m),
    )
    copies = [pltpu.make_async_copy(a, b, sems.at[i]) for i, (a, b) in enumerate(pairs)]
    for copy in copies:
        copy.start()
    for copy in copies[:3]:
        copy.wait()
    device = lax.axis_index("depth")
    rows = lax.broadcasted_iota(jnp.int32, (8, NR), 0)
    c = coefficients(own_ids(lids), (mat, jkd))
    mine = (rows >= 2) & (rows < 6)
    for n, name in enumerate(OWN):
        state[COEF + n] = jnp.where(mine, c[name], 0.0)
    state[COEF + FLAGS] = jnp.full((8, NR), jnp.where(device > 0, 1.0, 0.0), F32)
    state[COEF + FLAGS + 1] = jnp.full((8, NR), jnp.where(device < lax.axis_size("depth") - 1, 1.0, 0.0), F32)
    for n, name in enumerate(SHARED):
        swapped = pltpu.roll(c[name], 4, 0)
        up[UP_COEF + n] = jnp.where(rows < 2, swapped, 0.0)
        dn[DN_COEF + n] = jnp.where(rows >= 6, swapped, 0.0)
    element = lax.broadcasted_iota(jnp.int32, (8, 256), 1) // 64
    group = lax.axis_index("az")
    ids = jnp.zeros((8, 256), jnp.int32)
    for e in range(4):
        ids = jnp.where(element == e, lids[e, 4 * group], ids)
    rc = coefficients(ids.astype(F32), (mat, jkd))
    for n, name in enumerate(RING):
        ring_coef[n] = rc[name]

    def sp(value):
        return spread_rows(value, 2, 4)

    has_below = jnp.where(device > 0, 1.0, 0.0)
    q = inverse_radius(0, NR)
    cv, cf, cr, fric = [sp(c[n]) for n in ("cv", "cf", "cr", "fric")]
    weights = [sp(w) for w in c["weights"]]
    decayed = [sp(w * d) for w, d in zip(c["weights"], c["decay"])]
    for copy in copies[3:]:
        copy.wait()
    rr, tt, zz, rt, rz, tz, p = [s[f] for f in range(7)]
    stacked = jnp.concatenate([flat(x) for x in (rr, rt, rz, p)], axis=0)
    y = mm(stacked, dr_m[0], dr_m[1])
    r_rr, r_rt, r_rz, r_p = [y[128 * i : 128 * i + 128].reshape(16, 8, NR) for i in range(4)]
    zero = jnp.zeros((1, 8, NR), F32)
    z_rz, z_tz, z_zz, z_p = [
        depth_derivative(jnp.concatenate([x, zero], axis=0), 0, 4, 0, has_below, float(ROW[4, 4]) * x[0], zero[0])[:16]
        for x in (rz, tz, zz, p)
    ]
    div = [r_rr + z_rz + q * (rr - tt), r_rt + z_tz + 2.0 * q * rt, r_rz + z_zz + q * rz]
    grads = (r_p, None, z_p)
    new = []
    for i in range(3):
        memory = [psi[3 * l + i] for l in range(4)]
        total = sum(w * m for w, m in zip(weights, memory))
        later = sum(w * (m - v[3 + i]) for w, m in zip(decayed, memory))
        g0, g1 = fric * total, fric * later
        if grads[i] is not None:
            g0, g1 = g0 + grads[i], g1 + grads[i]
        d_v, d_w = cv * div[i], cf * div[i]
        for n, x in enumerate(
            (v[i] + d_v + cf * g0, v[3 + i] - d_w - cr * g0, d_v + cf * g1, d_w + cr * g1)
        ):
            at = 16 * (3 * n + i)
            state[at : at + 16] = x
            if n < 2:
                f = 3 * n + i
                up[4 * f : 4 * f + 4] = x[12:]
                dn[f] = x[0]
                if f < 3 or f == 5:
                    place = min(f, 3)
                    up[40 + place] = below_partial(x[8:12])
                    dn[12 + place] = combine(ROW[0, 1:], [x[1 + l] for l in range(4)])
    q_rt, q_tt, q_tz, q_p = q * rt, q * tt, q * tz, q * p
    u = [cv * q_rt, cv * q_tt + cf * q_p, cv * q_tz, -(cf * q_tz)]
    for i, x in enumerate(u):
        up[44 + i] = below_partial(x[8:12])
        dn[16 + i] = combine(ROW[0, 1:], [x[1 + l] for l in range(4)])
    for i, x in enumerate((rt, tt, tz, p)):
        up[24 + 4 * i : 28 + 4 * i] = x[12:]
    for i, x in enumerate((rt, tt, tz, p, rz, zz)):
        dn[6 + i] = x[0]
    for i, x in enumerate((rz, tz, zz, p)):
        up[48 + i] = below_partial(x[12:])


def stage(*refs):
    src, *pairs, mark, sems = refs
    count = 6
    first_r = jnp.where(lax.axis_index("az") == 0, 1, 0)
    first_z = jnp.where(lax.axis_index("depth") == 0, 1, 0)
    sources = list(pairs[:count])
    sources[0] = sources[0].at[first_r]
    sources[1] = sources[1].at[first_z]
    state = sources.pop()
    sources += [state.at[0:COEF], state.at[COEF:]]
    copies = [pltpu.make_async_copy(a, b, sems.at[i]) for i, (a, b) in enumerate(zip(sources, pairs[count:]))]
    for copy in copies:
        copy.start()
    mark[...] = jnp.full((8, 256), (src[0] - PLANES * lax.axis_index("depth")).astype(F32), F32)
    for copy in copies:
        copy.wait()


def launch(s, state, up, dn, coef, mark, dr_m, items, pk, keep, hold):
    has_below = coef[FLAGS]
    has_above = coef[FLAGS + 1]
    c = {name: coef[n] for n, name in enumerate(OWN)}
    for n, name in enumerate(SHARED):
        c[name] = c[name] + up[UP_COEF + n] + dn[DN_COEF + n]
    q = inverse_radius(0, NR)
    cv, cf, cr, bulk, couple, modulus, shear = [spread_rows(c[n], 1, 5, True) for n in SHARED]

    def radial(fields):
        stacked = jnp.concatenate([flat(x) for x in fields], axis=0)
        out = mm(stacked, dr_m[0], dr_m[1])
        count = fields[0].shape[0]
        return [out[8 * count * i : 8 * count * (i + 1)].reshape(count, 8, NR) for i in range(len(fields))]

    def added(f, partial, above):
        x = s[f]
        planes = [float(ROW[l, 4]) * x[0] for l in range(4)]
        planes.append(has_below * partial)
        planes += [float(ROW[l, 4]) * above for l in range(4)]
        planes.append(has_above * below_partial(x[12:]))
        return jnp.stack(planes)

    def edges(x):
        return jnp.concatenate([x[:5], x[16:]], axis=0)

    e_cv, e_cf, e_cr = edges(cv), edges(cf), edges(cr)
    m_rz, m_tz, m_zz, m_p = [
        added(f, up[48 + i], dn[n]) for i, (f, n) in enumerate(((4, 10), (5, 8), (2, 11), (6, 9)))
    ]
    to_v = [e_cv * m_rz, e_cv * m_tz, e_cv * m_zz + e_cf * m_p]
    to_w = [e_cf * m_rz, e_cf * m_tz, e_cf * m_zz + e_cr * m_p]

    def inner_planes(n, more):
        x = state[16 * n : 16 * n + 16]
        return [x[:1] + more[4:5], x[1:12], x[12:] + more[5:9]]

    def whole(f, more):
        ends = [up[4 * f : 4 * f + 4] + more[:4]], [dn[f : f + 1] + more[9:]]
        return jnp.concatenate(ends[0] + inner_planes(f, more) + ends[1], axis=0)

    v1 = [whole(i, to_v[i]) for i in range(3)]
    w1 = [whole(3 + i, -to_w[i]) for i in range(3)]
    q_rt, q_tt, q_tz, q_p = [
        q * jnp.concatenate([up[24 + 4 * i : 28 + 4 * i], s[f], dn[6 + i : 7 + i]], axis=0)
        for i, f in enumerate((3, 1, 5, 6))
    ]
    u = [cv * q_rt, cv * q_tt + cf * q_p, cv * q_tz]
    uw = [-(cf * q_rt), -(cf * q_tt + cr * q_p), -(cf * q_tz)]

    def pack(f, planes):
        hold[2 * f] = planes[:8]
        hold[2 * f + 1] = planes[8:]

    for f, x in enumerate((3, 1, 5, 6)):
        pack(f, s[x])
    fk = spread_rows(c["fric"] * c["kappa"], 2, 4)
    o_cf, o_cr = cf[4:20], cr[4:20]
    for i in range(3):
        v_i, w_i = v1[i][4:20], w1[i][4:20]
        a = jnp.concatenate(inner_planes(6 + i, to_v[i]), axis=0) + o_cf * (fk * w_i)
        b = jnp.concatenate(inner_planes(9 + i, to_w[i]), axis=0) + o_cr * (fk * w_i)
        pack(4 + i, v_i)
        pack(9 + i, a)
        keep[i] = v_i
        keep[3 + i] = w_i
        keep[6 + i] = a
        keep[9 + i] = b
        if i == 1:
            pack(7, w_i)
            pack(12, b)

    mask21 = jnp.where(lax.broadcasted_iota(jnp.int32, (21, 8, NR), 0) < 20, 1.0, has_above)
    plane21 = lax.broadcasted_iota(jnp.int32, (21, 8, NR), 0) - 4
    lane21 = lax.broadcasted_iota(jnp.int32, (21, 8, NR), 2)
    source = jnp.where((plane21.astype(F32) == mark[:, :NR]) & (lane21 < 4 * RB), SOURCE, 0.0)

    def stresses(v, w, extra):
        at = 12 if extra is None else 16
        low = 40 if extra is None else 44
        vr, vt, wr = v[0], v[1], w[0]
        r_r, r_t, r_z, r_w = radial([vr, vt, v[2], wr])
        z_r, z_t, z_z, z_w = [
            depth_derivative(
                x,
                0,
                5,
                1,
                has_below,
                up[low + n] + float(ROW[4, 4]) * x[0],
                dn[at + n] + float(ROW[0, 0]) * x[20],
            )
            for n, x in enumerate((v[0], v[1], v[2], w[2]))
        ]
        e_tt, g_rt, g_tz, div_w = q * vr, r_t - q * vt, z_t, r_w + q * wr + z_w
        if extra is not None:
            e_tt, g_rt, g_tz, div_w = e_tt + extra[1], g_rt + extra[0], g_tz + extra[2], div_w + extra[3]
        div_v = r_r + e_tt + z_z
        total = bulk * div_v + couple * div_w
        return dict(
            rr=mask21 * (total + 2.0 * shear * r_r),
            zz=mask21 * (total + 2.0 * shear * z_z),
            rt=mask21 * (shear * g_rt),
            rz=mask21 * (shear * (z_r + r_z)),
            tz=mask21 * (shear * g_tz),
            p=mask21 * (-(couple * div_v + modulus * div_w) + (source if extra is None else 0.0)),
            w=div_w,
        )

    x0 = stresses(v1, w1, None)
    pack(8, x0["w"][4:20])
    x1 = stresses(u, uw, [q * v1[0], q * v1[1], q * v1[2], q * w1[1]])
    e2, dw2 = q * u[1], q * uw[1]
    total2 = bulk * e2 + couple * dw2
    x2 = dict(
        rr=mask21 * total2,
        zz=mask21 * total2,
        rt=mask21 * (shear * (q * u[0])),
        tz=mask21 * (shear * (q * u[2])),
        p=mask21 * (-(couple * e2 + modulus * dw2)),
    )

    def radius_items(fields):
        slots = [i for i, x in enumerate(fields) if x is not None]
        stacked = jnp.concatenate([flat(fields[i]) for i in slots], axis=1)
        hi, lo = [jnp.concatenate([items[h, NR * i : NR * i + NR] for i in slots], axis=0) for h in range(2)]
        return mm(stacked, hi, lo).reshape(-1, 8, NR)

    def depth_items(fields):
        out = []
        for x in fields:
            if x is None:
                out += [jnp.zeros((8, NR), F32)] * 2
            else:
                out.append(x[20])
                out.append(has_below * below_partial(x[:4]))
        return jnp.stack(out)

    velocity_r = [v1[0], v1[1], v1[2], None, u[0], u[1], u[2], uw[0]]
    pack(13, radius_items([None if x is None else x[4:20] for x in velocity_r]))
    names_r = ("rr", "rt", "rz", "p")
    pack(14, radius_items([x[n][4:20] for x in (x0, x1) for n in names_r]))
    pack(15, depth_items([v1[0], v1[1], v1[2], None, u[0], u[1], u[2], uw[2]]))
    names_z = ("rz", "tz", "zz", "p")
    pack(16, depth_items([x[n] for x in (x0, x1) for n in names_z]))
    second = [x2[n][4 + 8 * h : 12 + 8 * h] if n in x2 else None for h in range(2) for n in names_r]
    pack(17, jnp.concatenate([radius_items(second), depth_items([x2.get(n) for n in names_z])], axis=0))

    def send(i):
        chunks = exchange_groups(hold[i])
        for k in range(8):
            pk[k, i] = chunks[k]

    for_each(2 * FIELDS_IN, send, unroll=9)


def ring(recv, coef, mark, mr, mz, dt_m, wr, wz, out):
    group = lax.axis_index("az")
    c = {name: coef[n] for n, name in enumerate(RING)}
    q = inverse_radius(group, GROUP)

    def field(f):
        return jnp.concatenate([recv[:, 2 * f], recv[:, 2 * f + 1]], axis=-1)

    def az(fields):
        x = jnp.concatenate([y.reshape(NT, -1) for y in fields], axis=1)
        xh, xl = parts(x)
        y = dot(dt_m[0], xh) + dot(dt_m[0], xl) + dot(dt_m[1], xh)
        res, at = [], 0
        for f in fields:
            n = f.shape[-1]
            res.append(y[:, at : at + n].reshape(f.shape))
            at += n
        return res

    def by_half(x):
        x = x.reshape(NT, 256)
        return [x[:, :128], x[:, 128:]]

    mr_h, mr_l = mr[0], mr[1]
    mz_h, mz_l = mz[0], mz[1]

    def radial(fields, halo):
        stacked = jnp.concatenate([h for f in fields for h in by_half(f)], axis=0)
        y = mm(stacked, mr_h, mr_l)
        res = []
        for i in range(len(fields)):
            halves_ = [
                y[128 * i + 64 * g : 128 * i + 64 * g + 64] + halo[64 * g : 64 * g + 64, 128 * i : 128 * i + 128]
                for g in range(2)
            ]
            res.append(jnp.concatenate(halves_, axis=1).reshape(8, 8, 256))
        return res

    def depth(fields, halo):
        stacked = jnp.concatenate([f.reshape(NT, 256) for f in fields], axis=0)
        y = mm(stacked, mz_h, mz_l)
        return [
            (y[64 * i : 64 * i + 64] + halo[:, 256 * i : 256 * i + 256]).reshape(8, 8, 256)
            for i in range(len(fields))
        ]

    rt, tt, tz, p = [field(f) for f in range(4)]
    pr2, pr3 = field(13), field(14)
    pd2 = [recv[:, 30], recv[:, 31]]
    pd3 = [recv[:, 32], recv[:, 33]]
    px = field(17)
    s_rt, s_tt, s_tz, s_p, d_pr2, d_pr3, d_pd2, d_pd3, d_px = az([rt, tt, tz, p, pr2, pr3, pd2[1], pd3[1], px])
    (dd_px,) = az([d_px])
    wr0, wr1 = (wr[0, 0], wr[0, 1]), (wr[1, 0], wr[1, 1])

    def stack_halves(x):
        return jnp.concatenate(by_half(x), axis=0)

    def radius_halo(zero, one):
        return mm(stack_halves(zero), *wr0) + mm(stack_halves(one), *wr1)

    hr2 = radius_halo(pr2, d_pr2)
    hz2 = mm((pd2[0] + d_pd2).reshape(NT, 128), wz[0], wz[1])
    half = dd_px.reshape(NT, 256)[:, :128]
    hr3 = radius_halo(pr3, d_pr3) + jnp.concatenate([mm(half, *wr0), mm(half, *wr1)], axis=0)
    hz3 = mm((pd3[0] + d_pd3).reshape(NT, 128) + dd_px.reshape(NT, 256)[:, 128:], wz[0], wz[1])

    cv, cf, cr = c["cv"], c["cf"], c["cr"]
    q_rt, q_tt, q_tz, q_p = q * s_rt, q * s_tt, q * s_tz, q * s_p
    dw = [-(cf * q_rt), -(cf * q_tt + cr * q_p), -(cf * q_tz)]
    v1 = [
        field(4) + cv * q_rt,
        field(5) + cv * q_tt + cf * q_p,
        field(6) + cv * q_tz,
    ]
    w1_t = field(7) + dw[1]
    r_r, r_t, r_z, r_w = radial([v1[0], v1[1], v1[2], dw[0]], hr2)
    z_r, z_t, z_z, z_w = depth([v1[0], v1[1], v1[2], dw[2]], hz2)
    a_r, a_t, a_z, a_w = az([v1[0], v1[1], v1[2], w1_t])
    e_tt = q * (v1[0] + a_t)
    div_v = r_r + e_tt + z_z
    div_w = field(8) + r_w + q * (dw[0] + a_w) + z_w
    total = c["bulk"] * div_v + c["couple"] * div_w
    shear = c["shear"]
    lanes = lax.broadcasted_iota(jnp.int32, (8, 256), 1) // GROUP
    source = jnp.where(lanes.astype(F32) == mark[...], jnp.where(group == 0, SOURCE, 0.0), 0.0)
    n_rr = total + 2.0 * shear * r_r
    n_tt = total + 2.0 * shear * e_tt
    n_zz = total + 2.0 * shear * z_z
    n_rt = shear * (q * (a_r - v1[1]) + r_t)
    n_rz = shear * (z_r + r_z)
    n_tz = shear * (z_t + q * a_z)
    n_p = source - (c["couple"] * div_v + c["modulus"] * div_w)

    r_rr, r_rt, r_rz, r_p = radial([n_rr, n_rt, n_rz, n_p], hr3)
    z_rz, z_tz, z_zz, z_p = depth([n_rz, n_tz, n_zz, n_p], hz3)
    a_rt, a_tt, a_tz, a_p = az([n_rt, n_tt, n_tz, n_p])
    d_r = q_rt + r_rr + z_rz + q * (a_rt + n_rr - n_tt)
    d_t = q_tt + r_rt + z_tz + q * (a_tt + 2.0 * n_rt)
    d_z = q_tz + r_rz + z_zz + q * (a_tz + n_rz)
    fk = c["fk"]
    g_r = r_p + fk * dw[0]
    g_t = q_p + q * a_p + fk * dw[1]
    g_z = z_p + fk * dw[2]
    sums = [
        2.0 * v1[0] + field(9) + cv * d_r + cf * g_r,
        2.0 * v1[1] + field(10) + cv * d_t + cf * g_t,
        2.0 * v1[2] + field(11) + cv * d_z + cf * g_z,
        2.0 * w1_t - field(12) - cf * d_t - cr * g_t,
    ]
    results = [s_rt, s_tt, s_tz, s_p, d_r, d_t, d_z, g_r, g_t, g_z] + az(sums)
    for f, x in enumerate(results):
        out[:, 2 * f] = x[:, :, :128]
        out[:, 2 * f + 1] = x[:, :, 128:]


def unpack(recv, hold, first, count):
    def receive(i):
        rows = exchange_groups([recv[k, 2 * first + i] for k in range(8)])
        for j in range(8):
            hold[i, j] = rows[j]

    for_each(2 * count, receive)
    return lambda f: jnp.concatenate([hold[2 * (f - first)], hold[2 * (f - first) + 1]], axis=0)


def advance(recv, keep, coef, new, mid, up, dn, hold):
    field = unpack(recv, hold, 0, 10)
    c = {name: coef[n] for n, name in enumerate(OWN)}
    q = inverse_radius(0, NR)
    cv, cf, cr = [spread_rows(c[n], 2, 4) for n in ("cv", "cf", "cr")]
    q_rt, q_tt, q_tz, q_p = [q * field(f) for f in range(4)]
    dv = [cv * q_rt, cv * q_tt + cf * q_p, cv * q_tz]
    dw = [-(cf * q_rt), -(cf * q_tt + cr * q_p), -(cf * q_tz)]
    for i in range(3):
        d, g = field(4 + i), field(7 + i)
        v1 = keep[i] + dv[i]
        w1 = keep[3 + i] + dw[i]
        v2 = v1 + keep[6 + i] + cv * d + cf * g
        w2 = w1 - keep[9 + i] - cf * d - cr * g
        new[i] = v2
        new[3 + i] = w2
        mid[i] = v1
        mid[3 + i] = w1
        x = v1 + v2
        up[i] = below_partial(x[12:])
        dn[i] = x[0]
        if i == 2:
            x = w1 + w2
            up[3] = below_partial(x[12:])
            dn[3] = x[0]


def settle(recv, v2, mid, v, s, psi, coef, mark, dr_m, v_out, s_out, m_out, edge, hold):
    field = unpack(recv, hold, 10, 4)
    v_out[...] = v2[...]
    has_below = coef[FLAGS]
    c = {name: coef[n] for n, name in enumerate(OWN)}
    q = inverse_radius(0, NR)

    def sp(value):
        return spread_rows(value, 2, 4)

    omega = sp(c["omega"])
    decay = [sp(c[f"decay{l}"]) for l in range(4)]
    for i in range(3):
        w1, w2 = mid[3 + i], v2[3 + i]
        first = w1 - v[3 + i] + omega * w1
        second = w2 - w1 + omega * w2
        for l in range(4):
            m_out[3 * l + i] = decay[l] * (decay[l] * (psi[3 * l + i] + first) + second)
    sums = [mid[i] + v2[i] for i in range(6)]
    zero = jnp.zeros((1, 8, NR), F32)
    z_r, z_t, z_z, z_w = [
        depth_derivative(jnp.concatenate([x, zero], axis=0), 0, 4, 0, has_below, float(ROW[4, 4]) * x[0], zero[0])[:16]
        for x in (sums[0], sums[1], sums[2], sums[5])
    ]
    stacked = jnp.concatenate([flat(x) for x in sums[:4]], axis=0)
    y = mm(stacked, dr_m[0], dr_m[1])
    r_r, r_t, r_z, r_w = [y[128 * i : 128 * i + 128].reshape(16, 8, NR) for i in range(4)]
    a_r, a_t, a_z, a_w = [field(10 + i) for i in range(4)]
    e_tt = q * (sums[0] + a_t)
    div_v = r_r + e_tt + z_z
    div_w = r_w + q * (sums[3] + a_w) + z_w
    couple, shear = sp(c["couple"]), sp(c["shear"])
    total = sp(c["bulk"]) * div_v + couple * div_w
    plane = lax.broadcasted_iota(jnp.int32, (16, 8, NR), 0)
    lane = lax.broadcasted_iota(jnp.int32, (16, 8, NR), 2)
    source = jnp.where((plane.astype(F32) == mark[:, :NR]) & (lane < 4 * RB), SOURCE * (1.0 + math.cos(0.9)), 0.0)
    updates = [
        total + 2.0 * shear * r_r,
        total + 2.0 * shear * e_tt,
        total + 2.0 * shear * z_z,
        shear * (q * (a_r - sums[1]) + r_t),
        shear * (z_r + r_z),
        shear * (z_t + q * a_z),
        source - (couple * div_v + sp(c["modulus"]) * div_w),
    ]
    for f, x in enumerate(updates):
        x = s[f] + x
        s_out[f] = x
        edge[f, 0] = x[0]
        edge[f, 1:] = x[12:]


def close(s_in, edge, up, dn, coef, s_out, new, sems):
    has_below = coef[FLAGS]
    c = {name: coef[n] for n, name in enumerate(OWN)}

    def update(slot, row, z_r, z_t, z_z, z_w):
        def at(name):
            return jnp.broadcast_to(c[name][row : row + 1, :], (8, NR))

        bulk, couple, modulus, shear = at("bulk"), at("couple"), at("modulus"), at("shear")
        total = bulk * z_z + couple * z_w
        new[0, slot] = edge[0, slot] + total
        new[1, slot] = edge[1, slot] + total
        new[2, slot] = edge[2, slot] + total + 2.0 * shear * z_z
        new[3, slot] = edge[3, slot]
        new[4, slot] = edge[4, slot] + shear * z_r
        new[5, slot] = edge[5, slot] + shear * z_t
        new[6, slot] = edge[6, slot] - (couple * z_z + modulus * z_w)

    update(0, 2, *[has_below * up[i] for i in range(4)])
    for slot in range(1, 5):
        weight = float(ROW[slot - 1, 4])
        update(slot, 5, *[weight * dn[i] for i in range(4)])
    copies = [
        pltpu.make_async_copy(new.at[:, 0:1], s_out.at[:, 0:1], sems.at[0]),
        pltpu.make_async_copy(new.at[:, 1:5], s_out.at[:, 12:16], sems.at[1]),
    ]
    for copy in copies:
        copy.start()
    for copy in copies:
        copy.wait()


def call(body, inputs, shapes, types=None, hbm=(), smem=(), scratch=(), out_hbm=False, alias=None, micros=1, vmem=VMEM_LIMIT):
    def space(i):
        return pltpu.HBM if i in hbm else pltpu.SMEM if i in smem else pltpu.VMEM

    return pl.pallas_call(
        body,
        out_shape=[jax.ShapeDtypeStruct(x, t) for x, t in zip(shapes, types or [F32] * len(shapes))],
        in_specs=[pl.BlockSpec(memory_space=space(i)) for i in range(len(inputs))],
        out_specs=[pl.BlockSpec(memory_space=pltpu.HBM if out_hbm else pltpu.VMEM) for _ in shapes],
        scratch_shapes=list(scratch),
        input_output_aliases=alias or {},
        compiler_params=pltpu.CompilerParams(vmem_limit_bytes=vmem),
        cost_estimate=pl.CostEstimate(flops=0, bytes_accessed=3 * 10**6 * micros, transcendentals=0),
        name=body.__name__,
    )(*inputs)


def shift(value, steps):
    count = lax.axis_size("depth")
    first, last = max(0, -steps), min(count, count - steps)
    return lax.ppermute(value, "depth", [(i, i + steps) for i in range(first, last)])


def on_device(velocity, stress, memory, layer_ids, materials, jkd, source_depth):
    c = constants()
    block = (PLANES, AZ, NR)
    tables = [layer_ids, materials, jkd]
    state, up, dn, ring_coef = call(
        prepare,
        tables + [stress, memory, velocity, c["dr"]],
        [(COEF + FLAGS + 2, AZ, NR), (UP_COEF + 7, AZ, NR), (DN_COEF + 7, AZ, NR), (len(RING), 8, 256)],
        hbm=range(7),
        scratch=[pltpu.SMEM(x.shape, x.dtype) for x in tables]
        + [pltpu.VMEM((n,) + block, F32) for n in (7, 12, 6)]
        + [pltpu.VMEM(c["dr"].shape, BF16), pltpu.SemaphoreType.DMA((7,))],
        vmem=VMEM_FULL,
    )
    up, dn = shift(up, 1), shift(dn, -1)
    staged = [c[n] for n in ("mr", "mz", "dt", "wr", "wz")]
    shapes = [x.shape[1:] if n < 2 else x.shape for n, x in enumerate(staged)]
    *matrices, state, coef, mark = call(
        stage,
        [source_depth] + staged + [state],
        shapes + [(COEF, AZ, NR), (FLAGS + 2, AZ, NR), (8, 256)],
        types=[BF16] * 5 + [F32] * 3,
        hbm=range(1, 7),
        smem=(0,),
        scratch=[pltpu.SemaphoreType.DMA((7,))],
    )
    packed, keep = call(
        launch,
        [stress, state, up, dn, coef, mark, c["dr"], c["items"]],
        [(8, 2 * FIELDS_IN, AZ, NR), (12,) + block],
        scratch=[pltpu.VMEM((2 * FIELDS_IN, 8, AZ, NR), F32)],
        micros=4,
    )
    packed = lax.all_to_all(packed, "az", split_axis=0, concat_axis=0, tiled=True)
    (back,) = call(ring, [packed, ring_coef, mark] + matrices, [(8, 2 * FIELDS_OUT, AZ, NR)], micros=3)
    back = lax.all_to_all(back, "az", split_axis=0, concat_axis=0, tiled=True)
    new, mid, up, dn = call(
        advance,
        [back, keep, coef],
        [(6,) + block, (6,) + block, (4, AZ, NR), (4, AZ, NR)],
        scratch=[pltpu.VMEM((20, 8, AZ, NR), F32)],
    )
    up, dn = shift(up, 1), shift(dn, -1)
    v_out, s_part, m_out, edge = call(
        settle,
        [back, new, mid, velocity, stress, memory, coef, mark, c["dr"]],
        [(6,) + block, (7,) + block, (12,) + block, (7, 5, AZ, NR)],
        scratch=[pltpu.VMEM((8, 8, AZ, NR), F32)],
        micros=3,
    )
    (s_out,) = call(
        close,
        [s_part, edge, up, dn, coef],
        [(7,) + block],
        hbm=(0,),
        scratch=[pltpu.VMEM((7, 5, AZ, NR), F32), pltpu.SemaphoreType.DMA((2,))],
        out_hbm=True,
        alias={0: 0},
    )
    return v_out, s_out, m_out


def solution(mesh):
    field = P(None, "depth", "az", None)
    return jax.shard_map(
        on_device,
        mesh=mesh,
        in_specs=(field, field, field, P("depth", None), P(), P(), P()),
        out_specs=(field, field, field),
        check_vma=False,
    )
```

```python
import functools
import math

import jax
import jax.numpy as jnp
import ml_dtypes
import numpy as np
from jax import lax
from jax.experimental import pallas as pl
from jax.experimental.pallas import tpu as pltpu
from jax.sharding import PartitionSpec as P

NR = 128
NT = 64
RB = 4
PLANES = 16
AZ = 8
GROUP = 16
DT = 0.02
SOURCE = DT * 40.0
R_INNER = 1.0
F32 = jnp.float32
BF16 = jnp.bfloat16
FIELDS_IN = 18
FIELDS_OUT = 14
VMEM_LIMIT = 32 * 2**20
VMEM_FULL = 56 * 2**20
UP_COEF = 52
DN_COEF = 20
SHARED = ("cv", "cf", "cr", "bulk", "couple", "modulus", "shear")
OWN = SHARED + ("fric", "kappa", "omega", "decay0", "decay1", "decay2", "decay3")
FLAGS = len(OWN)
COEF = 12 * PLANES
RING = SHARED + ("fk",)


def gll_basis():
    root_value = math.sqrt(3.0 / 7.0)
    nodes = np.array([-1.0, -root_value, 0.0, root_value, 1.0])
    weights = np.array([0.1, 49.0 / 90.0, 32.0 / 45.0, 49.0 / 90.0, 0.1])
    offsets = nodes[:, None] - nodes[None, :] + np.eye(5)
    factors = np.prod(offsets, axis=1)
    derivative = factors[:, None] / factors[None, :] / offsets
    diagonal = np.sum(1.0 / offsets, axis=1) - 1.0
    derivative = derivative * (1.0 - np.eye(5)) + np.eye(5) * diagonal[:, None]
    return nodes, weights, derivative


NODES, WEIGHTS, DERIV = gll_basis()
ROW = DERIV * np.array([1.0, 2.0, 2.0, 2.0, 1.0])[:, None]


def line_operator(count, first):
    matrix = np.zeros((count + 1, count + 1))
    for e in range(count // 4):
        matrix[4 * e : 4 * e + 5, 4 * e : 4 * e + 5] += ROW
    if first:
        matrix[0] *= 2.0
    else:
        matrix[0, 0] += ROW[4, 4]
    return matrix[:count, :count]


def halves(matrix):
    hi = matrix.astype(np.float32).astype(ml_dtypes.bfloat16)
    lo = (matrix - hi.astype(np.float64)).astype(np.float32).astype(ml_dtypes.bfloat16)
    return np.stack([hi, lo])


def azimuth_operator():
    positions = np.arange(NT)
    offsets = positions[:, None] - positions[None, :]
    modes = np.arange(1, NT // 2)
    phases = 2.0 * np.pi * offsets[:, :, None] * modes / NT
    return -(2.0 / NT) * np.sum(modes * np.sin(phases), axis=2)


@functools.lru_cache(None)
def constants():
    groups = NR // GROUP
    c = {}
    c["dr"] = halves(line_operator(NR, True).T)
    items = np.zeros((8, NR, groups, 16))
    for s in range(8):
        for k in range(groups):
            if GROUP * (k + 1) < NR:
                items[s, GROUP * (k + 1), k, 2 * s] = 1.0
            if k:
                items[s, GROUP * k - 4 : GROUP * k, k, 2 * s + 1] = ROW[4, :4]
    c["items"] = halves(items.reshape(8 * NR, 128))
    c["dt"] = halves(azimuth_operator())
    c["mr"] = np.stack([halves(np.kron(np.eye(8), line_operator(16, first).T)) for first in (False, True)])
    c["mz"] = np.stack([halves(np.kron(line_operator(16, first).T, np.eye(16))) for first in (False, True)])
    spread = np.zeros((2, 16))
    spread[0, 12:] = ROW[:4, 4]
    spread[1, 0] = 1.0
    wr = np.zeros((2, 8, 16, 4, 8, 16))
    wz = np.zeros((8, 16, 4, 16, 16))
    for f in range(4):
        for side in range(2):
            for j in range(8):
                for order in range(2):
                    wr[order, j, 8 * order + 2 * f + side, f, j] = spread[side]
            for r in range(16):
                wz[2 * f + side, r, f, :, r] = spread[side]
    c["wr"] = np.stack([halves(w) for w in wr.reshape(2, 128, 512)])
    c["wz"] = halves(wz.reshape(128, 1024))
    return c


def roll(x, shift):
    return pltpu.roll(x, shift % x.shape[-1], x.ndim - 1)


def dot(a, b):
    return jnp.dot(a, b, preferred_element_type=F32)


def parts(x):
    hi = x.astype(BF16)
    return hi, (x - hi.astype(F32)).astype(BF16)


def mm(x, hi, lo):
    xh, xl = parts(x)
    return dot(xh, hi) + dot(xl, hi) + dot(xh, lo)


def inverse_radius(group, width):
    lane = lax.broadcasted_iota(jnp.int32, (8, 128 if width == NR else 256), 1) % width
    place = lane % 4
    offset = jnp.zeros(lane.shape, F32)
    for j in range(4):
        offset = jnp.where(place == j, float(R_INNER + 0.5 * (1.0 + NODES[j])), offset)
    return 1.0 / (offset + (lane // 4 + 4 * group).astype(F32))


def own_ids(lids):
    row = lax.broadcasted_iota(jnp.int32, (8, NR), 0)
    fluid = lax.broadcasted_iota(jnp.int32, (8, NR), 1) < 4 * RB
    value = jnp.zeros((8, NR), jnp.int32)
    for e in range(4):
        value = jnp.where(row == 2 + e, jnp.where(fluid, lids[e, 0], lids[e, NR // 4 - 1]), value)
    return value.astype(F32)


def coefficients(ids, tab):
    hits = [ids == float(m) for m in range(8)]
    materials, jkd = tab

    def pick(table, column):
        value = jnp.where(hits[0], table[0, column], 0.0)
        for m in range(1, 8):
            value = jnp.where(hits[m], table[m, column], value)
        return value

    lame, mu, modulus, beta, rho, rho_f, tort, fric = [pick(materials, c) for c in range(8)]
    omega = pick(jkd, 0)
    weights = [pick(jkd, 1 + l) for l in range(4)]
    rates = [pick(jkd, 5 + l) for l in range(4)]
    rho_w = tort * rho_f
    scale = DT / (rho * rho_w - rho_f * rho_f)
    decay = [1.0 / (1.0 + DT * (rate + omega)) for rate in rates]
    gain = sum(a * c for a, c in zip(weights, decay))
    return dict(
        cv=rho_w * scale,
        cf=rho_f * scale,
        cr=rho * scale,
        fric=fric,
        omega=DT * omega,
        weights=weights,
        decay=decay,
        decay0=decay[0],
        decay1=decay[1],
        decay2=decay[2],
        decay3=decay[3],
        kappa=(1.0 + DT * omega) * gain,
        fk=fric * ((1.0 + DT * omega) * gain),
        bulk=DT * (lame + beta * beta * modulus),
        couple=DT * beta * modulus,
        modulus=DT * modulus,
        shear=DT * mu,
    )


def spread_rows(value, first, count, tail=False):
    rows = [jnp.broadcast_to(value[first + e : first + e + 1, :], (8, NR)) for e in range(count + tail)]
    planes = [rows[i // 4] for i in range(4 * count + tail)]
    return jnp.stack(planes)


def combine(row, nodes):
    total = None
    for weight, node in zip(row, nodes):
        term = float(weight) * node
        total = term if total is None else total + term
    return total


def depth_derivative(x, lo, hi, edge, has_below, low=None, high=None):
    count = (x.shape[0] - 1) // 4
    blocks = x[: 4 * count].reshape((count, 4) + x.shape[1:])
    last = [blocks[e + 1, 0] if e + 1 < count else x[4 * count] for e in range(count)]

    def nodes(e):
        return [blocks[e, l] for l in range(4)] + [last[e]]

    out = []
    for e in range(lo, hi + 1):
        upper = combine(ROW[0], nodes(e)) if e < count else high
        lower = combine(ROW[4], nodes(e - 1)) if e > 0 else low
        if e == edge:
            upper = (2.0 - has_below) * upper
            lower = has_below * lower
        out.append(upper + lower)
        if e < hi:
            for i in range(1, 4):
                out.append(combine(ROW[i], nodes(e)))
    return jnp.stack(out)


def below_partial(x):
    return combine(ROW[4, :4], [x[l] for l in range(4)])


def lane_groups():
    return lax.broadcasted_iota(jnp.int32, (8, NR), 1) // GROUP


def exchange_groups(x):
    groups = lane_groups()
    rows = [roll(x[j], GROUP * j) if j else x[j] for j in range(8)]
    for s in (1, 2, 4):
        stay = (groups & s) == 0
        rows = [jnp.where(stay, rows[j], rows[(j + s) % 8]) for j in range(8)]
    return [roll(rows[-k % 8], -GROUP * k) if k else rows[0] for k in range(8)]


def for_each(count, body, unroll=4):
    lax.fori_loop(0, count, lambda i, _: (body(i), 0)[1], 0, unroll=unroll)


def flat(x):
    return x.reshape(-1, NR)


def prepare(
    lids_hbm, mat_hbm, jkd_hbm, s_hbm, psi_hbm, v_hbm, dr_hbm,
    state, far, near, ring_coef,
    up, dn, lids, mat, jkd, s, psi, v, dr_m, sems,
):
    pairs = (
        (lids_hbm, lids), (mat_hbm, mat), (jkd_hbm, jkd), (s_hbm, s), (psi_hbm, psi),
        (v_hbm, v), (dr_hbm, dr_m),
    )
    copies = [pltpu.make_async_copy(a, b, sems.at[i]) for i, (a, b) in enumerate(pairs)]
    for copy in copies:
        copy.start()
    for copy in copies[:3]:
        copy.wait()
    device = lax.axis_index("depth")
    rows = lax.broadcasted_iota(jnp.int32, (8, NR), 0)
    c = coefficients(own_ids(lids), (mat, jkd))
    mine = (rows >= 2) & (rows < 6)
    for n, name in enumerate(OWN):
        state[COEF + n] = jnp.where(mine, c[name], 0.0)
    state[COEF + FLAGS] = jnp.full((8, NR), jnp.where(device > 0, 1.0, 0.0), F32)
    state[COEF + FLAGS + 1] = jnp.full((8, NR), jnp.where(device < lax.axis_size("depth") - 1, 1.0, 0.0), F32)
    for n, name in enumerate(SHARED):
        swapped = pltpu.roll(c[name], 4, 0)
        up[UP_COEF + n] = jnp.where(rows < 2, swapped, 0.0)
        dn[DN_COEF + n] = jnp.where(rows >= 6, swapped, 0.0)
    element = lax.broadcasted_iota(jnp.int32, (8, 256), 1) // 64
    group = lax.axis_index("az")
    ids = jnp.zeros((8, 256), jnp.int32)
    for e in range(4):
        ids = jnp.where(element == e, lids[e, 4 * group], ids)
    rc = coefficients(ids.astype(F32), (mat, jkd))
    for n, name in enumerate(RING):
        ring_coef[n] = rc[name]

    def sp(value):
        return spread_rows(value, 2, 4)

    has_below = jnp.where(device > 0, 1.0, 0.0)
    q = inverse_radius(0, NR)
    cv, cf, cr, fric = [sp(c[n]) for n in ("cv", "cf", "cr", "fric")]
    weights = [sp(w) for w in c["weights"]]
    decayed = [sp(w * d) for w, d in zip(c["weights"], c["decay"])]
    for copy in copies[3:]:
        copy.wait()
    rr, tt, zz, rt, rz, tz, p = [s[f] for f in range(7)]
    stacked = jnp.concatenate([flat(x) for x in (rr, rt, rz, p)], axis=0)
    y = mm(stacked, dr_m[0], dr_m[1])
    r_rr, r_rt, r_rz, r_p = [y[128 * i : 128 * i + 128].reshape(16, 8, NR) for i in range(4)]
    zero = jnp.zeros((1, 8, NR), F32)
    z_rz, z_tz, z_zz, z_p = [
        depth_derivative(jnp.concatenate([x, zero], axis=0), 0, 4, 0, has_below, float(ROW[4, 4]) * x[0], zero[0])[:16]
        for x in (rz, tz, zz, p)
    ]
    div = [r_rr + z_rz + q * (rr - tt), r_rt + z_tz + 2.0 * q * rt, r_rz + z_zz + q * rz]
    grads = (r_p, None, z_p)
    new = []
    for i in range(3):
        memory = [psi[3 * l + i] for l in range(4)]
        total = sum(w * m for w, m in zip(weights, memory))
        later = sum(w * (m - v[3 + i]) for w, m in zip(decayed, memory))
        g0, g1 = fric * total, fric * later
        if grads[i] is not None:
            g0, g1 = g0 + grads[i], g1 + grads[i]
        d_v, d_w = cv * div[i], cf * div[i]
        for n, x in enumerate(
            (v[i] + d_v + cf * g0, v[3 + i] - d_w - cr * g0, d_v + cf * g1, d_w + cr * g1)
        ):
            at = 16 * (3 * n + i)
            state[at : at + 16] = x
            if n < 2:
                f = 3 * n + i
                up[4 * f : 4 * f + 4] = x[12:]
                dn[f] = x[0]
                if f < 3 or f == 5:
                    place = min(f, 3)
                    up[40 + place] = below_partial(x[8:12])
                    dn[12 + place] = combine(ROW[0, 1:], [x[1 + l] for l in range(4)])
    q_rt, q_tt, q_tz, q_p = q * rt, q * tt, q * tz, q * p
    u = [cv * q_rt, cv * q_tt + cf * q_p, cv * q_tz, -(cf * q_tz)]
    for i, x in enumerate(u):
        up[44 + i] = below_partial(x[8:12])
        dn[16 + i] = combine(ROW[0, 1:], [x[1 + l] for l in range(4)])
    for i, x in enumerate((rt, tt, tz, p)):
        up[24 + 4 * i : 28 + 4 * i] = x[12:]
    for i, x in enumerate((rt, tt, tz, p, rz, zz)):
        dn[6 + i] = x[0]
    for i, x in enumerate((rz, tz, zz, p)):
        up[48 + i] = below_partial(x[12:])
    dn[DN_COEF + 7 :] = jnp.zeros((UP_COEF - DN_COEF, 8, NR), F32)
    outgoing(up[...], dn[...], near, far)


def is_even():
    return lax.axis_index("depth") % 2 == 0


def outgoing(up, dn, near, far):
    even = is_even()
    near[...] = jnp.where(even, up, dn)
    far[...] = jnp.where(even, dn, up)


def incoming(near, far):
    even = is_even()
    x, y = near[...], far[...]
    return jnp.where(even, y, x), jnp.where(even, x, y)


def stage(*refs):
    src, *pairs, mark, sems = refs
    count = 6
    first_r = jnp.where(lax.axis_index("az") == 0, 1, 0)
    first_z = jnp.where(lax.axis_index("depth") == 0, 1, 0)
    sources = list(pairs[:count])
    sources[0] = sources[0].at[first_r]
    sources[1] = sources[1].at[first_z]
    state = sources.pop()
    sources += [state.at[0:COEF], state.at[COEF:]]
    copies = [pltpu.make_async_copy(a, b, sems.at[i]) for i, (a, b) in enumerate(zip(sources, pairs[count:]))]
    for copy in copies:
        copy.start()
    mark[...] = jnp.full((8, 256), (src[0] - PLANES * lax.axis_index("depth")).astype(F32), F32)
    for copy in copies:
        copy.wait()


def launch(s, state, far, near, coef, mark, dr_m, items, pk, keep, hold):
    has_below = coef[FLAGS]
    has_above = coef[FLAGS + 1]
    up, dn = incoming(near, far)
    c = {name: coef[n] for n, name in enumerate(OWN)}
    for n, name in enumerate(SHARED):
        c[name] = c[name] + up[UP_COEF + n] + dn[DN_COEF + n]
    q = inverse_radius(0, NR)
    cv, cf, cr, bulk, couple, modulus, shear = [spread_rows(c[n], 1, 5, True) for n in SHARED]

    def radial(fields):
        stacked = jnp.concatenate([flat(x) for x in fields], axis=0)
        out = mm(stacked, dr_m[0], dr_m[1])
        count = fields[0].shape[0]
        return [out[8 * count * i : 8 * count * (i + 1)].reshape(count, 8, NR) for i in range(len(fields))]

    def added(f, partial, above):
        x = s[f]
        planes = [float(ROW[l, 4]) * x[0] for l in range(4)]
        planes.append(has_below * partial)
        planes += [float(ROW[l, 4]) * above for l in range(4)]
        planes.append(has_above * below_partial(x[12:]))
        return jnp.stack(planes)

    def edges(x):
        return jnp.concatenate([x[:5], x[16:]], axis=0)

    e_cv, e_cf, e_cr = edges(cv), edges(cf), edges(cr)
    m_rz, m_tz, m_zz, m_p = [
        added(f, up[48 + i], dn[n]) for i, (f, n) in enumerate(((4, 10), (5, 8), (2, 11), (6, 9)))
    ]
    to_v = [e_cv * m_rz, e_cv * m_tz, e_cv * m_zz + e_cf * m_p]
    to_w = [e_cf * m_rz, e_cf * m_tz, e_cf * m_zz + e_cr * m_p]

    def inner_planes(n, more):
        x = state[16 * n : 16 * n + 16]
        return [x[:1] + more[4:5], x[1:12], x[12:] + more[5:9]]

    def whole(f, more):
        ends = [up[4 * f : 4 * f + 4] + more[:4]], [dn[f : f + 1] + more[9:]]
        return jnp.concatenate(ends[0] + inner_planes(f, more) + ends[1], axis=0)

    v1 = [whole(i, to_v[i]) for i in range(3)]
    w1 = [whole(3 + i, -to_w[i]) for i in range(3)]
    q_rt, q_tt, q_tz, q_p = [
        q * jnp.concatenate([up[24 + 4 * i : 28 + 4 * i], s[f], dn[6 + i : 7 + i]], axis=0)
        for i, f in enumerate((3, 1, 5, 6))
    ]
    u = [cv * q_rt, cv * q_tt + cf * q_p, cv * q_tz]
    uw = [-(cf * q_rt), -(cf * q_tt + cr * q_p), -(cf * q_tz)]

    def pack(f, planes):
        hold[2 * f] = planes[:8]
        hold[2 * f + 1] = planes[8:]

    for f, x in enumerate((3, 1, 5, 6)):
        pack(f, s[x])
    fk = spread_rows(c["fric"] * c["kappa"], 2, 4)
    o_cf, o_cr = cf[4:20], cr[4:20]
    for i in range(3):
        v_i, w_i = v1[i][4:20], w1[i][4:20]
        a = jnp.concatenate(inner_planes(6 + i, to_v[i]), axis=0) + o_cf * (fk * w_i)
        b = jnp.concatenate(inner_planes(9 + i, to_w[i]), axis=0) + o_cr * (fk * w_i)
        pack(4 + i, v_i)
        pack(9 + i, a)
        keep[i] = v_i
        keep[3 + i] = w_i
        keep[6 + i] = a
        keep[9 + i] = b
        if i == 1:
            pack(7, w_i)
            pack(12, b)

    mask21 = jnp.where(lax.broadcasted_iota(jnp.int32, (21, 8, NR), 0) < 20, 1.0, has_above)
    plane21 = lax.broadcasted_iota(jnp.int32, (21, 8, NR), 0) - 4
    lane21 = lax.broadcasted_iota(jnp.int32, (21, 8, NR), 2)
    source = jnp.where((plane21.astype(F32) == mark[:, :NR]) & (lane21 < 4 * RB), SOURCE, 0.0)

    def stresses(v, w, extra):
        at = 12 if extra is None else 16
        low = 40 if extra is None else 44
        vr, vt, wr = v[0], v[1], w[0]
        r_r, r_t, r_z, r_w = radial([vr, vt, v[2], wr])
        z_r, z_t, z_z, z_w = [
            depth_derivative(
                x,
                0,
                5,
                1,
                has_below,
                up[low + n] + float(ROW[4, 4]) * x[0],
                dn[at + n] + float(ROW[0, 0]) * x[20],
            )
            for n, x in enumerate((v[0], v[1], v[2], w[2]))
        ]
        e_tt, g_rt, g_tz, div_w = q * vr, r_t - q * vt, z_t, r_w + q * wr + z_w
        if extra is not None:
            e_tt, g_rt, g_tz, div_w = e_tt + extra[1], g_rt + extra[0], g_tz + extra[2], div_w + extra[3]
        div_v = r_r + e_tt + z_z
        total = bulk * div_v + couple * div_w
        return dict(
            rr=mask21 * (total + 2.0 * shear * r_r),
            zz=mask21 * (total + 2.0 * shear * z_z),
            rt=mask21 * (shear * g_rt),
            rz=mask21 * (shear * (z_r + r_z)),
            tz=mask21 * (shear * g_tz),
            p=mask21 * (-(couple * div_v + modulus * div_w) + (source if extra is None else 0.0)),
            w=div_w,
        )

    x0 = stresses(v1, w1, None)
    pack(8, x0["w"][4:20])
    x1 = stresses(u, uw, [q * v1[0], q * v1[1], q * v1[2], q * w1[1]])
    e2, dw2 = q * u[1], q * uw[1]
    total2 = bulk * e2 + couple * dw2
    x2 = dict(
        rr=mask21 * total2,
        zz=mask21 * total2,
        rt=mask21 * (shear * (q * u[0])),
        tz=mask21 * (shear * (q * u[2])),
        p=mask21 * (-(couple * e2 + modulus * dw2)),
    )

    def radius_items(fields):
        slots = [i for i, x in enumerate(fields) if x is not None]
        stacked = jnp.concatenate([flat(fields[i]) for i in slots], axis=1)
        hi, lo = [jnp.concatenate([items[h, NR * i : NR * i + NR] for i in slots], axis=0) for h in range(2)]
        return mm(stacked, hi, lo).reshape(-1, 8, NR)

    def depth_items(fields):
        out = []
        for x in fields:
            if x is None:
                out += [jnp.zeros((8, NR), F32)] * 2
            else:
                out.append(x[20])
                out.append(has_below * below_partial(x[:4]))
        return jnp.stack(out)

    velocity_r = [v1[0], v1[1], v1[2], None, u[0], u[1], u[2], uw[0]]
    pack(13, radius_items([None if x is None else x[4:20] for x in velocity_r]))
    names_r = ("rr", "rt", "rz", "p")
    pack(14, radius_items([x[n][4:20] for x in (x0, x1) for n in names_r]))
    pack(15, depth_items([v1[0], v1[1], v1[2], None, u[0], u[1], u[2], uw[2]]))
    names_z = ("rz", "tz", "zz", "p")
    pack(16, depth_items([x[n] for x in (x0, x1) for n in names_z]))
    second = [x2[n][4 + 8 * h : 12 + 8 * h] if n in x2 else None for h in range(2) for n in names_r]
    pack(17, jnp.concatenate([radius_items(second), depth_items([x2.get(n) for n in names_z])], axis=0))

    def send(i):
        chunks = exchange_groups(hold[i])
        for k in range(8):
            pk[k, i] = chunks[k]

    for_each(2 * FIELDS_IN, send, unroll=9)


def ring(recv, coef, mark, mr, mz, dt_m, wr, wz, out):
    group = lax.axis_index("az")
    c = {name: coef[n] for n, name in enumerate(RING)}
    q = inverse_radius(group, GROUP)

    def field(f):
        return jnp.concatenate([recv[:, 2 * f], recv[:, 2 * f + 1]], axis=-1)

    def az(fields):
        x = jnp.concatenate([y.reshape(NT, -1) for y in fields], axis=1)
        xh, xl = parts(x)
        y = dot(dt_m[0], xh) + dot(dt_m[0], xl) + dot(dt_m[1], xh)
        res, at = [], 0
        for f in fields:
            n = f.shape[-1]
            res.append(y[:, at : at + n].reshape(f.shape))
            at += n
        return res

    def by_half(x):
        x = x.reshape(NT, 256)
        return [x[:, :128], x[:, 128:]]

    mr_h, mr_l = mr[0], mr[1]
    mz_h, mz_l = mz[0], mz[1]

    def radial(fields, halo):
        stacked = jnp.concatenate([h for f in fields for h in by_half(f)], axis=0)
        y = mm(stacked, mr_h, mr_l)
        res = []
        for i in range(len(fields)):
            halves_ = [
                y[128 * i + 64 * g : 128 * i + 64 * g + 64] + halo[64 * g : 64 * g + 64, 128 * i : 128 * i + 128]
                for g in range(2)
            ]
            res.append(jnp.concatenate(halves_, axis=1).reshape(8, 8, 256))
        return res

    def depth(fields, halo):
        stacked = jnp.concatenate([f.reshape(NT, 256) for f in fields], axis=0)
        y = mm(stacked, mz_h, mz_l)
        return [
            (y[64 * i : 64 * i + 64] + halo[:, 256 * i : 256 * i + 256]).reshape(8, 8, 256)
            for i in range(len(fields))
        ]

    rt, tt, tz, p = [field(f) for f in range(4)]
    pr2, pr3 = field(13), field(14)
    pd2 = [recv[:, 30], recv[:, 31]]
    pd3 = [recv[:, 32], recv[:, 33]]
    px = field(17)
    s_rt, s_tt, s_tz, s_p, d_pr2, d_pr3, d_pd2, d_pd3, d_px = az([rt, tt, tz, p, pr2, pr3, pd2[1], pd3[1], px])
    (dd_px,) = az([d_px])
    wr0, wr1 = (wr[0, 0], wr[0, 1]), (wr[1, 0], wr[1, 1])

    def stack_halves(x):
        return jnp.concatenate(by_half(x), axis=0)

    def radius_halo(zero, one):
        return mm(stack_halves(zero), *wr0) + mm(stack_halves(one), *wr1)

    hr2 = radius_halo(pr2, d_pr2)
    hz2 = mm((pd2[0] + d_pd2).reshape(NT, 128), wz[0], wz[1])
    half = dd_px.reshape(NT, 256)[:, :128]
    hr3 = radius_halo(pr3, d_pr3) + jnp.concatenate([mm(half, *wr0), mm(half, *wr1)], axis=0)
    hz3 = mm((pd3[0] + d_pd3).reshape(NT, 128) + dd_px.reshape(NT, 256)[:, 128:], wz[0], wz[1])

    cv, cf, cr = c["cv"], c["cf"], c["cr"]
    q_rt, q_tt, q_tz, q_p = q * s_rt, q * s_tt, q * s_tz, q * s_p
    dw = [-(cf * q_rt), -(cf * q_tt + cr * q_p), -(cf * q_tz)]
    v1 = [
        field(4) + cv * q_rt,
        field(5) + cv * q_tt + cf * q_p,
        field(6) + cv * q_tz,
    ]
    w1_t = field(7) + dw[1]
    r_r, r_t, r_z, r_w = radial([v1[0], v1[1], v1[2], dw[0]], hr2)
    z_r, z_t, z_z, z_w = depth([v1[0], v1[1], v1[2], dw[2]], hz2)
    a_r, a_t, a_z, a_w = az([v1[0], v1[1], v1[2], w1_t])
    e_tt = q * (v1[0] + a_t)
    div_v = r_r + e_tt + z_z
    div_w = field(8) + r_w + q * (dw[0] + a_w) + z_w
    total = c["bulk"] * div_v + c["couple"] * div_w
    shear = c["shear"]
    lanes = lax.broadcasted_iota(jnp.int32, (8, 256), 1) // GROUP
    source = jnp.where(lanes.astype(F32) == mark[...], jnp.where(group == 0, SOURCE, 0.0), 0.0)
    n_rr = total + 2.0 * shear * r_r
    n_tt = total + 2.0 * shear * e_tt
    n_zz = total + 2.0 * shear * z_z
    n_rt = shear * (q * (a_r - v1[1]) + r_t)
    n_rz = shear * (z_r + r_z)
    n_tz = shear * (z_t + q * a_z)
    n_p = source - (c["couple"] * div_v + c["modulus"] * div_w)

    r_rr, r_rt, r_rz, r_p = radial([n_rr, n_rt, n_rz, n_p], hr3)
    z_rz, z_tz, z_zz, z_p = depth([n_rz, n_tz, n_zz, n_p], hz3)
    a_rt, a_tt, a_tz, a_p = az([n_rt, n_tt, n_tz, n_p])
    d_r = q_rt + r_rr + z_rz + q * (a_rt + n_rr - n_tt)
    d_t = q_tt + r_rt + z_tz + q * (a_tt + 2.0 * n_rt)
    d_z = q_tz + r_rz + z_zz + q * (a_tz + n_rz)
    fk = c["fk"]
    g_r = r_p + fk * dw[0]
    g_t = q_p + q * a_p + fk * dw[1]
    g_z = z_p + fk * dw[2]
    sums = [
        2.0 * v1[0] + field(9) + cv * d_r + cf * g_r,
        2.0 * v1[1] + field(10) + cv * d_t + cf * g_t,
        2.0 * v1[2] + field(11) + cv * d_z + cf * g_z,
        2.0 * w1_t - field(12) - cf * d_t - cr * g_t,
    ]
    results = [s_rt, s_tt, s_tz, s_p, d_r, d_t, d_z, g_r, g_t, g_z] + az(sums)
    for f, x in enumerate(results):
        out[:, 2 * f] = x[:, :, :128]
        out[:, 2 * f + 1] = x[:, :, 128:]


def unpack(recv, hold, first, count):
    def receive(i):
        rows = exchange_groups([recv[k, 2 * first + i] for k in range(8)])
        for j in range(8):
            hold[i, j] = rows[j]

    for_each(2 * count, receive)
    return lambda f: jnp.concatenate([hold[2 * (f - first)], hold[2 * (f - first) + 1]], axis=0)


def advance(recv, keep, coef, new, mid, far, near, hold):
    up, dn = [], []
    field = unpack(recv, hold, 0, 10)
    c = {name: coef[n] for n, name in enumerate(OWN)}
    q = inverse_radius(0, NR)
    cv, cf, cr = [spread_rows(c[n], 2, 4) for n in ("cv", "cf", "cr")]
    q_rt, q_tt, q_tz, q_p = [q * field(f) for f in range(4)]
    dv = [cv * q_rt, cv * q_tt + cf * q_p, cv * q_tz]
    dw = [-(cf * q_rt), -(cf * q_tt + cr * q_p), -(cf * q_tz)]
    for i in range(3):
        d, g = field(4 + i), field(7 + i)
        v1 = keep[i] + dv[i]
        w1 = keep[3 + i] + dw[i]
        v2 = v1 + keep[6 + i] + cv * d + cf * g
        w2 = w1 - keep[9 + i] - cf * d - cr * g
        new[i] = v2
        new[3 + i] = w2
        mid[i] = v1
        mid[3 + i] = w1
        x = v1 + v2
        up.append(below_partial(x[12:]))
        dn.append(x[0])
        if i == 2:
            x = w1 + w2
            up.append(below_partial(x[12:]))
            dn.append(x[0])
    outgoing(jnp.stack(up), jnp.stack(dn), near, far)


def settle(recv, v2, mid, v, s, psi, coef, mark, dr_m, v_out, s_out, m_out, edge, hold):
    field = unpack(recv, hold, 10, 4)
    v_out[...] = v2[...]
    has_below = coef[FLAGS]
    c = {name: coef[n] for n, name in enumerate(OWN)}
    q = inverse_radius(0, NR)

    def sp(value):
        return spread_rows(value, 2, 4)

    omega = sp(c["omega"])
    decay = [sp(c[f"decay{l}"]) for l in range(4)]
    for i in range(3):
        w1, w2 = mid[3 + i], v2[3 + i]
        first = w1 - v[3 + i] + omega * w1
        second = w2 - w1 + omega * w2
        for l in range(4):
            m_out[3 * l + i] = decay[l] * (decay[l] * (psi[3 * l + i] + first) + second)
    sums = [mid[i] + v2[i] for i in range(6)]
    zero = jnp.zeros((1, 8, NR), F32)
    z_r, z_t, z_z, z_w = [
        depth_derivative(jnp.concatenate([x, zero], axis=0), 0, 4, 0, has_below, float(ROW[4, 4]) * x[0], zero[0])[:16]
        for x in (sums[0], sums[1], sums[2], sums[5])
    ]
    stacked = jnp.concatenate([flat(x) for x in sums[:4]], axis=0)
    y = mm(stacked, dr_m[0], dr_m[1])
    r_r, r_t, r_z, r_w = [y[128 * i : 128 * i + 128].reshape(16, 8, NR) for i in range(4)]
    a_r, a_t, a_z, a_w = [field(10 + i) for i in range(4)]
    e_tt = q * (sums[0] + a_t)
    div_v = r_r + e_tt + z_z
    div_w = r_w + q * (sums[3] + a_w) + z_w
    couple, shear = sp(c["couple"]), sp(c["shear"])
    total = sp(c["bulk"]) * div_v + couple * div_w
    plane = lax.broadcasted_iota(jnp.int32, (16, 8, NR), 0)
    lane = lax.broadcasted_iota(jnp.int32, (16, 8, NR), 2)
    source = jnp.where((plane.astype(F32) == mark[:, :NR]) & (lane < 4 * RB), SOURCE * (1.0 + math.cos(0.9)), 0.0)
    updates = [
        total + 2.0 * shear * r_r,
        total + 2.0 * shear * e_tt,
        total + 2.0 * shear * z_z,
        shear * (q * (a_r - sums[1]) + r_t),
        shear * (z_r + r_z),
        shear * (z_t + q * a_z),
        source - (couple * div_v + sp(c["modulus"]) * div_w),
    ]
    for f, x in enumerate(updates):
        x = s[f] + x
        s_out[f] = x
        edge[f, 0] = x[0]
        edge[f, 1:] = x[12:]


def close(s_in, edge, far, near, coef, s_out, new, sems):
    up, dn = incoming(near, far)
    has_below = coef[FLAGS]
    c = {name: coef[n] for n, name in enumerate(OWN)}

    def update(slot, row, z_r, z_t, z_z, z_w):
        def at(name):
            return jnp.broadcast_to(c[name][row : row + 1, :], (8, NR))

        bulk, couple, modulus, shear = at("bulk"), at("couple"), at("modulus"), at("shear")
        total = bulk * z_z + couple * z_w
        new[0, slot] = edge[0, slot] + total
        new[1, slot] = edge[1, slot] + total
        new[2, slot] = edge[2, slot] + total + 2.0 * shear * z_z
        new[3, slot] = edge[3, slot]
        new[4, slot] = edge[4, slot] + shear * z_r
        new[5, slot] = edge[5, slot] + shear * z_t
        new[6, slot] = edge[6, slot] - (couple * z_z + modulus * z_w)

    update(0, 2, *[has_below * up[i] for i in range(4)])
    for slot in range(1, 5):
        weight = float(ROW[slot - 1, 4])
        update(slot, 5, *[weight * dn[i] for i in range(4)])
    copies = [
        pltpu.make_async_copy(new.at[:, 0:1], s_out.at[:, 0:1], sems.at[0]),
        pltpu.make_async_copy(new.at[:, 1:5], s_out.at[:, 12:16], sems.at[1]),
    ]
    for copy in copies:
        copy.start()
    for copy in copies:
        copy.wait()


def call(body, inputs, shapes, types=None, hbm=(), smem=(), scratch=(), out_hbm=False, alias=None, micros=1, vmem=VMEM_LIMIT):
    def space(i):
        return pltpu.HBM if i in hbm else pltpu.SMEM if i in smem else pltpu.VMEM

    return pl.pallas_call(
        body,
        out_shape=[jax.ShapeDtypeStruct(x, t) for x, t in zip(shapes, types or [F32] * len(shapes))],
        in_specs=[pl.BlockSpec(memory_space=space(i)) for i in range(len(inputs))],
        out_specs=[pl.BlockSpec(memory_space=pltpu.HBM if out_hbm else pltpu.VMEM) for _ in shapes],
        scratch_shapes=list(scratch),
        input_output_aliases=alias or {},
        compiler_params=pltpu.CompilerParams(vmem_limit_bytes=vmem),
        cost_estimate=pl.CostEstimate(flops=0, bytes_accessed=3 * 10**6 * micros, transcendentals=0),
        name=body.__name__,
    )(*inputs)


def swap(value, first):
    lows = range(first, lax.axis_size("depth") - 1, 2)
    return lax.ppermute(value, "depth", [p for i in lows for p in ((i, i + 1), (i + 1, i))])


def neighbours(near, far):
    far = swap(far, 1)
    return swap(near, 0), far


def on_device(velocity, stress, memory, layer_ids, materials, jkd, source_depth):
    c = constants()
    block = (PLANES, AZ, NR)
    tables = [layer_ids, materials, jkd]
    state, far, near, ring_coef = call(
        prepare,
        tables + [stress, memory, velocity, c["dr"]],
        [(COEF + FLAGS + 2, AZ, NR), (UP_COEF + 7, AZ, NR), (UP_COEF + 7, AZ, NR), (len(RING), 8, 256)],
        hbm=range(7),
        scratch=[pltpu.VMEM((UP_COEF + 7, AZ, NR), F32)] * 2
        + [pltpu.SMEM(x.shape, x.dtype) for x in tables]
        + [pltpu.VMEM((n,) + block, F32) for n in (7, 12, 6)]
        + [pltpu.VMEM(c["dr"].shape, BF16), pltpu.SemaphoreType.DMA((7,))],
        vmem=VMEM_FULL,
    )
    near, far = neighbours(near, far)
    staged = [c[n] for n in ("mr", "mz", "dt", "wr", "wz")]
    shapes = [x.shape[1:] if n < 2 else x.shape for n, x in enumerate(staged)]
    *matrices, state, coef, mark = call(
        stage,
        [source_depth] + staged + [state],
        shapes + [(COEF, AZ, NR), (FLAGS + 2, AZ, NR), (8, 256)],
        types=[BF16] * 5 + [F32] * 3,
        hbm=range(1, 7),
        smem=(0,),
        scratch=[pltpu.SemaphoreType.DMA((7,))],
    )
    packed, keep = call(
        launch,
        [stress, state, far, near, coef, mark, c["dr"], c["items"]],
        [(8, 2 * FIELDS_IN, AZ, NR), (12,) + block],
        scratch=[pltpu.VMEM((2 * FIELDS_IN, 8, AZ, NR), F32)],
        micros=4,
    )
    packed = lax.all_to_all(packed, "az", split_axis=0, concat_axis=0, tiled=True)
    (back,) = call(ring, [packed, ring_coef, mark] + matrices, [(8, 2 * FIELDS_OUT, AZ, NR)], micros=3)
    back = lax.all_to_all(back, "az", split_axis=0, concat_axis=0, tiled=True)
    new, mid, far, near = call(
        advance,
        [back, keep, coef],
        [(6,) + block, (6,) + block, (4, AZ, NR), (4, AZ, NR)],
        scratch=[pltpu.VMEM((20, 8, AZ, NR), F32)],
    )
    near, far = neighbours(near, far)
    v_out, s_part, m_out, edge = call(
        settle,
        [back, new, mid, velocity, stress, memory, coef, mark, c["dr"]],
        [(6,) + block, (7,) + block, (12,) + block, (7, 5, AZ, NR)],
        scratch=[pltpu.VMEM((8, 8, AZ, NR), F32)],
        micros=3,
    )
    (s_out,) = call(
        close,
        [s_part, edge, far, near, coef],
        [(7,) + block],
        hbm=(0,),
        scratch=[pltpu.VMEM((7, 5, AZ, NR), F32), pltpu.SemaphoreType.DMA((2,))],
        out_hbm=True,
        alias={0: 0},
    )
    return v_out, s_out, m_out


def solution(mesh):
    field = P(None, "depth", "az", None)
    return jax.shard_map(
        on_device,
        mesh=mesh,
        in_specs=(field, field, field, P("depth", None), P(), P(), P()),
        out_specs=(field, field, field),
        check_vma=False,
    )
```

```python
import functools
import math

import jax
import jax.numpy as jnp
import ml_dtypes
import numpy as np
from jax import lax
from jax.experimental import pallas as pl
from jax.experimental.pallas import tpu as pltpu
from jax.sharding import PartitionSpec as P

NR = 128
NT = 64
RB = 4
PLANES = 16
AZ = 8
GROUP = 16
DT = 0.02
SOURCE = DT * 40.0
R_INNER = 1.0
F32 = jnp.float32
BF16 = jnp.bfloat16
FIELDS_IN = 18
FIELDS_OUT = 14
VMEM_LIMIT = 32 * 2**20
VMEM_FULL = 56 * 2**20
UP_COEF = 52
DN_COEF = 20
SHARED = ("cv", "cf", "cr", "bulk", "couple", "modulus", "shear")
OWN = SHARED + ("fric", "kappa", "omega", "decay0", "decay1", "decay2", "decay3")
FLAGS = len(OWN)
COEF = 12 * PLANES
RING = SHARED + ("fk",)


def gll_basis():
    root_value = math.sqrt(3.0 / 7.0)
    nodes = np.array([-1.0, -root_value, 0.0, root_value, 1.0])
    weights = np.array([0.1, 49.0 / 90.0, 32.0 / 45.0, 49.0 / 90.0, 0.1])
    offsets = nodes[:, None] - nodes[None, :] + np.eye(5)
    factors = np.prod(offsets, axis=1)
    derivative = factors[:, None] / factors[None, :] / offsets
    diagonal = np.sum(1.0 / offsets, axis=1) - 1.0
    derivative = derivative * (1.0 - np.eye(5)) + np.eye(5) * diagonal[:, None]
    return nodes, weights, derivative


NODES, WEIGHTS, DERIV = gll_basis()
ROW = DERIV * np.array([1.0, 2.0, 2.0, 2.0, 1.0])[:, None]


def line_operator(count, first):
    matrix = np.zeros((count + 1, count + 1))
    for e in range(count // 4):
        matrix[4 * e : 4 * e + 5, 4 * e : 4 * e + 5] += ROW
    if first:
        matrix[0] *= 2.0
    else:
        matrix[0, 0] += ROW[4, 4]
    return matrix[:count, :count]


def halves(matrix):
    hi = matrix.astype(np.float32).astype(ml_dtypes.bfloat16)
    lo = (matrix - hi.astype(np.float64)).astype(np.float32).astype(ml_dtypes.bfloat16)
    return np.stack([hi, lo])


def azimuth_operator():
    positions = np.arange(NT)
    offsets = positions[:, None] - positions[None, :]
    modes = np.arange(1, NT // 2)
    phases = 2.0 * np.pi * offsets[:, :, None] * modes / NT
    return -(2.0 / NT) * np.sum(modes * np.sin(phases), axis=2)


@functools.lru_cache(None)
def constants():
    groups = NR // GROUP
    c = {}
    c["dr"] = halves(line_operator(NR, True).T)
    items = np.zeros((8, NR, groups, 16))
    for s in range(8):
        for k in range(groups):
            if GROUP * (k + 1) < NR:
                items[s, GROUP * (k + 1), k, 2 * s] = 1.0
            if k:
                items[s, GROUP * k - 4 : GROUP * k, k, 2 * s + 1] = ROW[4, :4]
    c["items"] = halves(items.reshape(8 * NR, 128))
    azimuth = np.zeros((128, 128))
    azimuth[:NT, :NT] = azimuth_operator()
    small = [np.kron(np.eye(8), line_operator(16, first).T) for first in (False, True)] + [azimuth]
    c["mr"] = np.stack([halves(m) for m in small])
    c["mz"] = np.stack([halves(np.kron(line_operator(16, first).T, np.eye(16))) for first in (False, True)])
    spread = np.zeros((2, 16))
    spread[0, 12:] = ROW[:4, 4]
    spread[1, 0] = 1.0
    wr = np.zeros((2, 8, 16, 4, 8, 16))
    wz = np.zeros((8, 16, 4, 16, 16))
    for f in range(4):
        for side in range(2):
            for j in range(8):
                for order in range(2):
                    wr[order, j, 8 * order + 2 * f + side, f, j] = spread[side]
            for r in range(16):
                wz[2 * f + side, r, f, :, r] = spread[side]
    c["wr"] = np.stack([halves(w) for w in wr.reshape(2, 128, 512)])
    c["wz"] = halves(wz.reshape(128, 1024))
    return c


def roll(x, shift):
    return pltpu.roll(x, shift % x.shape[-1], x.ndim - 1)


def dot(a, b):
    return jnp.dot(a, b, preferred_element_type=F32)


def parts(x):
    hi = x.astype(BF16)
    return hi, (x - hi.astype(F32)).astype(BF16)


def mm(x, hi, lo):
    xh, xl = parts(x)
    return dot(xh, hi) + dot(xl, hi) + dot(xh, lo)


def inverse_radius(group, width):
    lane = lax.broadcasted_iota(jnp.int32, (8, 128 if width == NR else 256), 1) % width
    place = lane % 4
    offset = jnp.zeros(lane.shape, F32)
    for j in range(4):
        offset = jnp.where(place == j, float(R_INNER + 0.5 * (1.0 + NODES[j])), offset)
    return 1.0 / (offset + (lane // 4 + 4 * group).astype(F32))


def own_ids(lids):
    row = lax.broadcasted_iota(jnp.int32, (8, NR), 0)
    fluid = lax.broadcasted_iota(jnp.int32, (8, NR), 1) < 4 * RB
    value = jnp.zeros((8, NR), jnp.int32)
    for e in range(4):
        value = jnp.where(row == 2 + e, jnp.where(fluid, lids[e, 0], lids[e, NR // 4 - 1]), value)
    return value.astype(F32)


def coefficients(ids, tab):
    hits = [ids == float(m) for m in range(8)]
    materials, jkd = tab

    def pick(table, column):
        value = jnp.where(hits[0], table[0, column], 0.0)
        for m in range(1, 8):
            value = jnp.where(hits[m], table[m, column], value)
        return value

    lame, mu, modulus, beta, rho, rho_f, tort, fric = [pick(materials, c) for c in range(8)]
    omega = pick(jkd, 0)
    weights = [pick(jkd, 1 + l) for l in range(4)]
    rates = [pick(jkd, 5 + l) for l in range(4)]
    rho_w = tort * rho_f
    scale = DT / (rho * rho_w - rho_f * rho_f)
    decay = [1.0 / (1.0 + DT * (rate + omega)) for rate in rates]
    gain = sum(a * c for a, c in zip(weights, decay))
    return dict(
        cv=rho_w * scale,
        cf=rho_f * scale,
        cr=rho * scale,
        fric=fric,
        omega=DT * omega,
        weights=weights,
        decay=decay,
        decay0=decay[0],
        decay1=decay[1],
        decay2=decay[2],
        decay3=decay[3],
        kappa=(1.0 + DT * omega) * gain,
        fk=fric * ((1.0 + DT * omega) * gain),
        bulk=DT * (lame + beta * beta * modulus),
        couple=DT * beta * modulus,
        modulus=DT * modulus,
        shear=DT * mu,
    )


def spread_rows(value, first, count, tail=False):
    rows = [jnp.broadcast_to(value[first + e : first + e + 1, :], (8, NR)) for e in range(count + tail)]
    planes = [rows[i // 4] for i in range(4 * count + tail)]
    return jnp.stack(planes)


def combine(row, nodes):
    total = None
    for weight, node in zip(row, nodes):
        term = float(weight) * node
        total = term if total is None else total + term
    return total


def depth_derivative(x, lo, hi, edge, has_below, low=None, high=None):
    count = (x.shape[0] - 1) // 4
    blocks = x[: 4 * count].reshape((count, 4) + x.shape[1:])
    last = [blocks[e + 1, 0] if e + 1 < count else x[4 * count] for e in range(count)]

    def nodes(e):
        return [blocks[e, l] for l in range(4)] + [last[e]]

    out = []
    for e in range(lo, hi + 1):
        upper = combine(ROW[0], nodes(e)) if e < count else high
        lower = combine(ROW[4], nodes(e - 1)) if e > 0 else low
        if e == edge:
            upper = (2.0 - has_below) * upper
            lower = has_below * lower
        out.append(upper + lower)
        if e < hi:
            for i in range(1, 4):
                out.append(combine(ROW[i], nodes(e)))
    return jnp.stack(out)


def below_partial(x):
    return combine(ROW[4, :4], [x[l] for l in range(4)])


def lane_groups():
    return lax.broadcasted_iota(jnp.int32, (8, NR), 1) // GROUP


def exchange_groups(x):
    groups = lane_groups()
    rows = [roll(x[j], GROUP * j) if j else x[j] for j in range(8)]
    for s in (1, 2, 4):
        stay = (groups & s) == 0
        rows = [jnp.where(stay, rows[j], rows[(j + s) % 8]) for j in range(8)]
    return [roll(rows[-k % 8], -GROUP * k) if k else rows[0] for k in range(8)]


def for_each(count, body, unroll=4):
    lax.fori_loop(0, count, lambda i, _: (body(i), 0)[1], 0, unroll=unroll)


def flat(x):
    return x.reshape(-1, NR)


def prepare(
    lids_hbm, mat_hbm, jkd_hbm, s_hbm, dr_hbm, v_hbm, psi_hbm,
    state, far, near, ring_coef,
    up, dn, lids, mat, jkd, s, dr_m, v, psi, sems,
):
    pairs = (
        (lids_hbm, lids), (mat_hbm, mat), (jkd_hbm, jkd), (s_hbm, s), (dr_hbm, dr_m),
        (v_hbm, v), (psi_hbm, psi),
    )
    copies = [pltpu.make_async_copy(a, b, sems.at[i]) for i, (a, b) in enumerate(pairs)]
    for copy in copies:
        copy.start()
    for copy in copies[:3]:
        copy.wait()
    device = lax.axis_index("depth")
    rows = lax.broadcasted_iota(jnp.int32, (8, NR), 0)
    c = coefficients(own_ids(lids), (mat, jkd))
    mine = (rows >= 2) & (rows < 6)
    for n, name in enumerate(OWN):
        state[COEF + n] = jnp.where(mine, c[name], 0.0)
    state[COEF + FLAGS] = jnp.full((8, NR), jnp.where(device > 0, 1.0, 0.0), F32)
    state[COEF + FLAGS + 1] = jnp.full((8, NR), jnp.where(device < lax.axis_size("depth") - 1, 1.0, 0.0), F32)
    for n, name in enumerate(SHARED):
        swapped = pltpu.roll(c[name], 4, 0)
        up[UP_COEF + n] = jnp.where(rows < 2, swapped, 0.0)
        dn[DN_COEF + n] = jnp.where(rows >= 6, swapped, 0.0)
    element = lax.broadcasted_iota(jnp.int32, (8, 256), 1) // 64
    group = lax.axis_index("az")
    ids = jnp.zeros((8, 256), jnp.int32)
    for e in range(4):
        ids = jnp.where(element == e, lids[e, 4 * group], ids)
    rc = coefficients(ids.astype(F32), (mat, jkd))
    for n, name in enumerate(RING):
        ring_coef[n] = rc[name]

    def sp(value):
        return spread_rows(value, 2, 4)

    has_below = jnp.where(device > 0, 1.0, 0.0)
    q = inverse_radius(0, NR)
    cv, cf, cr, fric = [sp(c[n]) for n in ("cv", "cf", "cr", "fric")]
    weights = [sp(w) for w in c["weights"]]
    decayed = [sp(w * d) for w, d in zip(c["weights"], c["decay"])]
    for copy in copies[3:5]:
        copy.wait()
    rr, tt, zz, rt, rz, tz, p = [s[f] for f in range(7)]
    stacked = jnp.concatenate([flat(x) for x in (rr, rt, rz, p)], axis=0)
    y = mm(stacked, dr_m[0], dr_m[1])
    r_rr, r_rt, r_rz, r_p = [y[128 * i : 128 * i + 128].reshape(16, 8, NR) for i in range(4)]
    zero = jnp.zeros((1, 8, NR), F32)
    z_rz, z_tz, z_zz, z_p = [
        depth_derivative(jnp.concatenate([x, zero], axis=0), 0, 4, 0, has_below, float(ROW[4, 4]) * x[0], zero[0])[:16]
        for x in (rz, tz, zz, p)
    ]
    div = [r_rr + z_rz + q * (rr - tt), r_rt + z_tz + 2.0 * q * rt, r_rz + z_zz + q * rz]
    grads = (r_p, None, z_p)
    for copy in copies[5:]:
        copy.wait()
    for i in range(3):
        memory = [psi[3 * l + i] for l in range(4)]
        total = sum(w * m for w, m in zip(weights, memory))
        later = sum(w * (m - v[3 + i]) for w, m in zip(decayed, memory))
        g0, g1 = fric * total, fric * later
        if grads[i] is not None:
            g0, g1 = g0 + grads[i], g1 + grads[i]
        d_v, d_w = cv * div[i], cf * div[i]
        for n, x in enumerate(
            (v[i] + d_v + cf * g0, v[3 + i] - d_w - cr * g0, d_v + cf * g1, d_w + cr * g1)
        ):
            at = 16 * (3 * n + i)
            state[at : at + 16] = x
            if n < 2:
                f = 3 * n + i
                up[4 * f : 4 * f + 4] = x[12:]
                dn[f] = x[0]
                if f < 3 or f == 5:
                    place = min(f, 3)
                    up[40 + place] = below_partial(x[8:12])
                    dn[12 + place] = combine(ROW[0, 1:], [x[1 + l] for l in range(4)])
    q_rt, q_tt, q_tz, q_p = q * rt, q * tt, q * tz, q * p
    u = [cv * q_rt, cv * q_tt + cf * q_p, cv * q_tz, -(cf * q_tz)]
    for i, x in enumerate(u):
        up[44 + i] = below_partial(x[8:12])
        dn[16 + i] = combine(ROW[0, 1:], [x[1 + l] for l in range(4)])
    for i, x in enumerate((rt, tt, tz, p)):
        up[24 + 4 * i : 28 + 4 * i] = x[12:]
    for i, x in enumerate((rt, tt, tz, p, rz, zz)):
        dn[6 + i] = x[0]
    for i, x in enumerate((rz, tz, zz, p)):
        up[48 + i] = below_partial(x[12:])
    dn[DN_COEF + 7 :] = jnp.zeros((UP_COEF - DN_COEF, 8, NR), F32)
    outgoing(up[...], dn[...], near, far)


def is_even():
    return lax.axis_index("depth") % 2 == 0


def outgoing(up, dn, near, far):
    even = is_even()
    near[...] = jnp.where(even, up, dn)
    far[...] = jnp.where(even, dn, up)


def incoming(near, far):
    even = is_even()
    x, y = near[...], far[...]
    return jnp.where(even, y, x), jnp.where(even, x, y)


def stage(src, mr_in, mz_in, wr_in, wz_in, state_in, mr, mz, dt_m, wr, wz, state, coef, mark, sems):
    device = lax.axis_index("depth")
    pairs = (
        (state_in.at[0:COEF], state),
        (state_in.at[COEF:], coef),
        (mr_in.at[jnp.where(lax.axis_index("az") == 0, 1, 0)], mr),
        (mz_in.at[jnp.where(device == 0, 1, 0)], mz),
        (mr_in.at[2], dt_m),
        (wr_in, wr),
        (wz_in, wz),
    )
    copies = [pltpu.make_async_copy(a, b, sems.at[i]) for i, (a, b) in enumerate(pairs)]
    for copy in copies:
        copy.start()
    mark[...] = jnp.full((8, 256), (src[0] - PLANES * device).astype(F32), F32)
    for copy in copies:
        copy.wait()


def launch(s, state, far, near, coef, mark, dr_m, items, pk, keep, hold):
    has_below = coef[FLAGS]
    has_above = coef[FLAGS + 1]
    up, dn = incoming(near, far)
    c = {name: coef[n] for n, name in enumerate(OWN)}
    for n, name in enumerate(SHARED):
        c[name] = c[name] + up[UP_COEF + n] + dn[DN_COEF + n]
    q = inverse_radius(0, NR)
    cv, cf, cr, bulk, couple, modulus, shear = [spread_rows(c[n], 1, 5, True) for n in SHARED]

    def radial(fields):
        stacked = jnp.concatenate([flat(x) for x in fields], axis=0)
        out = mm(stacked, dr_m[0], dr_m[1])
        count = fields[0].shape[0]
        return [out[8 * count * i : 8 * count * (i + 1)].reshape(count, 8, NR) for i in range(len(fields))]

    def added(f, partial, above):
        x = s[f]
        planes = [float(ROW[l, 4]) * x[0] for l in range(4)]
        planes.append(has_below * partial)
        planes += [float(ROW[l, 4]) * above for l in range(4)]
        planes.append(has_above * below_partial(x[12:]))
        return jnp.stack(planes)

    def edges(x):
        return jnp.concatenate([x[:5], x[16:]], axis=0)

    e_cv, e_cf, e_cr = edges(cv), edges(cf), edges(cr)
    m_rz, m_tz, m_zz, m_p = [
        added(f, up[48 + i], dn[n]) for i, (f, n) in enumerate(((4, 10), (5, 8), (2, 11), (6, 9)))
    ]
    to_v = [e_cv * m_rz, e_cv * m_tz, e_cv * m_zz + e_cf * m_p]
    to_w = [e_cf * m_rz, e_cf * m_tz, e_cf * m_zz + e_cr * m_p]

    def inner_planes(n, more):
        x = state[16 * n : 16 * n + 16]
        return [x[:1] + more[4:5], x[1:12], x[12:] + more[5:9]]

    def whole(f, more):
        ends = [up[4 * f : 4 * f + 4] + more[:4]], [dn[f : f + 1] + more[9:]]
        return jnp.concatenate(ends[0] + inner_planes(f, more) + ends[1], axis=0)

    v1 = [whole(i, to_v[i]) for i in range(3)]
    w1 = [whole(3 + i, -to_w[i]) for i in range(3)]
    q_rt, q_tt, q_tz, q_p = [
        q * jnp.concatenate([up[24 + 4 * i : 28 + 4 * i], s[f], dn[6 + i : 7 + i]], axis=0)
        for i, f in enumerate((3, 1, 5, 6))
    ]
    u = [cv * q_rt, cv * q_tt + cf * q_p, cv * q_tz]
    uw = [-(cf * q_rt), -(cf * q_tt + cr * q_p), -(cf * q_tz)]

    def pack(f, planes):
        hold[2 * f] = planes[:8]
        hold[2 * f + 1] = planes[8:]

    for f, x in enumerate((3, 1, 5, 6)):
        pack(f, s[x])
    fk = spread_rows(c["fric"] * c["kappa"], 2, 4)
    o_cf, o_cr = cf[4:20], cr[4:20]
    for i in range(3):
        v_i, w_i = v1[i][4:20], w1[i][4:20]
        a = jnp.concatenate(inner_planes(6 + i, to_v[i]), axis=0) + o_cf * (fk * w_i)
        b = jnp.concatenate(inner_planes(9 + i, to_w[i]), axis=0) + o_cr * (fk * w_i)
        pack(4 + i, v_i)
        pack(9 + i, a)
        keep[i] = v_i
        keep[3 + i] = w_i
        keep[6 + i] = a
        keep[9 + i] = b
        if i == 1:
            pack(7, w_i)
            pack(12, b)

    mask21 = jnp.where(lax.broadcasted_iota(jnp.int32, (21, 8, NR), 0) < 20, 1.0, has_above)
    plane21 = lax.broadcasted_iota(jnp.int32, (21, 8, NR), 0) - 4
    lane21 = lax.broadcasted_iota(jnp.int32, (21, 8, NR), 2)
    source = jnp.where((plane21.astype(F32) == mark[:, :NR]) & (lane21 < 4 * RB), SOURCE, 0.0)

    def stresses(v, w, extra):
        at = 12 if extra is None else 16
        low = 40 if extra is None else 44
        vr, vt, wr = v[0], v[1], w[0]
        r_r, r_t, r_z, r_w = radial([vr, vt, v[2], wr])
        z_r, z_t, z_z, z_w = [
            depth_derivative(
                x,
                0,
                5,
                1,
                has_below,
                up[low + n] + float(ROW[4, 4]) * x[0],
                dn[at + n] + float(ROW[0, 0]) * x[20],
            )
            for n, x in enumerate((v[0], v[1], v[2], w[2]))
        ]
        e_tt, g_rt, g_tz, div_w = q * vr, r_t - q * vt, z_t, r_w + q * wr + z_w
        if extra is not None:
            e_tt, g_rt, g_tz, div_w = e_tt + extra[1], g_rt + extra[0], g_tz + extra[2], div_w + extra[3]
        div_v = r_r + e_tt + z_z
        total = bulk * div_v + couple * div_w
        return dict(
            rr=mask21 * (total + 2.0 * shear * r_r),
            zz=mask21 * (total + 2.0 * shear * z_z),
            rt=mask21 * (shear * g_rt),
            rz=mask21 * (shear * (z_r + r_z)),
            tz=mask21 * (shear * g_tz),
            p=mask21 * (-(couple * div_v + modulus * div_w) + (source if extra is None else 0.0)),
            w=div_w,
        )

    x0 = stresses(v1, w1, None)
    pack(8, x0["w"][4:20])
    x1 = stresses(u, uw, [q * v1[0], q * v1[1], q * v1[2], q * w1[1]])
    e2, dw2 = q * u[1], q * uw[1]
    total2 = bulk * e2 + couple * dw2
    x2 = dict(
        rr=mask21 * total2,
        zz=mask21 * total2,
        rt=mask21 * (shear * (q * u[0])),
        tz=mask21 * (shear * (q * u[2])),
        p=mask21 * (-(couple * e2 + modulus * dw2)),
    )

    def radius_items(fields):
        slots = [i for i, x in enumerate(fields) if x is not None]
        stacked = jnp.concatenate([flat(fields[i]) for i in slots], axis=1)
        hi, lo = [jnp.concatenate([items[h, NR * i : NR * i + NR] for i in slots], axis=0) for h in range(2)]
        return mm(stacked, hi, lo).reshape(-1, 8, NR)

    def depth_items(fields):
        out = []
        for x in fields:
            if x is None:
                out += [jnp.zeros((8, NR), F32)] * 2
            else:
                out.append(x[20])
                out.append(has_below * below_partial(x[:4]))
        return jnp.stack(out)

    velocity_r = [v1[0], v1[1], v1[2], None, u[0], u[1], u[2], uw[0]]
    pack(13, radius_items([None if x is None else x[4:20] for x in velocity_r]))
    names_r = ("rr", "rt", "rz", "p")
    pack(14, radius_items([x[n][4:20] for x in (x0, x1) for n in names_r]))
    pack(15, depth_items([v1[0], v1[1], v1[2], None, u[0], u[1], u[2], uw[2]]))
    names_z = ("rz", "tz", "zz", "p")
    pack(16, depth_items([x[n] for x in (x0, x1) for n in names_z]))
    second = [x2[n][4 + 8 * h : 12 + 8 * h] if n in x2 else None for h in range(2) for n in names_r]
    pack(17, jnp.concatenate([radius_items(second), depth_items([x2.get(n) for n in names_z])], axis=0))

    def send(i):
        chunks = exchange_groups(hold[i])
        for k in range(8):
            pk[k, i] = chunks[k]

    for_each(2 * FIELDS_IN, send, unroll=9)


def ring(recv, coef, mark, mr, mz, dt_m, wr, wz, out):
    group = lax.axis_index("az")
    c = {name: coef[n] for n, name in enumerate(RING)}
    q = inverse_radius(group, GROUP)

    def field(f):
        return jnp.concatenate([recv[:, 2 * f], recv[:, 2 * f + 1]], axis=-1)

    dt_h, dt_l = dt_m[0, :NT, :NT], dt_m[1, :NT, :NT]

    def az(fields):
        x = jnp.concatenate([y.reshape(NT, -1) for y in fields], axis=1)
        xh, xl = parts(x)
        y = dot(dt_h, xh) + dot(dt_h, xl) + dot(dt_l, xh)
        res, at = [], 0
        for f in fields:
            n = f.shape[-1]
            res.append(y[:, at : at + n].reshape(f.shape))
            at += n
        return res

    def by_half(x):
        x = x.reshape(NT, 256)
        return [x[:, :128], x[:, 128:]]

    mr_h, mr_l = mr[0], mr[1]
    mz_h, mz_l = mz[0], mz[1]

    def radial(fields, halo):
        stacked = jnp.concatenate([h for f in fields for h in by_half(f)], axis=0)
        y = mm(stacked, mr_h, mr_l)
        res = []
        for i in range(len(fields)):
            halves_ = [
                y[128 * i + 64 * g : 128 * i + 64 * g + 64] + halo[64 * g : 64 * g + 64, 128 * i : 128 * i + 128]
                for g in range(2)
            ]
            res.append(jnp.concatenate(halves_, axis=1).reshape(8, 8, 256))
        return res

    def depth(fields, halo):
        stacked = jnp.concatenate([f.reshape(NT, 256) for f in fields], axis=0)
        y = mm(stacked, mz_h, mz_l)
        return [
            (y[64 * i : 64 * i + 64] + halo[:, 256 * i : 256 * i + 256]).reshape(8, 8, 256)
            for i in range(len(fields))
        ]

    rt, tt, tz, p = [field(f) for f in range(4)]
    pr2, pr3 = field(13), field(14)
    pd2 = [recv[:, 30], recv[:, 31]]
    pd3 = [recv[:, 32], recv[:, 33]]
    px = field(17)
    s_rt, s_tt, s_tz, s_p, d_pr2, d_pr3, d_pd2, d_pd3, d_px = az([rt, tt, tz, p, pr2, pr3, pd2[1], pd3[1], px])
    (dd_px,) = az([d_px])
    wr0, wr1 = (wr[0, 0], wr[0, 1]), (wr[1, 0], wr[1, 1])

    def stack_halves(x):
        return jnp.concatenate(by_half(x), axis=0)

    def radius_halo(zero, one):
        return mm(stack_halves(zero), *wr0) + mm(stack_halves(one), *wr1)

    hr2 = radius_halo(pr2, d_pr2)
    hz2 = mm((pd2[0] + d_pd2).reshape(NT, 128), wz[0], wz[1])
    half = dd_px.reshape(NT, 256)[:, :128]
    hr3 = radius_halo(pr3, d_pr3) + jnp.concatenate([mm(half, *wr0), mm(half, *wr1)], axis=0)
    hz3 = mm((pd3[0] + d_pd3).reshape(NT, 128) + dd_px.reshape(NT, 256)[:, 128:], wz[0], wz[1])

    cv, cf, cr = c["cv"], c["cf"], c["cr"]
    q_rt, q_tt, q_tz, q_p = q * s_rt, q * s_tt, q * s_tz, q * s_p
    dw = [-(cf * q_rt), -(cf * q_tt + cr * q_p), -(cf * q_tz)]
    v1 = [
        field(4) + cv * q_rt,
        field(5) + cv * q_tt + cf * q_p,
        field(6) + cv * q_tz,
    ]
    w1_t = field(7) + dw[1]
    r_r, r_t, r_z, r_w = radial([v1[0], v1[1], v1[2], dw[0]], hr2)
    z_r, z_t, z_z, z_w = depth([v1[0], v1[1], v1[2], dw[2]], hz2)
    a_r, a_t, a_z, a_w = az([v1[0], v1[1], v1[2], w1_t])
    e_tt = q * (v1[0] + a_t)
    div_v = r_r + e_tt + z_z
    div_w = field(8) + r_w + q * (dw[0] + a_w) + z_w
    total = c["bulk"] * div_v + c["couple"] * div_w
    shear = c["shear"]
    lanes = lax.broadcasted_iota(jnp.int32, (8, 256), 1) // GROUP
    source = jnp.where(lanes.astype(F32) == mark[...], jnp.where(group == 0, SOURCE, 0.0), 0.0)
    n_rr = total + 2.0 * shear * r_r
    n_tt = total + 2.0 * shear * e_tt
    n_zz = total + 2.0 * shear * z_z
    n_rt = shear * (q * (a_r - v1[1]) + r_t)
    n_rz = shear * (z_r + r_z)
    n_tz = shear * (z_t + q * a_z)
    n_p = source - (c["couple"] * div_v + c["modulus"] * div_w)

    r_rr, r_rt, r_rz, r_p = radial([n_rr, n_rt, n_rz, n_p], hr3)
    z_rz, z_tz, z_zz, z_p = depth([n_rz, n_tz, n_zz, n_p], hz3)
    a_rt, a_tt, a_tz, a_p = az([n_rt, n_tt, n_tz, n_p])
    d_r = q_rt + r_rr + z_rz + q * (a_rt + n_rr - n_tt)
    d_t = q_tt + r_rt + z_tz + q * (a_tt + 2.0 * n_rt)
    d_z = q_tz + r_rz + z_zz + q * (a_tz + n_rz)
    fk = c["fk"]
    g_r = r_p + fk * dw[0]
    g_t = q_p + q * a_p + fk * dw[1]
    g_z = z_p + fk * dw[2]
    sums = [
        2.0 * v1[0] + field(9) + cv * d_r + cf * g_r,
        2.0 * v1[1] + field(10) + cv * d_t + cf * g_t,
        2.0 * v1[2] + field(11) + cv * d_z + cf * g_z,
        2.0 * w1_t - field(12) - cf * d_t - cr * g_t,
    ]
    results = [s_rt, s_tt, s_tz, s_p, d_r, d_t, d_z, g_r, g_t, g_z] + az(sums)
    for f, x in enumerate(results):
        out[:, 2 * f] = x[:, :, :128]
        out[:, 2 * f + 1] = x[:, :, 128:]


def unpack(recv, hold, first, count):
    def receive(i):
        rows = exchange_groups([recv[k, 2 * first + i] for k in range(8)])
        for j in range(8):
            hold[i, j] = rows[j]

    for_each(2 * count, receive)
    return lambda f: jnp.concatenate([hold[2 * (f - first)], hold[2 * (f - first) + 1]], axis=0)


def advance(recv, keep, coef, new, mid, far, near, hold):
    up, dn = [], []
    field = unpack(recv, hold, 0, 10)
    c = {name: coef[n] for n, name in enumerate(OWN)}
    q = inverse_radius(0, NR)
    cv, cf, cr = [spread_rows(c[n], 2, 4) for n in ("cv", "cf", "cr")]
    q_rt, q_tt, q_tz, q_p = [q * field(f) for f in range(4)]
    dv = [cv * q_rt, cv * q_tt + cf * q_p, cv * q_tz]
    dw = [-(cf * q_rt), -(cf * q_tt + cr * q_p), -(cf * q_tz)]
    for i in range(3):
        d, g = field(4 + i), field(7 + i)
        v1 = keep[i] + dv[i]
        w1 = keep[3 + i] + dw[i]
        v2 = v1 + keep[6 + i] + cv * d + cf * g
        w2 = w1 - keep[9 + i] - cf * d - cr * g
        new[i] = v2
        new[3 + i] = w2
        mid[i] = v1
        mid[3 + i] = w1
        x = v1 + v2
        up.append(below_partial(x[12:]))
        dn.append(x[0])
        if i == 2:
            x = w1 + w2
            up.append(below_partial(x[12:]))
            dn.append(x[0])
    outgoing(jnp.stack(up), jnp.stack(dn), near, far)


def settle(recv, v2, mid, v, s, psi, coef, mark, dr_m, v_hbm, s_hbm, m_hbm, edge, hold, s_out, m_out, sems):
    copies = [
        pltpu.make_async_copy(a, b, sems.at[i])
        for i, (a, b) in enumerate(((v2, v_hbm), (m_out, m_hbm), (s_out, s_hbm)))
    ]
    copies[0].start()
    field = unpack(recv, hold, 10, 4)
    has_below = coef[FLAGS]
    c = {name: coef[n] for n, name in enumerate(OWN)}
    q = inverse_radius(0, NR)

    def sp(value):
        return spread_rows(value, 2, 4)

    omega = sp(c["omega"])
    decay = [sp(c[f"decay{l}"]) for l in range(4)]
    for i in range(3):
        w1, w2 = mid[3 + i], v2[3 + i]
        first = w1 - v[3 + i] + omega * w1
        second = w2 - w1 + omega * w2
        for l in range(4):
            m_out[3 * l + i] = decay[l] * (decay[l] * (psi[3 * l + i] + first) + second)
    copies[1].start()
    sums = [mid[i] + v2[i] for i in range(6)]
    zero = jnp.zeros((1, 8, NR), F32)
    z_r, z_t, z_z, z_w = [
        depth_derivative(jnp.concatenate([x, zero], axis=0), 0, 4, 0, has_below, float(ROW[4, 4]) * x[0], zero[0])[:16]
        for x in (sums[0], sums[1], sums[2], sums[5])
    ]
    stacked = jnp.concatenate([flat(x) for x in sums[:4]], axis=0)
    y = mm(stacked, dr_m[0], dr_m[1])
    r_r, r_t, r_z, r_w = [y[128 * i : 128 * i + 128].reshape(16, 8, NR) for i in range(4)]
    a_r, a_t, a_z, a_w = [field(10 + i) for i in range(4)]
    e_tt = q * (sums[0] + a_t)
    div_v = r_r + e_tt + z_z
    div_w = r_w + q * (sums[3] + a_w) + z_w
    couple, shear = sp(c["couple"]), sp(c["shear"])
    total = sp(c["bulk"]) * div_v + couple * div_w
    plane = lax.broadcasted_iota(jnp.int32, (16, 8, NR), 0)
    lane = lax.broadcasted_iota(jnp.int32, (16, 8, NR), 2)
    source = jnp.where((plane.astype(F32) == mark[:, :NR]) & (lane < 4 * RB), SOURCE * (1.0 + math.cos(0.9)), 0.0)
    updates = [
        total + 2.0 * shear * r_r,
        total + 2.0 * shear * e_tt,
        total + 2.0 * shear * z_z,
        shear * (q * (a_r - sums[1]) + r_t),
        shear * (z_r + r_z),
        shear * (z_t + q * a_z),
        source - (couple * div_v + sp(c["modulus"]) * div_w),
    ]
    for f, x in enumerate(updates):
        x = s[f] + x
        s_out[f] = x
        edge[f, 0] = x[0]
        edge[f, 1:] = x[12:]
    copies[2].start()
    for copy in copies:
        copy.wait()


def close(s_in, edge, far, near, coef, s_out, new, sems):
    up, dn = incoming(near, far)
    has_below = coef[FLAGS]
    c = {name: coef[n] for n, name in enumerate(OWN)}

    def update(slot, row, z_r, z_t, z_z, z_w):
        def at(name):
            return jnp.broadcast_to(c[name][row : row + 1, :], (8, NR))

        bulk, couple, modulus, shear = at("bulk"), at("couple"), at("modulus"), at("shear")
        total = bulk * z_z + couple * z_w
        new[0, slot] = edge[0, slot] + total
        new[1, slot] = edge[1, slot] + total
        new[2, slot] = edge[2, slot] + total + 2.0 * shear * z_z
        new[3, slot] = edge[3, slot]
        new[4, slot] = edge[4, slot] + shear * z_r
        new[5, slot] = edge[5, slot] + shear * z_t
        new[6, slot] = edge[6, slot] - (couple * z_z + modulus * z_w)

    update(0, 2, *[has_below * up[i] for i in range(4)])
    for slot in range(1, 5):
        weight = float(ROW[slot - 1, 4])
        update(slot, 5, *[weight * dn[i] for i in range(4)])
    copies = [
        pltpu.make_async_copy(new.at[:, 0:1], s_out.at[:, 0:1], sems.at[0]),
        pltpu.make_async_copy(new.at[:, 1:5], s_out.at[:, 12:16], sems.at[1]),
    ]
    for copy in copies:
        copy.start()
    for copy in copies:
        copy.wait()


def call(body, inputs, shapes, types=None, hbm=(), smem=(), scratch=(), out_hbm=(), alias=None, micros=1, vmem=VMEM_LIMIT):
    def space(i):
        return pltpu.HBM if i in hbm else pltpu.SMEM if i in smem else pltpu.VMEM

    return pl.pallas_call(
        body,
        out_shape=[jax.ShapeDtypeStruct(x, t) for x, t in zip(shapes, types or [F32] * len(shapes))],
        in_specs=[pl.BlockSpec(memory_space=space(i)) for i in range(len(inputs))],
        out_specs=[pl.BlockSpec(memory_space=pltpu.HBM if i in out_hbm else pltpu.VMEM) for i in range(len(shapes))],
        scratch_shapes=list(scratch),
        input_output_aliases=alias or {},
        compiler_params=pltpu.CompilerParams(vmem_limit_bytes=vmem),
        cost_estimate=pl.CostEstimate(flops=0, bytes_accessed=3 * 10**6 * micros, transcendentals=0),
        name=body.__name__,
    )(*inputs)


def swap(value, first):
    lows = range(first, lax.axis_size("depth") - 1, 2)
    return lax.ppermute(value, "depth", [p for i in lows for p in ((i, i + 1), (i + 1, i))])


def neighbours(near, far):
    far = swap(far, 1)
    return swap(near, 0), far


def on_device(velocity, stress, memory, layer_ids, materials, jkd, source_depth):
    c = constants()
    block = (PLANES, AZ, NR)
    tables = [layer_ids, materials, jkd]
    state, far, near, ring_coef = call(
        prepare,
        tables + [stress, c["dr"], velocity, memory],
        [(COEF + FLAGS + 2, AZ, NR), (UP_COEF + 7, AZ, NR), (UP_COEF + 7, AZ, NR), (len(RING), 8, 256)],
        hbm=range(7),
        scratch=[pltpu.VMEM((UP_COEF + 7, AZ, NR), F32)] * 2
        + [pltpu.SMEM(x.shape, x.dtype) for x in tables]
        + [pltpu.VMEM((7,) + block, F32), pltpu.VMEM(c["dr"].shape, BF16)]
        + [pltpu.VMEM((n,) + block, F32) for n in (6, 12)]
        + [pltpu.SemaphoreType.DMA((7,))],
        vmem=VMEM_FULL,
    )
    near, far = neighbours(near, far)
    staged = [c[n] for n in ("mr", "mz", "wr", "wz")]
    shapes = [c[n].shape[1:] for n in ("mr", "mz", "mr")] + [c["wr"].shape, c["wz"].shape]
    *matrices, state, coef, mark = call(
        stage,
        [source_depth] + staged + [state],
        shapes + [(COEF, AZ, NR), (FLAGS + 2, AZ, NR), (8, 256)],
        types=[BF16] * 5 + [F32] * 3,
        hbm=range(1, 6),
        smem=(0,),
        scratch=[pltpu.SemaphoreType.DMA((7,))],
    )
    packed, keep = call(
        launch,
        [stress, state, far, near, coef, mark, c["dr"], c["items"]],
        [(8, 2 * FIELDS_IN, AZ, NR), (12,) + block],
        scratch=[pltpu.VMEM((2 * FIELDS_IN, 8, AZ, NR), F32)],
        micros=4,
    )
    packed = lax.all_to_all(packed, "az", split_axis=0, concat_axis=0, tiled=True)
    (back,) = call(ring, [packed, ring_coef, mark] + matrices, [(8, 2 * FIELDS_OUT, AZ, NR)], micros=3)
    back = lax.all_to_all(back, "az", split_axis=0, concat_axis=0, tiled=True)
    new, mid, far, near = call(
        advance,
        [back, keep, coef],
        [(6,) + block, (6,) + block, (4, AZ, NR), (4, AZ, NR)],
        scratch=[pltpu.VMEM((20, 8, AZ, NR), F32)],
    )
    near, far = neighbours(near, far)
    v_out, s_part, m_out, edge = call(
        settle,
        [back, new, mid, velocity, stress, memory, coef, mark, c["dr"]],
        [(6,) + block, (7,) + block, (12,) + block, (7, 5, AZ, NR)],
        scratch=[pltpu.VMEM((8, 8, AZ, NR), F32)]
        + [pltpu.VMEM((n,) + block, F32) for n in (7, 12)]
        + [pltpu.SemaphoreType.DMA((3,))],
        out_hbm=range(3),
        micros=3,
    )
    (s_out,) = call(
        close,
        [s_part, edge, far, near, coef],
        [(7,) + block],
        hbm=(0,),
        scratch=[pltpu.VMEM((7, 5, AZ, NR), F32), pltpu.SemaphoreType.DMA((2,))],
        out_hbm=(0,),
        alias={0: 0},
    )
    return v_out, s_out, m_out


def solution(mesh):
    field = P(None, "depth", "az", None)
    return jax.shard_map(
        on_device,
        mesh=mesh,
        in_specs=(field, field, field, P("depth", None), P(), P(), P()),
        out_specs=(field, field, field),
        check_vma=False,
    )
```

```python
import functools
import math

import jax
import jax.numpy as jnp
import ml_dtypes
import numpy as np
from jax import lax
from jax.experimental import pallas as pl
from jax.experimental.pallas import tpu as pltpu
from jax.sharding import PartitionSpec as P

NR = 128
NT = 64
RB = 4
PLANES = 16
AZ = 8
GROUP = 16
DT = 0.02
SOURCE = DT * 40.0
R_INNER = 1.0
F32 = jnp.float32
BF16 = jnp.bfloat16
FIELDS_IN = 18
FIELDS_OUT = 14
VMEM_LIMIT = 32 * 2**20
VMEM_FULL = 56 * 2**20
UP_COEF = 52
DN_COEF = 20
SHARED = ("cv", "cf", "cr", "bulk", "couple", "modulus", "shear")
OWN = SHARED + ("fric", "kappa", "omega", "decay0", "decay1", "decay2", "decay3")
FLAGS = len(OWN)
COEF = 12 * PLANES
RING = SHARED + ("fk",)


def gll_basis():
    root_value = math.sqrt(3.0 / 7.0)
    nodes = np.array([-1.0, -root_value, 0.0, root_value, 1.0])
    weights = np.array([0.1, 49.0 / 90.0, 32.0 / 45.0, 49.0 / 90.0, 0.1])
    offsets = nodes[:, None] - nodes[None, :] + np.eye(5)
    factors = np.prod(offsets, axis=1)
    derivative = factors[:, None] / factors[None, :] / offsets
    diagonal = np.sum(1.0 / offsets, axis=1) - 1.0
    derivative = derivative * (1.0 - np.eye(5)) + np.eye(5) * diagonal[:, None]
    return nodes, weights, derivative


NODES, WEIGHTS, DERIV = gll_basis()
ROW = DERIV * np.array([1.0, 2.0, 2.0, 2.0, 1.0])[:, None]


def line_operator(count, first):
    matrix = np.zeros((count + 1, count + 1))
    for e in range(count // 4):
        matrix[4 * e : 4 * e + 5, 4 * e : 4 * e + 5] += ROW
    if first:
        matrix[0] *= 2.0
    else:
        matrix[0, 0] += ROW[4, 4]
    return matrix[:count, :count]


def halves(matrix):
    hi = matrix.astype(np.float32).astype(ml_dtypes.bfloat16)
    lo = (matrix - hi.astype(np.float64)).astype(np.float32).astype(ml_dtypes.bfloat16)
    return np.stack([hi, lo])


def azimuth_operator():
    positions = np.arange(NT)
    offsets = positions[:, None] - positions[None, :]
    modes = np.arange(1, NT // 2)
    phases = 2.0 * np.pi * offsets[:, :, None] * modes / NT
    return -(2.0 / NT) * np.sum(modes * np.sin(phases), axis=2)


@functools.lru_cache(None)
def constants():
    groups = NR // GROUP
    c = {}
    c["dr"] = halves(line_operator(NR, True).T)
    items = np.zeros((8, NR, groups, 16))
    for s in range(8):
        for k in range(groups):
            if GROUP * (k + 1) < NR:
                items[s, GROUP * (k + 1), k, 2 * s] = 1.0
            if k:
                items[s, GROUP * k - 4 : GROUP * k, k, 2 * s + 1] = ROW[4, :4]
    c["items"] = halves(items.reshape(8 * NR, 128))
    azimuth = np.zeros((128, 128))
    azimuth[:NT, :NT] = azimuth_operator()
    small = [np.kron(np.eye(8), line_operator(16, first).T) for first in (False, True)] + [azimuth]
    c["mr"] = np.stack([halves(m) for m in small])
    c["mz"] = np.stack([halves(np.kron(line_operator(16, first).T, np.eye(16))) for first in (False, True)])
    spread = np.zeros((2, 16))
    spread[0, 12:] = ROW[:4, 4]
    spread[1, 0] = 1.0
    wr = np.zeros((2, 8, 16, 4, 8, 16))
    wz = np.zeros((8, 16, 4, 16, 16))
    for f in range(4):
        for side in range(2):
            for j in range(8):
                for order in range(2):
                    wr[order, j, 8 * order + 2 * f + side, f, j] = spread[side]
            for r in range(16):
                wz[2 * f + side, r, f, :, r] = spread[side]
    c["wr"] = np.stack([halves(w) for w in wr.reshape(2, 128, 512)])
    c["wz"] = halves(wz.reshape(128, 1024))
    return c


def roll(x, shift):
    return pltpu.roll(x, shift % x.shape[-1], x.ndim - 1)


def dot(a, b):
    return jnp.dot(a, b, preferred_element_type=F32)


def parts(x):
    hi = x.astype(BF16)
    return hi, (x - hi.astype(F32)).astype(BF16)


def mm(x, hi, lo):
    xh, xl = parts(x)
    return dot(xh, hi) + dot(xl, hi) + dot(xh, lo)


def inverse_radius(group, width):
    lane = lax.broadcasted_iota(jnp.int32, (8, 128 if width == NR else 256), 1) % width
    place = lane % 4
    offset = jnp.zeros(lane.shape, F32)
    for j in range(4):
        offset = jnp.where(place == j, float(R_INNER + 0.5 * (1.0 + NODES[j])), offset)
    return 1.0 / (offset + (lane // 4 + 4 * group).astype(F32))


def own_ids(lids):
    row = lax.broadcasted_iota(jnp.int32, (8, NR), 0)
    fluid = lax.broadcasted_iota(jnp.int32, (8, NR), 1) < 4 * RB
    value = jnp.zeros((8, NR), jnp.int32)
    for e in range(4):
        value = jnp.where(row == 2 + e, jnp.where(fluid, lids[e, 0], lids[e, NR // 4 - 1]), value)
    return value.astype(F32)


def coefficients(ids, tab):
    hits = [ids == float(m) for m in range(8)]
    materials, jkd = tab

    def pick(table, column):
        value = jnp.where(hits[0], table[0, column], 0.0)
        for m in range(1, 8):
            value = jnp.where(hits[m], table[m, column], value)
        return value

    lame, mu, modulus, beta, rho, rho_f, tort, fric = [pick(materials, c) for c in range(8)]
    omega = pick(jkd, 0)
    weights = [pick(jkd, 1 + l) for l in range(4)]
    rates = [pick(jkd, 5 + l) for l in range(4)]
    rho_w = tort * rho_f
    scale = DT / (rho * rho_w - rho_f * rho_f)
    decay = [1.0 / (1.0 + DT * (rate + omega)) for rate in rates]
    gain = sum(a * c for a, c in zip(weights, decay))
    return dict(
        cv=rho_w * scale,
        cf=rho_f * scale,
        cr=rho * scale,
        fric=fric,
        omega=DT * omega,
        weights=weights,
        decay=decay,
        decay0=decay[0],
        decay1=decay[1],
        decay2=decay[2],
        decay3=decay[3],
        kappa=(1.0 + DT * omega) * gain,
        fk=fric * ((1.0 + DT * omega) * gain),
        bulk=DT * (lame + beta * beta * modulus),
        couple=DT * beta * modulus,
        modulus=DT * modulus,
        shear=DT * mu,
    )


def spread_rows(value, first, count, tail=False):
    rows = [jnp.broadcast_to(value[first + e : first + e + 1, :], (8, NR)) for e in range(count + tail)]
    planes = [rows[i // 4] for i in range(4 * count + tail)]
    return jnp.stack(planes)


def combine(row, nodes):
    total = None
    for weight, node in zip(row, nodes):
        term = float(weight) * node
        total = term if total is None else total + term
    return total


def depth_derivative(x, lo, hi, edge, has_below, low=None, high=None):
    count = (x.shape[0] - 1) // 4
    blocks = x[: 4 * count].reshape((count, 4) + x.shape[1:])
    last = [blocks[e + 1, 0] if e + 1 < count else x[4 * count] for e in range(count)]

    def nodes(e):
        return [blocks[e, l] for l in range(4)] + [last[e]]

    out = []
    for e in range(lo, hi + 1):
        upper = combine(ROW[0], nodes(e)) if e < count else high
        lower = combine(ROW[4], nodes(e - 1)) if e > 0 else low
        if e == edge:
            upper = (2.0 - has_below) * upper
            lower = has_below * lower
        out.append(upper + lower)
        if e < hi:
            for i in range(1, 4):
                out.append(combine(ROW[i], nodes(e)))
    return jnp.stack(out)


def below_partial(x):
    return combine(ROW[4, :4], [x[l] for l in range(4)])


def lane_groups():
    return lax.broadcasted_iota(jnp.int32, (8, NR), 1) // GROUP


def exchange_groups(x):
    groups = lane_groups()
    rows = [roll(x[j], GROUP * j) if j else x[j] for j in range(8)]
    for s in (1, 2, 4):
        stay = (groups & s) == 0
        rows = [jnp.where(stay, rows[j], rows[(j + s) % 8]) for j in range(8)]
    return [roll(rows[-k % 8], -GROUP * k) if k else rows[0] for k in range(8)]


def for_each(count, body, unroll=4):
    lax.fori_loop(0, count, lambda i, _: (body(i), 0)[1], 0, unroll=unroll)


def flat(x):
    return x.reshape(-1, NR)


def prepare(
    lids_hbm, mat_hbm, jkd_hbm, s_hbm, dr_hbm, v_hbm, psi_hbm,
    state, far, near, ring_coef,
    up, dn, lids, mat, jkd, s, dr_m, v, psi, sems,
):
    pairs = (
        (lids_hbm, lids), (mat_hbm, mat), (jkd_hbm, jkd), (s_hbm, s), (dr_hbm, dr_m),
        (v_hbm, v), (psi_hbm, psi),
    )
    copies = [pltpu.make_async_copy(a, b, sems.at[i]) for i, (a, b) in enumerate(pairs)]
    for copy in copies:
        copy.start()
    for copy in copies[:3]:
        copy.wait()
    device = lax.axis_index("depth")
    rows = lax.broadcasted_iota(jnp.int32, (8, NR), 0)
    c = coefficients(own_ids(lids), (mat, jkd))
    mine = (rows >= 2) & (rows < 6)
    for n, name in enumerate(OWN):
        state[COEF + n] = jnp.where(mine, c[name], 0.0)
    state[COEF + FLAGS] = jnp.full((8, NR), jnp.where(device > 0, 1.0, 0.0), F32)
    state[COEF + FLAGS + 1] = jnp.full((8, NR), jnp.where(device < lax.axis_size("depth") - 1, 1.0, 0.0), F32)
    for n, name in enumerate(SHARED):
        swapped = pltpu.roll(c[name], 4, 0)
        up[UP_COEF + n] = jnp.where(rows < 2, swapped, 0.0)
        dn[DN_COEF + n] = jnp.where(rows >= 6, swapped, 0.0)
    element = lax.broadcasted_iota(jnp.int32, (8, 256), 1) // 64
    group = lax.axis_index("az")
    ids = jnp.zeros((8, 256), jnp.int32)
    for e in range(4):
        ids = jnp.where(element == e, lids[e, 4 * group], ids)
    rc = coefficients(ids.astype(F32), (mat, jkd))
    for n, name in enumerate(RING):
        ring_coef[n] = rc[name]

    def sp(value):
        return spread_rows(value, 2, 4)

    has_below = jnp.where(device > 0, 1.0, 0.0)
    q = inverse_radius(0, NR)
    cv, cf, cr, fric = [sp(c[n]) for n in ("cv", "cf", "cr", "fric")]
    weights = [sp(w) for w in c["weights"]]
    decayed = [sp(w * d) for w, d in zip(c["weights"], c["decay"])]
    for copy in copies[3:5]:
        copy.wait()
    rr, tt, zz, rt, rz, tz, p = [s[f] for f in range(7)]
    stacked = jnp.concatenate([flat(x) for x in (rr, rt, rz, p)], axis=0)
    y = mm(stacked, dr_m[0], dr_m[1])
    r_rr, r_rt, r_rz, r_p = [y[128 * i : 128 * i + 128].reshape(16, 8, NR) for i in range(4)]
    zero = jnp.zeros((1, 8, NR), F32)
    z_rz, z_tz, z_zz, z_p = [
        depth_derivative(jnp.concatenate([x, zero], axis=0), 0, 4, 0, has_below, float(ROW[4, 4]) * x[0], zero[0])[:16]
        for x in (rz, tz, zz, p)
    ]
    div = [r_rr + z_rz + q * (rr - tt), r_rt + z_tz + 2.0 * q * rt, r_rz + z_zz + q * rz]
    grads = (r_p, None, z_p)
    for copy in copies[5:]:
        copy.wait()
    for i in range(3):
        memory = [psi[3 * l + i] for l in range(4)]
        total = sum(w * m for w, m in zip(weights, memory))
        later = sum(w * (m - v[3 + i]) for w, m in zip(decayed, memory))
        g0, g1 = fric * total, fric * later
        if grads[i] is not None:
            g0, g1 = g0 + grads[i], g1 + grads[i]
        d_v, d_w = cv * div[i], cf * div[i]
        for n, x in enumerate(
            (v[i] + d_v + cf * g0, v[3 + i] - d_w - cr * g0, d_v + cf * g1, d_w + cr * g1)
        ):
            at = 16 * (3 * n + i)
            state[at : at + 16] = x
            if n < 2:
                f = 3 * n + i
                up[4 * f : 4 * f + 4] = x[12:]
                dn[f] = x[0]
                if f < 3 or f == 5:
                    place = min(f, 3)
                    up[40 + place] = below_partial(x[8:12])
                    dn[12 + place] = combine(ROW[0, 1:], [x[1 + l] for l in range(4)])
    q_rt, q_tt, q_tz, q_p = q * rt, q * tt, q * tz, q * p
    u = [cv * q_rt, cv * q_tt + cf * q_p, cv * q_tz, -(cf * q_tz)]
    for i, x in enumerate(u):
        up[44 + i] = below_partial(x[8:12])
        dn[16 + i] = combine(ROW[0, 1:], [x[1 + l] for l in range(4)])
    for i, x in enumerate((rt, tt, tz, p)):
        up[24 + 4 * i : 28 + 4 * i] = x[12:]
    for i, x in enumerate((rt, tt, tz, p, rz, zz)):
        dn[6 + i] = x[0]
    for i, x in enumerate((rz, tz, zz, p)):
        up[48 + i] = below_partial(x[12:])
    dn[DN_COEF + 7 :] = jnp.zeros((UP_COEF - DN_COEF, 8, NR), F32)
    outgoing(up[...], dn[...], near, far)


def is_even():
    return lax.axis_index("depth") % 2 == 0


def outgoing(up, dn, near, far):
    even = is_even()
    near[...] = jnp.where(even, up, dn)
    far[...] = jnp.where(even, dn, up)


def incoming(near, far):
    even = is_even()
    x, y = near[...], far[...]
    return jnp.where(even, y, x), jnp.where(even, x, y)


def stage(src, mr_in, mz_in, wr_in, wz_in, state_in, mr, mz, dt_m, wr, wz, state, coef, mark, sems):
    device = lax.axis_index("depth")
    pairs = (
        (state_in.at[0:COEF], state),
        (state_in.at[COEF:], coef),
        (mr_in.at[jnp.where(lax.axis_index("az") == 0, 1, 0)], mr),
        (mz_in.at[jnp.where(device == 0, 1, 0)], mz),
        (mr_in.at[2], dt_m),
        (wr_in, wr),
        (wz_in, wz),
    )
    copies = [pltpu.make_async_copy(a, b, sems.at[i]) for i, (a, b) in enumerate(pairs)]
    for copy in copies:
        copy.start()
    mark[...] = jnp.full((8, 256), (src[0] - PLANES * device).astype(F32), F32)
    for copy in copies:
        copy.wait()


def launch(s, state, far, near, coef, mark, dr_m, items, pk, keep, hold):
    has_below = coef[FLAGS]
    has_above = coef[FLAGS + 1]
    up, dn = incoming(near, far)
    c = {name: coef[n] for n, name in enumerate(OWN)}
    for n, name in enumerate(SHARED):
        c[name] = c[name] + up[UP_COEF + n] + dn[DN_COEF + n]
    q = inverse_radius(0, NR)
    cv, cf, cr, bulk, couple, modulus, shear = [spread_rows(c[n], 1, 5, True) for n in SHARED]

    def radial(fields):
        stacked = jnp.concatenate([flat(x) for x in fields], axis=0)
        out = mm(stacked, dr_m[0], dr_m[1])
        count = fields[0].shape[0]
        return [out[8 * count * i : 8 * count * (i + 1)].reshape(count, 8, NR) for i in range(len(fields))]

    def added(f, partial, above):
        x = s[f]
        planes = [float(ROW[l, 4]) * x[0] for l in range(4)]
        planes.append(has_below * partial)
        planes += [float(ROW[l, 4]) * above for l in range(4)]
        planes.append(has_above * below_partial(x[12:]))
        return jnp.stack(planes)

    def edges(x):
        return jnp.concatenate([x[:5], x[16:]], axis=0)

    e_cv, e_cf, e_cr = edges(cv), edges(cf), edges(cr)
    m_rz, m_tz, m_zz, m_p = [
        added(f, up[48 + i], dn[n]) for i, (f, n) in enumerate(((4, 10), (5, 8), (2, 11), (6, 9)))
    ]
    to_v = [e_cv * m_rz, e_cv * m_tz, e_cv * m_zz + e_cf * m_p]
    to_w = [e_cf * m_rz, e_cf * m_tz, e_cf * m_zz + e_cr * m_p]

    def inner_planes(n, more):
        x = state[16 * n : 16 * n + 16]
        return [x[:1] + more[4:5], x[1:12], x[12:] + more[5:9]]

    def whole(f, more):
        ends = [up[4 * f : 4 * f + 4] + more[:4]], [dn[f : f + 1] + more[9:]]
        return jnp.concatenate(ends[0] + inner_planes(f, more) + ends[1], axis=0)

    v1 = [whole(i, to_v[i]) for i in range(3)]
    w1 = [whole(3 + i, -to_w[i]) for i in range(3)]
    q_rt, q_tt, q_tz, q_p = [
        q * jnp.concatenate([up[24 + 4 * i : 28 + 4 * i], s[f], dn[6 + i : 7 + i]], axis=0)
        for i, f in enumerate((3, 1, 5, 6))
    ]
    u = [cv * q_rt, cv * q_tt + cf * q_p, cv * q_tz]
    uw = [-(cf * q_rt), -(cf * q_tt + cr * q_p), -(cf * q_tz)]

    def pack(f, planes):
        hold[2 * f] = planes[:8]
        hold[2 * f + 1] = planes[8:]

    for f, x in enumerate((3, 1, 5, 6)):
        pack(f, s[x])
    fk = spread_rows(c["fric"] * c["kappa"], 2, 4)
    o_cf, o_cr = cf[4:20], cr[4:20]
    for i in range(3):
        v_i, w_i = v1[i][4:20], w1[i][4:20]
        a = jnp.concatenate(inner_planes(6 + i, to_v[i]), axis=0) + o_cf * (fk * w_i)
        b = jnp.concatenate(inner_planes(9 + i, to_w[i]), axis=0) + o_cr * (fk * w_i)
        pack(4 + i, v_i)
        pack(9 + i, a)
        keep[i] = v_i
        keep[3 + i] = w_i
        keep[6 + i] = a
        keep[9 + i] = b
        if i == 1:
            pack(7, w_i)
            pack(12, b)

    mask21 = jnp.where(lax.broadcasted_iota(jnp.int32, (21, 8, NR), 0) < 20, 1.0, has_above)
    plane21 = lax.broadcasted_iota(jnp.int32, (21, 8, NR), 0) - 4
    lane21 = lax.broadcasted_iota(jnp.int32, (21, 8, NR), 2)
    source = jnp.where((plane21.astype(F32) == mark[:, :NR]) & (lane21 < 4 * RB), SOURCE, 0.0)

    def stresses(v, w, extra):
        at = 12 if extra is None else 16
        low = 40 if extra is None else 44
        vr, vt, wr = v[0], v[1], w[0]
        r_r, r_t, r_z, r_w = radial([vr, vt, v[2], wr])
        z_r, z_t, z_z, z_w = [
            depth_derivative(
                x,
                0,
                5,
                1,
                has_below,
                up[low + n] + float(ROW[4, 4]) * x[0],
                dn[at + n] + float(ROW[0, 0]) * x[20],
            )
            for n, x in enumerate((v[0], v[1], v[2], w[2]))
        ]
        e_tt, g_rt, g_tz, div_w = q * vr, r_t - q * vt, z_t, r_w + q * wr + z_w
        if extra is not None:
            e_tt, g_rt, g_tz, div_w = e_tt + extra[1], g_rt + extra[0], g_tz + extra[2], div_w + extra[3]
        div_v = r_r + e_tt + z_z
        total = bulk * div_v + couple * div_w
        return dict(
            rr=mask21 * (total + 2.0 * shear * r_r),
            zz=mask21 * (total + 2.0 * shear * z_z),
            rt=mask21 * (shear * g_rt),
            rz=mask21 * (shear * (z_r + r_z)),
            tz=mask21 * (shear * g_tz),
            p=mask21 * (-(couple * div_v + modulus * div_w) + (source if extra is None else 0.0)),
            w=div_w,
        )

    x0 = stresses(v1, w1, None)
    pack(8, x0["w"][4:20])
    x1 = stresses(u, uw, [q * v1[0], q * v1[1], q * v1[2], q * w1[1]])
    e2, dw2 = q * u[1], q * uw[1]
    total2 = bulk * e2 + couple * dw2
    x2 = dict(
        rr=mask21 * total2,
        zz=mask21 * total2,
        rt=mask21 * (shear * (q * u[0])),
        tz=mask21 * (shear * (q * u[2])),
        p=mask21 * (-(couple * e2 + modulus * dw2)),
    )

    def radius_items(fields):
        slots = [i for i, x in enumerate(fields) if x is not None]
        stacked = jnp.concatenate([flat(fields[i]) for i in slots], axis=1)
        hi, lo = [jnp.concatenate([items[h, NR * i : NR * i + NR] for i in slots], axis=0) for h in range(2)]
        return mm(stacked, hi, lo).reshape(-1, 8, NR)

    def depth_items(fields):
        out = []
        for x in fields:
            if x is None:
                out += [jnp.zeros((8, NR), F32)] * 2
            else:
                out.append(x[20])
                out.append(has_below * below_partial(x[:4]))
        return jnp.stack(out)

    velocity_r = [v1[0], v1[1], v1[2], None, u[0], u[1], u[2], uw[0]]
    pack(13, radius_items([None if x is None else x[4:20] for x in velocity_r]))
    names_r = ("rr", "rt", "rz", "p")
    pack(14, radius_items([x[n][4:20] for x in (x0, x1) for n in names_r]))
    pack(15, depth_items([v1[0], v1[1], v1[2], None, u[0], u[1], u[2], uw[2]]))
    names_z = ("rz", "tz", "zz", "p")
    pack(16, depth_items([x[n] for x in (x0, x1) for n in names_z]))
    second = [x2[n][4 + 8 * h : 12 + 8 * h] if n in x2 else None for h in range(2) for n in names_r]
    pack(17, jnp.concatenate([radius_items(second), depth_items([x2.get(n) for n in names_z])], axis=0))

    def send(i):
        chunks = exchange_groups(hold[i])
        for k in range(8):
            pk[k, i] = chunks[k]

    for_each(2 * FIELDS_IN, send, unroll=9)


def ring(recv, coef, mark, mr, mz, dt_m, wr, wz, out):
    group = lax.axis_index("az")
    c = {name: coef[n] for n, name in enumerate(RING)}
    q = inverse_radius(group, GROUP)

    def field(f):
        return jnp.concatenate([recv[:, 2 * f], recv[:, 2 * f + 1]], axis=-1)

    dt_h, dt_l = dt_m[0, :NT, :NT], dt_m[1, :NT, :NT]

    def az(fields):
        x = jnp.concatenate([y.reshape(NT, -1) for y in fields], axis=1)
        xh, xl = parts(x)
        y = dot(dt_h, xh) + dot(dt_h, xl) + dot(dt_l, xh)
        res, at = [], 0
        for f in fields:
            n = f.shape[-1]
            res.append(y[:, at : at + n].reshape(f.shape))
            at += n
        return res

    def by_half(x):
        x = x.reshape(NT, 256)
        return [x[:, :128], x[:, 128:]]

    mr_h, mr_l = mr[0], mr[1]
    mz_h, mz_l = mz[0], mz[1]

    def radial(fields, halo):
        stacked = jnp.concatenate([h for f in fields for h in by_half(f)], axis=0)
        y = mm(stacked, mr_h, mr_l)
        res = []
        for i in range(len(fields)):
            halves_ = [
                y[128 * i + 64 * g : 128 * i + 64 * g + 64] + halo[64 * g : 64 * g + 64, 128 * i : 128 * i + 128]
                for g in range(2)
            ]
            res.append(jnp.concatenate(halves_, axis=1).reshape(8, 8, 256))
        return res

    def depth(fields, halo):
        stacked = jnp.concatenate([f.reshape(NT, 256) for f in fields], axis=0)
        y = mm(stacked, mz_h, mz_l)
        return [
            (y[64 * i : 64 * i + 64] + halo[:, 256 * i : 256 * i + 256]).reshape(8, 8, 256)
            for i in range(len(fields))
        ]

    rt, tt, tz, p = [field(f) for f in range(4)]
    pr2, pr3 = field(13), field(14)
    pd2 = [recv[:, 30], recv[:, 31]]
    pd3 = [recv[:, 32], recv[:, 33]]
    px = field(17)
    s_rt, s_tt, s_tz, s_p, d_pr2, d_pr3, d_pd2, d_pd3, d_px = az([rt, tt, tz, p, pr2, pr3, pd2[1], pd3[1], px])
    (dd_px,) = az([d_px])
    wr0, wr1 = (wr[0, 0], wr[0, 1]), (wr[1, 0], wr[1, 1])

    def stack_halves(x):
        return jnp.concatenate(by_half(x), axis=0)

    def radius_halo(zero, one):
        return mm(stack_halves(zero), *wr0) + mm(stack_halves(one), *wr1)

    hr2 = radius_halo(pr2, d_pr2)
    hz2 = mm((pd2[0] + d_pd2).reshape(NT, 128), wz[0], wz[1])
    half = dd_px.reshape(NT, 256)[:, :128]
    hr3 = radius_halo(pr3, d_pr3) + jnp.concatenate([mm(half, *wr0), mm(half, *wr1)], axis=0)
    hz3 = mm((pd3[0] + d_pd3).reshape(NT, 128) + dd_px.reshape(NT, 256)[:, 128:], wz[0], wz[1])

    cv, cf, cr = c["cv"], c["cf"], c["cr"]
    q_rt, q_tt, q_tz, q_p = q * s_rt, q * s_tt, q * s_tz, q * s_p
    dw = [-(cf * q_rt), -(cf * q_tt + cr * q_p), -(cf * q_tz)]
    v1 = [
        field(4) + cv * q_rt,
        field(5) + cv * q_tt + cf * q_p,
        field(6) + cv * q_tz,
    ]
    w1_t = field(7) + dw[1]
    r_r, r_t, r_z, r_w = radial([v1[0], v1[1], v1[2], dw[0]], hr2)
    z_r, z_t, z_z, z_w = depth([v1[0], v1[1], v1[2], dw[2]], hz2)
    a_r, a_t, a_z, a_w = az([v1[0], v1[1], v1[2], w1_t])
    e_tt = q * (v1[0] + a_t)
    div_v = r_r + e_tt + z_z
    div_w = field(8) + r_w + q * (dw[0] + a_w) + z_w
    total = c["bulk"] * div_v + c["couple"] * div_w
    shear = c["shear"]
    lanes = lax.broadcasted_iota(jnp.int32, (8, 256), 1) // GROUP
    source = jnp.where(lanes.astype(F32) == mark[...], jnp.where(group == 0, SOURCE, 0.0), 0.0)
    n_rr = total + 2.0 * shear * r_r
    n_tt = total + 2.0 * shear * e_tt
    n_zz = total + 2.0 * shear * z_z
    n_rt = shear * (q * (a_r - v1[1]) + r_t)
    n_rz = shear * (z_r + r_z)
    n_tz = shear * (z_t + q * a_z)
    n_p = source - (c["couple"] * div_v + c["modulus"] * div_w)

    r_rr, r_rt, r_rz, r_p = radial([n_rr, n_rt, n_rz, n_p], hr3)
    z_rz, z_tz, z_zz, z_p = depth([n_rz, n_tz, n_zz, n_p], hz3)
    a_rt, a_tt, a_tz, a_p = az([n_rt, n_tt, n_tz, n_p])
    d_r = q_rt + r_rr + z_rz + q * (a_rt + n_rr - n_tt)
    d_t = q_tt + r_rt + z_tz + q * (a_tt + 2.0 * n_rt)
    d_z = q_tz + r_rz + z_zz + q * (a_tz + n_rz)
    fk = c["fk"]
    g_r = r_p + fk * dw[0]
    g_t = q_p + q * a_p + fk * dw[1]
    g_z = z_p + fk * dw[2]
    sums = [
        2.0 * v1[0] + field(9) + cv * d_r + cf * g_r,
        2.0 * v1[1] + field(10) + cv * d_t + cf * g_t,
        2.0 * v1[2] + field(11) + cv * d_z + cf * g_z,
        2.0 * w1_t - field(12) - cf * d_t - cr * g_t,
    ]
    results = [s_rt, s_tt, s_tz, s_p, d_r, d_t, d_z, g_r, g_t, g_z] + az(sums)
    for f, x in enumerate(results):
        out[:, 2 * f] = x[:, :, :128]
        out[:, 2 * f + 1] = x[:, :, 128:]


def unpack(recv, hold, first, count):
    def receive(i):
        rows = exchange_groups([recv[k, 2 * first + i] for k in range(8)])
        for j in range(8):
            hold[i, j] = rows[j]

    for_each(2 * count, receive)
    return lambda f: jnp.concatenate([hold[2 * (f - first)], hold[2 * (f - first) + 1]], axis=0)


def advance(recv, keep, coef, new, mid, far, near, hold):
    up, dn = [], []
    field = unpack(recv, hold, 0, 10)
    c = {name: coef[n] for n, name in enumerate(OWN)}
    q = inverse_radius(0, NR)
    cv, cf, cr = [spread_rows(c[n], 2, 4) for n in ("cv", "cf", "cr")]
    q_rt, q_tt, q_tz, q_p = [q * field(f) for f in range(4)]
    dv = [cv * q_rt, cv * q_tt + cf * q_p, cv * q_tz]
    dw = [-(cf * q_rt), -(cf * q_tt + cr * q_p), -(cf * q_tz)]
    for i in range(3):
        d, g = field(4 + i), field(7 + i)
        v1 = keep[i] + dv[i]
        w1 = keep[3 + i] + dw[i]
        v2 = v1 + keep[6 + i] + cv * d + cf * g
        w2 = w1 - keep[9 + i] - cf * d - cr * g
        new[i] = v2
        new[3 + i] = w2
        mid[i] = v1
        mid[3 + i] = w1
        x = v1 + v2
        up.append(below_partial(x[12:]))
        dn.append(x[0])
        if i == 2:
            x = w1 + w2
            up.append(below_partial(x[12:]))
            dn.append(x[0])
    outgoing(jnp.stack(up), jnp.stack(dn), near, far)


def settle(recv, v2, mid, v, s, psi, coef, mark, dr_m, v_hbm, m_hbm, s_out, hold, m_out, sems):
    copies = [
        pltpu.make_async_copy(a, b, sems.at[i])
        for i, (a, b) in enumerate(((v2, v_hbm), (m_out, m_hbm)))
    ]
    copies[0].start()
    field = unpack(recv, hold, 10, 4)
    has_below = coef[FLAGS]
    c = {name: coef[n] for n, name in enumerate(OWN)}
    q = inverse_radius(0, NR)

    def sp(value):
        return spread_rows(value, 2, 4)

    omega = sp(c["omega"])
    decay = [sp(c[f"decay{l}"]) for l in range(4)]
    for i in range(3):
        w1, w2 = mid[3 + i], v2[3 + i]
        first = w1 - v[3 + i] + omega * w1
        second = w2 - w1 + omega * w2
        for l in range(4):
            m_out[3 * l + i] = decay[l] * (decay[l] * (psi[3 * l + i] + first) + second)
    copies[1].start()
    sums = [mid[i] + v2[i] for i in range(6)]
    zero = jnp.zeros((1, 8, NR), F32)
    z_r, z_t, z_z, z_w = [
        depth_derivative(jnp.concatenate([x, zero], axis=0), 0, 4, 0, has_below, float(ROW[4, 4]) * x[0], zero[0])[:16]
        for x in (sums[0], sums[1], sums[2], sums[5])
    ]
    stacked = jnp.concatenate([flat(x) for x in sums[:4]], axis=0)
    y = mm(stacked, dr_m[0], dr_m[1])
    r_r, r_t, r_z, r_w = [y[128 * i : 128 * i + 128].reshape(16, 8, NR) for i in range(4)]
    a_r, a_t, a_z, a_w = [field(10 + i) for i in range(4)]
    e_tt = q * (sums[0] + a_t)
    div_v = r_r + e_tt + z_z
    div_w = r_w + q * (sums[3] + a_w) + z_w
    couple, shear = sp(c["couple"]), sp(c["shear"])
    total = sp(c["bulk"]) * div_v + couple * div_w
    plane = lax.broadcasted_iota(jnp.int32, (16, 8, NR), 0)
    lane = lax.broadcasted_iota(jnp.int32, (16, 8, NR), 2)
    source = jnp.where((plane.astype(F32) == mark[:, :NR]) & (lane < 4 * RB), SOURCE * (1.0 + math.cos(0.9)), 0.0)
    updates = [
        total + 2.0 * shear * r_r,
        total + 2.0 * shear * e_tt,
        total + 2.0 * shear * z_z,
        shear * (q * (a_r - sums[1]) + r_t),
        shear * (z_r + r_z),
        shear * (z_t + q * a_z),
        source - (couple * div_v + sp(c["modulus"]) * div_w),
    ]
    for f, x in enumerate(updates):
        s_out[f] = s[f] + x
    for copy in copies:
        copy.wait()


def close(s, far, near, coef, s_out, new, sems):
    inner = pltpu.make_async_copy(s.at[:, 1:12], s_out.at[:, 1:12], sems.at[2])
    inner.start()
    up, dn = incoming(near, far)
    has_below = coef[FLAGS]
    c = {name: coef[n] for n, name in enumerate(OWN)}

    def update(slot, row, plane, z_r, z_t, z_z, z_w):
        def at(name):
            return jnp.broadcast_to(c[name][row : row + 1, :], (8, NR))

        bulk, couple, modulus, shear = at("bulk"), at("couple"), at("modulus"), at("shear")
        total = bulk * z_z + couple * z_w
        new[0, slot] = s[0, plane] + total
        new[1, slot] = s[1, plane] + total
        new[2, slot] = s[2, plane] + total + 2.0 * shear * z_z
        new[3, slot] = s[3, plane]
        new[4, slot] = s[4, plane] + shear * z_r
        new[5, slot] = s[5, plane] + shear * z_t
        new[6, slot] = s[6, plane] - (couple * z_z + modulus * z_w)

    update(0, 2, 0, *[has_below * up[i] for i in range(4)])
    for slot in range(1, 5):
        weight = float(ROW[slot - 1, 4])
        update(slot, 5, 11 + slot, *[weight * dn[i] for i in range(4)])
    copies = [
        pltpu.make_async_copy(new.at[:, 0:1], s_out.at[:, 0:1], sems.at[0]),
        pltpu.make_async_copy(new.at[:, 1:5], s_out.at[:, 12:16], sems.at[1]),
    ]
    for copy in copies:
        copy.start()
    for copy in copies + [inner]:
        copy.wait()


def call(body, inputs, shapes, types=None, hbm=(), smem=(), scratch=(), out_hbm=(), micros=1, vmem=VMEM_LIMIT):
    def space(i):
        return pltpu.HBM if i in hbm else pltpu.SMEM if i in smem else pltpu.VMEM

    return pl.pallas_call(
        body,
        out_shape=[jax.ShapeDtypeStruct(x, t) for x, t in zip(shapes, types or [F32] * len(shapes))],
        in_specs=[pl.BlockSpec(memory_space=space(i)) for i in range(len(inputs))],
        out_specs=[pl.BlockSpec(memory_space=pltpu.HBM if i in out_hbm else pltpu.VMEM) for i in range(len(shapes))],
        scratch_shapes=list(scratch),
        compiler_params=pltpu.CompilerParams(vmem_limit_bytes=vmem),
        cost_estimate=pl.CostEstimate(flops=0, bytes_accessed=3 * 10**6 * micros, transcendentals=0),
        name=body.__name__,
    )(*inputs)


def swap(value, first):
    lows = range(first, lax.axis_size("depth") - 1, 2)
    return lax.ppermute(value, "depth", [p for i in lows for p in ((i, i + 1), (i + 1, i))])


def neighbours(near, far):
    far = swap(far, 1)
    return swap(near, 0), far


def on_device(velocity, stress, memory, layer_ids, materials, jkd, source_depth):
    c = constants()
    block = (PLANES, AZ, NR)
    tables = [layer_ids, materials, jkd]
    state, far, near, ring_coef = call(
        prepare,
        tables + [stress, c["dr"], velocity, memory],
        [(COEF + FLAGS + 2, AZ, NR), (UP_COEF + 7, AZ, NR), (UP_COEF + 7, AZ, NR), (len(RING), 8, 256)],
        hbm=range(7),
        scratch=[pltpu.VMEM((UP_COEF + 7, AZ, NR), F32)] * 2
        + [pltpu.SMEM(x.shape, x.dtype) for x in tables]
        + [pltpu.VMEM((7,) + block, F32), pltpu.VMEM(c["dr"].shape, BF16)]
        + [pltpu.VMEM((n,) + block, F32) for n in (6, 12)]
        + [pltpu.SemaphoreType.DMA((7,))],
        vmem=VMEM_FULL,
    )
    near, far = neighbours(near, far)
    staged = [c[n] for n in ("mr", "mz", "wr", "wz")]
    shapes = [c[n].shape[1:] for n in ("mr", "mz", "mr")] + [c["wr"].shape, c["wz"].shape]
    *matrices, state, coef, mark = call(
        stage,
        [source_depth] + staged + [state],
        shapes + [(COEF, AZ, NR), (FLAGS + 2, AZ, NR), (8, 256)],
        types=[BF16] * 5 + [F32] * 3,
        hbm=range(1, 6),
        smem=(0,),
        scratch=[pltpu.SemaphoreType.DMA((7,))],
    )
    packed, keep = call(
        launch,
        [stress, state, far, near, coef, mark, c["dr"], c["items"]],
        [(8, 2 * FIELDS_IN, AZ, NR), (12,) + block],
        scratch=[pltpu.VMEM((2 * FIELDS_IN, 8, AZ, NR), F32)],
        micros=4,
    )
    packed = lax.all_to_all(packed, "az", split_axis=0, concat_axis=0, tiled=True)
    (back,) = call(ring, [packed, ring_coef, mark] + matrices, [(8, 2 * FIELDS_OUT, AZ, NR)], micros=3)
    back = lax.all_to_all(back, "az", split_axis=0, concat_axis=0, tiled=True)
    new, mid, far, near = call(
        advance,
        [back, keep, coef],
        [(6,) + block, (6,) + block, (4, AZ, NR), (4, AZ, NR)],
        scratch=[pltpu.VMEM((20, 8, AZ, NR), F32)],
    )
    near, far = neighbours(near, far)
    v_out, m_out, s_part = call(
        settle,
        [back, new, mid, velocity, stress, memory, coef, mark, c["dr"]],
        [(6,) + block, (12,) + block, (7,) + block],
        scratch=[pltpu.VMEM((8, 8, AZ, NR), F32)]
        + [pltpu.VMEM((n,) + block, F32) for n in (12,)]
        + [pltpu.SemaphoreType.DMA((2,))],
        out_hbm=range(2),
        micros=3,
    )
    (s_out,) = call(
        close,
        [s_part, far, near, coef],
        [(7,) + block],
        scratch=[pltpu.VMEM((7, 5, AZ, NR), F32), pltpu.SemaphoreType.DMA((3,))],
        out_hbm=(0,),
    )
    return v_out, s_out, m_out


def solution(mesh):
    field = P(None, "depth", "az", None)
    return jax.shard_map(
        on_device,
        mesh=mesh,
        in_specs=(field, field, field, P("depth", None), P(), P(), P()),
        out_specs=(field, field, field),
        check_vma=False,
    )
```
